32 devices in a mesh: batch: 8 (over y, x, core), group: 4 (over z).
Axes of the slice: x: 2, y: 2, z: 4, core: 2. Of those that a mesh axis runs over, the one named last changes fastest.
Arguments:
- tokens: bfloat16 [2, 8192, 1024], P(None, ('batch', 'group')), may hold values from -6 to 6
- memory: bfloat16 [2, 4096, 1024], P(None, ('batch', 'group')), may hold values from -6 to 6
- dec_segments: int32 [2, 8192], P(None, 'batch'), may hold values from 0 to 3, as said below
- enc_segments: int32 [2, 4096], P(None, 'batch'), may hold values from 0 to 3, as said below
- buckets: int32 [1024], replicated, may hold values from 0 to 31
- self_gain: float32 [1024], replicated, may hold values from 0.1 to 1.9
- self_query: bfloat16 [1024, 1024], P(None, 'group'), may hold values from -0.09375 to 0.09375
- self_key: bfloat16 [1024, 512], P(None, 'group'), may hold values from -0.09375 to 0.09375
- self_value: bfloat16 [1024, 512], P(None, 'group'), may hold values from -0.1875 to 0.1875
- self_output: bfloat16 [1024, 1024], P('group'), may hold values from -0.75 to 0.75
- rel_bias: float32 [32, 16], P(None, 'group'), may hold values from -4 to 4
- cross_gain: float32 [1024], replicated, may hold values from 0.1 to 1.9
- cross_query: bfloat16 [1024, 1024], P(None, 'group'), may hold values from -0.09375 to 0.09375
- cross_key: bfloat16 [1024, 512], P(None, 'group'), may hold values from -0.09375 to 0.09375
- cross_value: bfloat16 [1024, 512], P(None, 'group'), may hold values from -0.1875 to 0.1875
- cross_output: bfloat16 [1024, 1024], P('group'), may hold values from -0.75 to 0.75
- ffn_gain: float32 [1024], replicated, may hold values from 0.1 to 1.9
- ffn_gate: bfloat16 [1024, 2816], P(None, 'group'), may hold values from -0.1875 to 0.1875
- ffn_up: bfloat16 [1024, 2816], P(None, 'group'), may hold values from -0.1875 to 0.1875
- ffn_down: bfloat16 [2816, 1024], P('group'), may hold values from -0.109375 to 0.109375
- out_grad: bfloat16 [2, 8192, 1024], P(None, ('batch', 'group')), may hold values from -6 to 6
Outputs:
- block_out: bfloat16 [2, 8192, 1024], P(None, ('batch', 'group'))
- tokens_grad: float32 [2, 8192, 1024], P(None, ('batch', 'group'))
- memory_grad: float32 [2, 4096, 1024], P(None, ('batch', 'group'))
- self_gain_grad: float32 [1024], replicated
- self_query_grad: float32 [1024, 1024], P(None, 'group')
- self_key_grad: float32 [1024, 512], P(None, 'group')
- self_value_grad: float32 [1024, 512], P(None, 'group')
- self_output_grad: float32 [1024, 1024], P('group')
- rel_bias_grad: float32 [32, 16], P(None, 'group')
- cross_gain_grad: float32 [1024], replicated
- cross_query_grad: float32 [1024, 1024], P(None, 'group')
- cross_key_grad: float32 [1024, 512], P(None, 'group')
- cross_value_grad: float32 [1024, 512], P(None, 'group')
- cross_output_grad: float32 [1024, 1024], P('group')
- ffn_gain_grad: float32 [1024], replicated
- ffn_gate_grad: float32 [1024, 2816], P(None, 'group')
- ffn_up_grad: float32 [1024, 2816], P(None, 'group')
- ffn_down_grad: float32 [2816, 1024], P('group')
The draws below stay inside these ranges and needn't reach their ends.
Inputs may be any that keep to these rules, and one draw needn't show every extreme that they name: `dec_segments`: within each aligned block of 1024 entries (one sequence) the ids never fall, start at 0 and take every value up to 3. `enc_segments`: within each aligned block of 512 entries (one sequence) the ids never fall, start at 0 and take every value up to 3.
All inputs are finite; a program needn't handle non-finite values.
Results may differ from the reference program's by a relative error of at most 0.028.
The reference program's roundings to bfloat16 on the way count: a program that leaves them out, or rounds other values in their place, can miss the bound.
Values may be sent and summed in bfloat16 or wider, within the bound.
No kernel may reach another device: no remote copies, remote signals or barrier semaphores. Data moves between devices by JAX's collectives and lax.ppermute only.
A program may use at most 320 MiB of HBM per device.

```python
import jax
import jax.numpy as jnp
from jax import lax

D = 1024
HEADS = 16
KV_GROUPS = 8
HEAD_DIM = 64
FF = 2816
BUCKETS = 32
MICRO = 2
SEQ_LEN = 1024
ENC_LEN = 512
DOCS = 4
ROWS = 8192
ENC_ROWS = 4096


def segment_ids(key, length, sequences):

    def one_sequence(seq_key):
        boundaries = jnp.sort(jax.random.permutation(seq_key, length - 1)[:DOCS - 1] + 1)
        positions = jnp.arange(length)
        return jnp.sum((positions[:, None] >= boundaries[None, :]).astype(jnp.int32), axis=1).astype(jnp.int32)
    seq_keys = jax.random.split(key, sequences)
    return jax.vmap(one_sequence)(seq_keys)


def draw_dec_segments(key, part):
    sequences = MICRO * (ROWS // SEQ_LEN)
    return segment_ids(jax.random.fold_in(key, 11), SEQ_LEN, sequences).reshape(MICRO, ROWS)


def draw_enc_segments(key, part):
    sequences = MICRO * (ENC_ROWS // ENC_LEN)
    return segment_ids(jax.random.fold_in(key, 23), ENC_LEN, sequences).reshape(MICRO, ENC_ROWS)


def with_ends(entries, own_key, low, top_value):
    spot = [jax.random.randint(jax.random.fold_in(own_key, axis), (), 0, length) for axis, length in enumerate(entries.shape)]
    widest = entries.shape.index(max(entries.shape))
    neighbour = spot[:widest] + [(spot[widest] + 1) % entries.shape[widest]] + spot[widest + 1:]
    return entries.at[tuple(spot)].set(low).at[tuple(neighbour)].set(top_value)


def steps_of(rng, dims, shards, low, high):
    loudness, own = 1.0, jax.random.fold_in(rng, 6)
    for axis_at, shards_of in shards:
        heights = jnp.exp(jax.random.uniform(jax.random.fold_in(own, axis_at), (shards_of,), jnp.float32, low / len(shards), high / len(shards)))
        loudness = loudness * jnp.repeat(heights, dims[axis_at] // shards_of).reshape([-1 if axis == axis_at else 1 for axis in range(len(dims))])
    return loudness


def noise(stream_key, extent, spread, reach, shards=(), held_as=jnp.bfloat16):
    values = spread * jax.random.normal(stream_key, extent, jnp.float32)
    if shards:
        values = values * steps_of(stream_key, extent, shards, -0.22, 0.18)
    return jnp.clip(values, -reach, reach).astype(held_as)


def setup_inputs(seed: int = 0) -> dict:
    key_of = jax.random.split(jax.random.key(seed), 22)
    tokens = noise(key_of[0], (MICRO, ROWS, D), 1.0, 6.0, ((1, 32),))
    memory = noise(key_of[1], (MICRO, ENC_ROWS, D), 1.0, 6.0, ((1, 32),))
    dec_segments = draw_dec_segments(jax.random.fold_in(key_of[21], 71), 0)
    enc_segments = draw_enc_segments(jax.random.fold_in(key_of[21], 71), 0)
    buckets = with_ends(jax.random.randint(key_of[4], (SEQ_LEN,), 0, BUCKETS), jax.random.fold_in(key_of[4], 1), 0, BUCKETS - 1).astype(jnp.int32)
    self_gain = jnp.clip(1.0 + 0.18 * jax.random.normal(key_of[5], (D,), jnp.float32), 0.1, 1.9)
    self_query = noise(key_of[6], (D, HEADS * HEAD_DIM), (4 * D) ** -0.5, 0.09375, ((1, 4),))
    self_key = noise(key_of[7], (D, KV_GROUPS * HEAD_DIM), (4 * D) ** -0.5, 0.09375, ((1, 4),))
    self_value = noise(key_of[8], (D, KV_GROUPS * HEAD_DIM), D ** -0.5, 0.1875, ((1, 4),))
    self_output = noise(key_of[9], (HEADS * HEAD_DIM, D), (HEADS * HEAD_DIM // 16) ** -0.5, 0.75, ((0, 4),))
    rel_bias = noise(key_of[10], (BUCKETS, HEADS), 1.0, 4.0, ((1, 4),), jnp.float32)
    cross_gain = jnp.clip(1.0 + 0.18 * jax.random.normal(key_of[11], (D,), jnp.float32), 0.1, 1.9)
    cross_query = noise(key_of[12], (D, HEADS * HEAD_DIM), (4 * D) ** -0.5, 0.09375, ((1, 4),))
    cross_key = noise(key_of[13], (D, KV_GROUPS * HEAD_DIM), (4 * D) ** -0.5, 0.09375, ((1, 4),))
    cross_value = noise(key_of[14], (D, KV_GROUPS * HEAD_DIM), D ** -0.5, 0.1875, ((1, 4),))
    cross_output = noise(key_of[15], (HEADS * HEAD_DIM, D), (HEADS * HEAD_DIM // 16) ** -0.5, 0.75, ((0, 4),))
    ffn_gain = jnp.clip(1.0 + 0.18 * jax.random.normal(key_of[16], (D,), jnp.float32), 0.1, 1.9)
    ffn_gate = noise(key_of[17], (D, FF), D ** -0.5, 0.1875, ((1, 4),))
    ffn_up = noise(key_of[18], (D, FF), D ** -0.5, 0.1875, ((1, 4),))
    ffn_down = noise(key_of[19], (FF, D), FF ** -0.5, 0.109375, ((0, 4),))
    out_grad = noise(key_of[20], (MICRO, ROWS, D), 1.0, 6.0, ((1, 32),))
    return {"tokens": tokens, "memory": memory, "dec_segments": dec_segments, "enc_segments": enc_segments, "buckets": buckets, "self_gain": self_gain, "self_query": self_query, "self_key": self_key, "self_value": self_value, "self_output": self_output, "rel_bias": rel_bias, "cross_gain": cross_gain, "cross_query": cross_query, "cross_key": cross_key, "cross_value": cross_value, "cross_output": cross_output, "ffn_gain": ffn_gain, "ffn_gate": ffn_gate, "ffn_up": ffn_up, "ffn_down": ffn_down, "out_grad": out_grad}


@jax.custom_vjp
def low(v):
    return lax.optimization_barrier(v.astype(jnp.bfloat16)).astype(jnp.float32)

@jax.custom_vjp
def low_back(v):
    return v

def low_keep(v):
    return (low(v), None)

def low_pass(kept, grad):
    return (grad,)

def back_keep(v):
    return (v, None)

def back_low(kept, grad):
    return (low(grad),)
low.defvjp(low_keep, low_pass)
low_back.defvjp(back_keep, back_low)
EPSILON = 1e-06
HIGHEST = lax.Precision.HIGHEST

def matmul(left, right):
    return jnp.dot(left, right, precision=HIGHEST, preferred_element_type=jnp.float32)

def rms_scale(values, gain):
    return values * lax.rsqrt(lax.optimization_barrier(jnp.mean(values * values, axis=-1, keepdims=True)) + EPSILON) * gain

def project(values, weight):
    return low(low_back(matmul(values, weight)))

def attention(query, keys, values, bias, allowed):
    length = query.shape[0]
    groups = keys.shape[1] // HEAD_DIM
    query = query.reshape(length, groups, -1, HEAD_DIM)
    keys = keys.reshape(keys.shape[0], groups, HEAD_DIM)
    values = values.reshape(values.shape[0], groups, HEAD_DIM)
    scores = low_back(jnp.einsum('qgrd,kgd->grqk', query, keys, precision=HIGHEST)) + bias
    scores = jnp.where(allowed, scores, -1e+30)
    row_max = lax.optimization_barrier(jnp.max(scores, axis=-1, keepdims=True))
    exponent = jnp.exp(scores - row_max)
    attn_probs = low(exponent / lax.optimization_barrier(jnp.sum(exponent, axis=-1, keepdims=True)))
    attended = jnp.einsum('grqk,kgd->qgrd', attn_probs, values, precision=HIGHEST)
    return low(low_back(attended.reshape(length, -1)))

def decoder_layer(stream, encoded, params, dec_seg, enc_seg, buckets):
    self_gain, self_query, self_key, self_value, self_output, rel_bias, cross_gain, cross_query, cross_key, cross_value, cross_output, ffn_gain, ffn_gate, ffn_up, ffn_down = params
    length = stream.shape[0]
    positions = jnp.arange(length)
    distance = positions[:, None] - positions[None, :]
    bucket_index = buckets[jnp.clip(distance, 0, length - 1)]
    bias_table = jnp.moveaxis(rel_bias[bucket_index], -1, 0)
    bias_table = bias_table.reshape(self_key.shape[1] // HEAD_DIM, -1, length, length)
    allowed = (distance >= 0) & (dec_seg[:, None] == dec_seg[None, :])
    normed = low(rms_scale(stream, self_gain))
    attended = attention(project(normed, self_query), project(normed, self_key), project(normed, self_value), bias_table, allowed)
    stream_one = stream + low_back(matmul(attended, self_output))
    normed = low(rms_scale(stream_one, cross_gain))
    cross_allowed = dec_seg[:, None] == enc_seg[None, :]
    attended = attention(project(normed, cross_query), project(encoded, cross_key), project(encoded, cross_value), 0.0, cross_allowed)
    stream_two = stream_one + low_back(matmul(attended, cross_output))
    normed = low(rms_scale(stream_two, ffn_gain))
    gate = low_back(matmul(normed, ffn_gate))
    upval = low_back(matmul(normed, ffn_up))
    hidden = low(low_back(jax.nn.gelu(gate, approximate=True) * upval))
    return stream_two + low_back(matmul(hidden, ffn_down))

def reference(tokens, memory, dec_segments, enc_segments, buckets, self_gain, self_query, self_key, self_value, self_output, rel_bias, cross_gain, cross_query, cross_key, cross_value, cross_output, ffn_gain, ffn_gate, ffn_up, ffn_down, out_grad):
    params = tuple((weight.astype(jnp.float32) for weight in (self_gain, self_query, self_key, self_value, self_output, rel_bias, cross_gain, cross_query, cross_key, cross_value, cross_output, ffn_gain, ffn_gate, ffn_up, ffn_down)))
    sequences = MICRO * (ROWS // SEQ_LEN)
    streams = tokens.astype(jnp.float32).reshape(sequences, SEQ_LEN, D)
    encodeds = memory.astype(jnp.float32).reshape(sequences, ENC_LEN, D)
    dec_all = dec_segments.reshape(sequences, SEQ_LEN)
    enc_all = enc_segments.reshape(sequences, ENC_LEN)
    cotangents = out_grad.astype(jnp.float32).reshape(sequences, SEQ_LEN, D)

    def one_sequence(totals, item):
        stream, encoded, dec_seg, enc_seg, cotangent = item

        def forward(stream_in, encoded_in, params_in):
            return decoder_layer(stream_in, encoded_in, params_in, dec_seg, enc_seg, buckets)
        result, pull = jax.vjp(forward, stream, encoded, params)
        grad_stream, grad_encoded, grad_params = pull(cotangent)
        totals = jax.tree.map(lambda left, right: left + right, totals, grad_params)
        return (totals, (result.astype(jnp.bfloat16), grad_stream, grad_encoded))
    zeros = jax.tree.map(jnp.zeros_like, params)
    totals, (results, grad_streams, grad_encodeds) = lax.scan(one_sequence, zeros, (streams, encodeds, dec_all, enc_all, cotangents))
    return (results.reshape(MICRO, ROWS, D), grad_streams.reshape(MICRO, ROWS, D), grad_encodeds.reshape(MICRO, ENC_ROWS, D), totals[0], totals[1], totals[2], totals[3], totals[4], totals[5], totals[6], totals[7], totals[8], totals[9], totals[10], totals[11], totals[12], totals[13], totals[14])
```

```python
import functools

import jax
import jax.numpy as jnp
from jax import lax
from jax.experimental import pallas as pl
from jax.experimental.pallas import tpu as pltpu
from jax.sharding import PartitionSpec as P

HEAD_DIM = 64
PAIR = 2 * HEAD_DIM
EPSILON = 1e-06
MASKED = -1e30
HIGHEST = lax.Precision.HIGHEST
BF16 = jnp.bfloat16
F32 = jnp.float32


def dot_nn(left, right):
    return lax.dot_general(left, right, (((1,), (0,)), ((), ())), preferred_element_type=F32)


def dot_nt(left, right):
    return lax.dot_general(left, right, (((1,), (1,)), ((), ())), preferred_element_type=F32)


def dot_tn(left, right):
    return lax.dot_general(left, right, (((0,), (0,)), ((), ())), preferred_element_type=F32)


def call(kernel, outs, grid, in_specs, out_specs, scratch=(), prefetch=0):
    return pl.pallas_call(
        kernel,
        out_shape=outs,
        grid_spec=pltpu.PrefetchScalarGridSpec(
            num_scalar_prefetch=prefetch,
            grid=grid,
            in_specs=in_specs,
            out_specs=out_specs,
            scratch_shapes=list(scratch),
        ),
        compiler_params=pltpu.CompilerParams(
            dimension_semantics=("arbitrary",) * len(grid),
        ),
    )


def shape(*dims, dtype=BF16):
    return jax.ShapeDtypeStruct(dims, dtype)


def whole(array):
    dims = array.shape
    return pl.BlockSpec(dims, lambda *ids: (0,) * len(dims))


def fixed(*dims):
    return pl.BlockSpec(dims, lambda *ids: (0,) * len(dims))


def rows_of(ref):
    block = ref[...]
    return block.reshape(block.shape[0] * block.shape[2], block.shape[3])


def store_rows(ref, value):
    ref[...] = value.reshape(ref.shape).astype(ref.dtype)


def weight_spec(weights, columns, index):
    cols, _, blk, _ = weights.shape
    return pl.BlockSpec((cols, 1, blk, columns), index)


def norm(values, gain):
    return values * lax.rsqrt(jnp.mean(values * values, axis=-1, keepdims=True) + EPSILON) * gain


def norm_back(values, gain, grad):
    scale = lax.rsqrt(jnp.mean(values * values, axis=-1, keepdims=True) + EPSILON)
    scaled = grad * gain
    inner = jnp.mean(scaled * values, axis=-1, keepdims=True)
    grad_values = scale * scaled - values * (scale * scale * scale * inner)
    grad_gain = jnp.sum(grad * values * scale, axis=0, keepdims=True)
    return grad_values, grad_gain


def qkv_kernel(x_ref, gain_ref, own_ref, oth_ref, n_ref, q_ref, kv_ref):
    half = x_ref.shape[1] // 2
    qcols = q_ref.shape[1]

    @pl.when(pl.program_id(0) == 0)
    def _():
        n_ref[...] = norm(x_ref[...].astype(F32), gain_ref[...]).astype(BF16)

    out = dot_nn(n_ref[:, :half], rows_of(own_ref)) + dot_nn(n_ref[:, half:], rows_of(oth_ref))
    q_ref[...] = out[:, :qcols].astype(BF16)
    kv_ref[...] = out[:, qcols:].astype(BF16)


def project_qkv(x, gain, own, oth, qcols):
    rows, width = x.shape
    shards = own.shape[1]
    spec = weight_spec(own, 2 * qcols, lambda z: (0, z, 0, 0))
    out = pl.BlockSpec((rows, qcols), lambda z: (0, z))
    return call(
        qkv_kernel,
        (shape(rows, width), shape(rows, shards * qcols), shape(rows, shards * qcols)),
        (shards,),
        [whole(x), whole(gain), spec, spec],
        (fixed(rows, width), out, out),
    )(x, gain, own, oth)


def kv_kernel(x_ref, own_ref, oth_ref, kv_ref):
    half = x_ref.shape[1] // 2
    out = dot_nn(x_ref[:, :half], rows_of(own_ref)) + dot_nn(x_ref[:, half:], rows_of(oth_ref))
    kv_ref[...] = out.astype(BF16)


def project_kv(x, own, oth, qcols):
    rows, width = x.shape
    shards = own.shape[1]
    spec = weight_spec(own, qcols, lambda z: (0, z, 0, 1))
    return call(
        kv_kernel,
        shape(rows, shards * qcols),
        (shards,),
        [whole(x), spec, spec],
        pl.BlockSpec((rows, qcols), lambda z: (0, z)),
    )(x, own, oth)


def mid_kernel(shards, x_ref, att_ref, gain_ref, wo_own, wo_oth, wq_own, wq_oth, s_ref, n_ref, q_ref):
    step = pl.program_id(0)
    half = x_ref.shape[1] // 2

    @pl.when(step == 0)
    def _():
        s_ref[...] = x_ref[...].astype(F32)

    @pl.when(step < shards)
    def _():
        att = att_ref[...]
        s_ref[:, :half] += dot_nt(att, rows_of(wo_own))
        s_ref[:, half:] += dot_nt(att, rows_of(wo_oth))

    @pl.when(step == shards - 1)
    def _():
        n_ref[...] = norm(s_ref[...], gain_ref[...]).astype(BF16)

    @pl.when(step >= shards)
    def _():
        out = dot_nn(n_ref[:, :half], rows_of(wq_own)) + dot_nn(n_ref[:, half:], rows_of(wq_oth))
        q_ref[...] = out.astype(BF16)


def output_and_query(x, att, gain, own, oth, next_own, next_oth, qcols):
    rows, width = x.shape
    shards = own.shape[1]
    first = lambda i: jnp.minimum(i, shards - 1)
    second = lambda i: jnp.maximum(i - shards, 0)
    wo = weight_spec(own, qcols, lambda i: (0, first(i), 0, 2))
    wq = weight_spec(own, qcols, lambda i: (0, second(i), 0, 0))
    return call(
        functools.partial(mid_kernel, shards),
        (shape(rows, width, dtype=F32), shape(rows, width), shape(rows, shards * qcols)),
        (2 * shards,),
        [
            whole(x),
            pl.BlockSpec((rows, qcols), lambda i: (0, first(i))),
            whole(gain),
            wo,
            wo,
            wq,
            wq,
        ],
        (
            fixed(rows, width),
            fixed(rows, width),
            pl.BlockSpec((rows, qcols), lambda i: (0, second(i))),
        ),
    )(x, att, gain, own, oth, next_own, next_oth)


def out_kernel(x_ref, att_ref, gain_ref, wo_own, wo_oth, s_ref, n_ref):
    half = x_ref.shape[1] // 2

    @pl.when(pl.program_id(0) == 0)
    def _():
        s_ref[...] = x_ref[...]

    att = att_ref[...]
    s_ref[:, :half] += dot_nt(att, rows_of(wo_own))
    s_ref[:, half:] += dot_nt(att, rows_of(wo_oth))

    @pl.when(pl.program_id(0) == pl.num_programs(0) - 1)
    def _():
        n_ref[...] = norm(s_ref[...], gain_ref[...]).astype(BF16)


def output_and_norm(x, att, gain, own, oth, qcols):
    rows, width = x.shape
    shards = own.shape[1]
    wo = weight_spec(own, qcols, lambda z: (0, z, 0, 2))
    return call(
        out_kernel,
        (shape(rows, width, dtype=F32), shape(rows, width)),
        (shards,),
        [whole(x), pl.BlockSpec((rows, qcols), lambda z: (0, z)), whole(gain), wo, wo],
        (fixed(rows, width), fixed(rows, width)),
    )(x, att, gain, own, oth)


def ffn_kernel(n_ref, r_ref, own_ref, oth_ref, y_ref, dn_ref, gown_ref, goth_ref, nt_ref, rt_ref):
    half = n_ref.shape[1] // 2
    ff = own_ref.shape[3] // 3

    @pl.when(pl.program_id(0) == 0)
    def _():
        y_ref[...] = jnp.zeros_like(y_ref)
        dn_ref[...] = jnp.zeros_like(dn_ref)
        nt_ref[...] = n_ref[...].T
        rt_ref[...] = r_ref[...].T

    own, oth = rows_of(own_ref), rows_of(oth_ref)
    up_own, up_oth = own[:, : 2 * ff], oth[:, : 2 * ff]
    down_own, down_oth = own[:, 2 * ff :], oth[:, 2 * ff :]
    both = dot_nn(n_ref[:, :half], up_own) + dot_nn(n_ref[:, half:], up_oth)
    gate, upval = both[:, :ff], both[:, ff:]
    grad_hidden = dot_nn(r_ref[:, :half], down_own) + dot_nn(r_ref[:, half:], down_oth)
    grad_hidden = grad_hidden.astype(BF16).astype(F32)
    root = 0.7978845608028654
    square = gate * gate
    tanh = jnp.tanh(root * gate * (1.0 + 0.044715 * square))
    cdf = 0.5 * (1.0 + tanh)
    gelu = gate * cdf
    slope = cdf + 0.5 * gate * (1.0 - tanh * tanh) * root * (1.0 + 3 * 0.044715 * square)
    hidden = (gelu * upval).astype(BF16)
    grad_gate = (grad_hidden * upval * slope).astype(BF16)
    grad_up = (grad_hidden * gelu).astype(BF16)
    grad_both = jnp.concatenate([grad_gate, grad_up], axis=1)
    y_ref[:, :half] += dot_nt(hidden, down_own)
    y_ref[:, half:] += dot_nt(hidden, down_oth)
    dn_ref[:, :half] += dot_nt(grad_both, up_own)
    dn_ref[:, half:] += dot_nt(grad_both, up_oth)
    cols, _, blk, _ = gown_ref.shape
    for ref, first in ((gown_ref, 0), (goth_ref, half)):
        grad = dot_nn(nt_ref[first : first + half, :], grad_both).astype(BF16)
        ref[:, 0, :, : 2 * ff] = grad.reshape(cols, blk, 2 * ff)
        grad = dot_nn(rt_ref[first : first + half, :], hidden).astype(BF16)
        ref[:, 0, :, 2 * ff :] = grad.reshape(cols, blk, ff)


def feed_forward(n, r, own, oth):
    rows, width = n.shape
    cols, shards, blk, packed = own.shape
    spec = weight_spec(own, packed, lambda z: (0, z, 0, 0))
    return call(
        ffn_kernel,
        (
            shape(rows, width, dtype=F32),
            shape(rows, width, dtype=F32),
            shape(*own.shape),
            shape(*own.shape),
        ),
        (shards,),
        [whole(n), whole(r), spec, spec],
        (fixed(rows, width), fixed(rows, width), spec, spec),
        [pltpu.VMEM((width, rows), BF16), pltpu.VMEM((width, rows), BF16)],
    )(n, r, own, oth)


def after_ffn_kernel(
    s_ref, ya_ref, yb_ref, da_ref, db_ref, cot_ref, gain_ref, wo_own, wo_oth,
    out_ref, new_ref, round_ref, gg_ref, ga_ref,
):
    half = s_ref.shape[1] // 2

    @pl.when(pl.program_id(0) == 0)
    def _():
        s = s_ref[...]
        out_ref[...] = (s + ya_ref[...] + yb_ref[...]).astype(BF16)
        dv, gg = norm_back(s, gain_ref[...], da_ref[...] + db_ref[...])
        gg_ref[...] = gg
        new = cot_ref[...].astype(F32) + dv
        new_ref[...] = new
        round_ref[...] = new.astype(BF16)

    out = dot_nn(round_ref[:, :half], rows_of(wo_own)) + dot_nn(round_ref[:, half:], rows_of(wo_oth))
    ga_ref[...] = out.astype(BF16)


def after_ffn(s, ya, yb, da, db, cot, gain, own, oth, qcols):
    rows, width = s.shape
    shards = own.shape[1]
    wo = weight_spec(own, qcols, lambda z: (0, z, 0, 2))
    full = fixed(rows, width)
    return call(
        after_ffn_kernel,
        (
            shape(rows, width),
            shape(rows, width, dtype=F32),
            shape(rows, width),
            shape(1, width, dtype=F32),
            shape(rows, shards * qcols),
        ),
        (shards,),
        [full] * 6 + [whole(gain), wo, wo],
        (full, full, full, fixed(1, width), pl.BlockSpec((rows, qcols), lambda z: (0, z))),
    )(s, ya, yb, da, db, cot, gain, own, oth)


def slab_kernel(base_ref, out_ref):
    base = base_ref[0]
    eight = jnp.concatenate([base] + [pltpu.roll(base, i, 1) for i in range(1, 8)], axis=0)
    for block in range(out_ref.shape[1] // 8):
        moved = eight if block == 0 else pltpu.roll(eight, 8 * block, 1)
        out_ref[0, 8 * block : 8 * block + 8, :] = moved


def bias_slabs(distance_bias):
    heads, length = distance_bias.shape
    width = length + 128
    base = jnp.pad(distance_bias, ((0, 0), (128, 0))).reshape(heads, 1, width)
    return call(
        slab_kernel,
        shape(heads, 128, width, dtype=F32),
        (heads,),
        [pl.BlockSpec((1, 1, width), lambda h: (h, 0, 0))],
        pl.BlockSpec((1, 128, width), lambda h: (h, 0, 0)),
    )(base)


def stack_heads(block, low_lanes):
    lanes = lax.broadcasted_iota(jnp.int32, block.shape, 1) < HEAD_DIM
    wide = block.astype(F32)
    moved = pltpu.roll(wide, HEAD_DIM, 1)
    if low_lanes:
        parts = [jnp.where(lanes, wide, 0.0), jnp.where(lanes, moved, 0.0)]
    else:
        parts = [jnp.where(lanes, 0.0, moved), jnp.where(lanes, 0.0, wide)]
    return jnp.concatenate(parts, axis=0).astype(BF16)


def join_heads(transposed, rows, first):
    parts = [transposed[first : first + HEAD_DIM, :rows], transposed[first : first + HEAD_DIM, rows:]]
    return jnp.concatenate(parts, axis=0).T


def allowed_mask(kseg, qseg, causal):
    allowed = kseg == qseg
    if causal:
        keys, rows = allowed.shape
        key_at = lax.broadcasted_iota(jnp.int32, allowed.shape, 0) - (keys - rows)
        row_at = lax.broadcasted_iota(jnp.int32, allowed.shape, 1)
        allowed = allowed & (key_at <= row_at)
    return allowed


def head_bias(slab_ref, head, keys, rows):
    blocks = keys // 128
    last = keys - rows
    parts = []
    for block in range(blocks):
        at = last - 128 * block + 128
        parts.append(slab_ref[head, :, at : at + rows])
    return jnp.concatenate(parts, axis=0)


def attend_block(keys, rows, kv, q_ref, kseg, qseg, slab_ref, att_ref, lse_ref):
    stacked = stack_heads(q_ref[...], True)
    scores = dot_nt(kv, stacked)
    allowed = allowed_mask(kseg, qseg, slab_ref is not None)
    outs = []
    for head in range(2):
        part = scores[:, head * rows : (head + 1) * rows]
        if slab_ref is not None:
            part = part + head_bias(slab_ref, head, keys, rows)
        part = jnp.where(allowed, part, MASKED)
        top = jnp.max(part, axis=0, keepdims=True)
        grown = jnp.exp(part - top)
        total = jnp.sum(grown, axis=0, keepdims=True)
        probs = (grown * (1.0 / total)).astype(BF16)
        outs.append(dot_tn(kv, probs))
        lse_ref[0, :, head * rows : (head + 1) * rows] = top + jnp.log(total)
    att_ref[...] = join_heads(jnp.concatenate(outs, axis=1), rows, HEAD_DIM).astype(BF16)


def sort_keys(ids_ref, own_ref, oth_ref, sorted_ref):
    rows = sorted_ref.shape[1]
    for slot in range(4):
        source = own_ref if slot < 2 else oth_ref
        at = (slot % 2) * rows
        sorted_ref[ids_ref[slot]] = source[at : at + rows, :]


def self_kernel(ids_ref, q_ref, own_ref, oth_ref, slab_ref, kseg_ref, qseg_ref, att_ref, lse_ref, sorted_ref):
    rows = q_ref.shape[0]

    @pl.when(pl.program_id(1) == 0)
    def _():
        sort_keys(ids_ref, own_ref, oth_ref, sorted_ref)

    mine = ids_ref[pl.program_id(1)]
    for count in range(1, 5):

        @pl.when(mine == count - 1)
        def _(count=count):
            keys = count * rows
            kv = sorted_ref[0:count].reshape(keys, PAIR)
            attend_block(
                keys, rows, kv, q_ref, kseg_ref[0:keys, :], qseg_ref[0], slab_ref, att_ref, lse_ref
            )


def attention_specs(rows, groups):
    block = pl.BlockSpec((rows, PAIR), lambda g, s, *_: (s, g))
    lse = pl.BlockSpec((1, 1, 2 * rows), lambda g, s, *_: (2 * g + s, 0, 0))
    qseg = pl.BlockSpec((1, 1, rows), lambda g, s, *_: (s, 0, 0))
    return block, lse, qseg


def group_spec(array):
    return pl.BlockSpec((array.shape[0], PAIR), lambda g, s, *_: (0, g))


def self_attention(ids, q, own, oth, slabs, kseg, qseg):
    rows, groups = q.shape[0] // 2, q.shape[1] // PAIR
    block, lse, qs = attention_specs(rows, groups)
    slab = pl.BlockSpec((2,) + slabs.shape[1:], lambda g, s, *_: (g, 0, 0))
    return call(
        self_kernel,
        (shape(*q.shape), shape(2 * groups, 1, 2 * rows, dtype=F32)),
        (groups, 2),
        [block, group_spec(own), group_spec(oth), slab, whole(kseg), qs],
        (block, lse),
        [pltpu.VMEM((4, rows, PAIR), BF16)],
        1,
    )(ids, q, own, oth, slabs, kseg, qseg)


def cross_kernel(q_ref, own_ref, oth_ref, kseg_ref, qseg_ref, att_ref, lse_ref):
    kv = jnp.concatenate([own_ref[...], oth_ref[...]], axis=0)
    attend_block(
        kv.shape[0], q_ref.shape[0], kv, q_ref, kseg_ref[...], qseg_ref[0], None, att_ref, lse_ref
    )


def cross_attention(q, own, oth, kseg, qseg):
    rows, groups = q.shape[0] // 2, q.shape[1] // PAIR
    block, lse, qs = attention_specs(rows, groups)
    return call(
        cross_kernel,
        (shape(*q.shape), shape(2 * groups, 1, 2 * rows, dtype=F32)),
        (groups, 2),
        [block, group_spec(own), group_spec(oth), whole(kseg), qs],
        (block, lse),
    )(q, own, oth, kseg, qseg)


def back_block(keys, rows, kv, q_ref, ga_ref, lse_ref, kseg, qseg, slab_ref, dslab_ref, dq_ref):
    stacked = stack_heads(q_ref[...], True)
    stacked_grad = stack_heads(ga_ref[...], False)
    scores = dot_nt(kv, stacked)
    grad_probs = dot_nt(kv, stacked_grad)
    allowed = allowed_mask(kseg, qseg, slab_ref is not None)
    queries, grad_kv = [], 0.0
    for head in range(2):
        span = slice(head * rows, (head + 1) * rows)
        part = scores[:, span]
        if slab_ref is not None:
            part = part + head_bias(slab_ref, head, keys, rows)
        part = jnp.where(allowed, part, MASKED)
        probs = jnp.exp(part - lse_ref[0, :, span])
        grad = grad_probs[:, span]
        inner = jnp.sum(probs * grad, axis=0, keepdims=True)
        grad_scores = probs * (grad - inner)
        low = grad_scores.astype(BF16)
        grad_kv = grad_kv + dot_nn(low, stacked[span, :])
        grad_kv = grad_kv + dot_nn(probs.astype(BF16), stacked_grad[span, :])
        queries.append(dot_tn(kv, low))
        if slab_ref is not None:
            last = keys - rows
            for block in range(keys // 128):
                at = last - 128 * block + 128
                dslab_ref[head, :, at : at + rows] += grad_scores[128 * block : 128 * block + 128, :]
    dq_ref[...] = join_heads(jnp.concatenate(queries, axis=1), rows, 0).astype(BF16)
    return grad_kv


def self_back_kernel(
    ids_ref, q_ref, ga_ref, lse_ref, own_ref, oth_ref, slab_ref, kseg_ref, qseg_ref,
    dq_ref, down_ref, doth_ref, fold_ref, sorted_ref, dsorted_ref, dslab_ref,
):
    rows = q_ref.shape[0]

    @pl.when(pl.program_id(1) == 0)
    def _():
        sort_keys(ids_ref, own_ref, oth_ref, sorted_ref)
        dsorted_ref[...] = jnp.zeros_like(dsorted_ref)
        dslab_ref[...] = jnp.zeros_like(dslab_ref)

    mine = ids_ref[pl.program_id(1)]
    for count in range(1, 5):

        @pl.when(mine == count - 1)
        def _(count=count):
            keys = count * rows
            kv = sorted_ref[0:count].reshape(keys, PAIR)
            grad_kv = back_block(
                keys, rows, kv, q_ref, ga_ref, lse_ref, kseg_ref[0:keys, :], qseg_ref[0],
                slab_ref, dslab_ref, dq_ref,
            )
            dsorted_ref[0:count] += grad_kv.reshape(count, rows, PAIR)

    @pl.when(pl.program_id(1) == 1)
    def _():
        for slot in range(4):
            at = (slot % 2) * rows
            value = dsorted_ref[ids_ref[slot]]
            target = down_ref if slot < 2 else doth_ref
            target[at : at + rows, :] = value.astype(target.dtype)
        width = dslab_ref.shape[2]
        for head in range(2):
            folded = dslab_ref[head]
            count = folded.shape[0] // 2
            while count >= 8:
                folded = folded[:count] + pltpu.roll(folded[count:], width - count, 1)
                count //= 2
            fold_ref[head] = folded


def self_attention_back(ids, q, ga, lses, own, oth, slabs, kseg, qseg):
    rows, groups = q.shape[0] // 2, q.shape[1] // PAIR
    block, lse, qs = attention_specs(rows, groups)
    heads, _, width = slabs.shape
    slab = pl.BlockSpec((2,) + slabs.shape[1:], lambda g, s, *_: (g, 0, 0))
    return call(
        self_back_kernel,
        (
            shape(*q.shape),
            shape(*own.shape, dtype=F32),
            shape(*own.shape),
            shape(heads, 8, width, dtype=F32),
        ),
        (groups, 2),
        [block, block, lse, group_spec(own), group_spec(oth), slab, whole(kseg), qs],
        (
            block,
            group_spec(own),
            group_spec(own),
            pl.BlockSpec((2, 8, width), lambda g, s, *_: (g, 0, 0)),
        ),
        [
            pltpu.VMEM((4, rows, PAIR), BF16),
            pltpu.VMEM((4, rows, PAIR), F32),
            pltpu.VMEM((2, 128, width), F32),
        ],
        1,
    )(ids, q, ga, lses, own, oth, slabs, kseg, qseg)


def cross_back_kernel(
    q_ref, ga_ref, lse_ref, own_ref, oth_ref, kseg_ref, qseg_ref, dq_ref, down_ref, doth_ref, acc_ref
):
    kv = jnp.concatenate([own_ref[...], oth_ref[...]], axis=0)
    grad_kv = back_block(
        kv.shape[0], q_ref.shape[0], kv, q_ref, ga_ref, lse_ref, kseg_ref[...], qseg_ref[0],
        None, None, dq_ref,
    )
    half = own_ref.shape[0]

    @pl.when(pl.program_id(1) == 0)
    def _():
        acc_ref[...] = grad_kv

    @pl.when(pl.program_id(1) == 1)
    def _():
        total = acc_ref[...] + grad_kv
        down_ref[...] = total[:half]
        doth_ref[...] = total[half:].astype(BF16)


def cross_attention_back(q, ga, lses, own, oth, kseg, qseg):
    rows, groups = q.shape[0] // 2, q.shape[1] // PAIR
    block, lse, qs = attention_specs(rows, groups)
    return call(
        cross_back_kernel,
        (shape(*q.shape), shape(*own.shape, dtype=F32), shape(*own.shape)),
        (groups, 2),
        [block, block, lse, group_spec(own), group_spec(oth), whole(kseg), qs],
        (block, group_spec(own), group_spec(own)),
        [pltpu.VMEM((2 * own.shape[0], PAIR), F32)],
    )(q, ga, lses, own, oth, kseg, qseg)


def weight_grads(half, parts, own_ref, oth_ref):
    for ref, first in ((own_ref, 0), (oth_ref, half)):
        for left, right, at in parts:
            grad = dot_nn(left[first : first + half, :], right).astype(BF16)
            cols, _, blk, _ = ref.shape
            ref[:, 0, :, at : at + right.shape[1]] = grad.reshape(cols, blk, right.shape[1])


def cross_post_kernel(
    shards, dq_ref, dko_ref, dkr_ref, n_ref, mem_ref, r_ref, att_ref, s_ref, cot_ref, gain_ref,
    own_ref, oth_ref, wo_own, wo_oth,
    gown_ref, goth_ref, new_ref, round_ref, gg_ref, dmem_ref, ga_ref,
    dn_ref, dmo_ref, nt_ref, mt_ref, rt_ref,
):
    step = pl.program_id(0)
    half = n_ref.shape[1] // 2
    qcols = dq_ref.shape[1]

    @pl.when(step == 0)
    def _():
        dn_ref[...] = jnp.zeros_like(dn_ref)
        dmo_ref[...] = jnp.zeros_like(dmo_ref)
        nt_ref[...] = n_ref[...].T
        mt_ref[...] = mem_ref[...].T
        rt_ref[...] = r_ref[...].T

    @pl.when(step < shards)
    def _():
        dq = dq_ref[...]
        dkv = (dko_ref[...] + dkr_ref[...].astype(F32)).astype(BF16)
        own, oth = rows_of(own_ref), rows_of(oth_ref)
        parts = ((nt_ref, dq, 0), (mt_ref, dkv, qcols), (rt_ref, att_ref[...], 2 * qcols))
        weight_grads(half, parts, gown_ref, goth_ref)
        for w, span in ((own, slice(0, half)), (oth, slice(half, 2 * half))):
            dn_ref[:, span] += dot_nt(dq, w[:, :qcols])
            dmo_ref[:, span] += dot_nt(dkv, w[:, qcols : 2 * qcols])

    @pl.when(step == shards - 1)
    def _():
        dmem_ref[...] = dmo_ref[...].astype(BF16)
        dv, gg = norm_back(s_ref[...], gain_ref[...], dn_ref[...])
        gg_ref[...] = gg
        new = cot_ref[...] + dv
        new_ref[...] = new
        round_ref[...] = new.astype(BF16)

    @pl.when(step >= shards)
    def _():
        r = round_ref[...]
        out = dot_nn(r[:, :half], rows_of(wo_own)) + dot_nn(r[:, half:], rows_of(wo_oth))
        ga_ref[...] = out.astype(BF16)


def cross_post(dq, dko, dkr, n, mem, r, att, s, cot, gain, own, oth, next_own, next_oth, qcols):
    rows, width = n.shape
    cols, shards, blk, packed = own.shape
    first = lambda i: jnp.minimum(i, shards - 1)
    second = lambda i: jnp.maximum(i - shards, 0)
    spec = weight_spec(own, packed, lambda i: (0, first(i), 0, 0))
    wo = weight_spec(own, qcols, lambda i: (0, second(i), 0, 2))
    enc_rows = mem.shape[0]
    by_shard = pl.BlockSpec((rows, qcols), lambda i: (0, first(i)))
    enc_by_shard = pl.BlockSpec((enc_rows, qcols), lambda i: (0, first(i)))
    full = fixed(rows, width)
    return call(
        functools.partial(cross_post_kernel, shards),
        (
            shape(*own.shape),
            shape(*own.shape),
            shape(rows, width, dtype=F32),
            shape(rows, width),
            shape(1, width, dtype=F32),
            shape(enc_rows, width),
            shape(rows, shards * qcols),
        ),
        (2 * shards,),
        [by_shard, enc_by_shard, enc_by_shard, full, whole(mem), full, by_shard, full, full]
        + [whole(gain), spec, spec, wo, wo],
        (
            spec,
            spec,
            full,
            full,
            fixed(1, width),
            fixed(enc_rows, width),
            pl.BlockSpec((rows, qcols), lambda i: (0, second(i))),
        ),
        [
            pltpu.VMEM((rows, width), F32),
            pltpu.VMEM((enc_rows, width), F32),
            pltpu.VMEM((width, rows), BF16),
            pltpu.VMEM((width, enc_rows), BF16),
            pltpu.VMEM((width, rows), BF16),
        ],
    )(dq, dko, dkr, n, mem, r, att, s, cot, gain, own, oth, next_own, next_oth)


def self_post_kernel(
    dq_ref, dko_ref, dkr_ref, n_ref, r_ref, att_ref, x_ref, cot_ref, gain_ref, own_ref, oth_ref,
    gown_ref, goth_ref, out_ref, gg_ref, dn_ref, nt_ref, rt_ref,
):
    step = pl.program_id(0)
    half = n_ref.shape[1] // 2
    qcols = dq_ref.shape[1]

    @pl.when(step == 0)
    def _():
        dn_ref[...] = jnp.zeros_like(dn_ref)
        nt_ref[...] = n_ref[...].T
        rt_ref[...] = r_ref[...].T

    dkv = (dko_ref[...] + dkr_ref[...].astype(F32)).astype(BF16)
    grad = jnp.concatenate([dq_ref[...], dkv], axis=1)
    own, oth = rows_of(own_ref), rows_of(oth_ref)
    parts = ((nt_ref, grad, 0), (rt_ref, att_ref[...], 2 * qcols))
    weight_grads(half, parts, gown_ref, goth_ref)
    dn_ref[:, :half] += dot_nt(grad, own[:, : 2 * qcols])
    dn_ref[:, half:] += dot_nt(grad, oth[:, : 2 * qcols])

    @pl.when(step == pl.num_programs(0) - 1)
    def _():
        dv, gg = norm_back(x_ref[...].astype(F32), gain_ref[...], dn_ref[...])
        gg_ref[...] = gg
        out_ref[...] = (cot_ref[...] + dv).astype(BF16)


def self_post(dq, dko, dkr, n, r, att, x, cot, gain, own, oth, qcols):
    rows, width = n.shape
    cols, shards, blk, packed = own.shape
    spec = weight_spec(own, packed, lambda i: (0, i, 0, 0))
    by_shard = pl.BlockSpec((rows, qcols), lambda i: (0, i))
    full = fixed(rows, width)
    return call(
        self_post_kernel,
        (shape(*own.shape), shape(*own.shape), shape(rows, width), shape(1, width, dtype=F32)),
        (shards,),
        [by_shard, by_shard, by_shard, full, full, by_shard, full, full, whole(gain), spec, spec],
        (spec, spec, full, fixed(1, width)),
        [
            pltpu.VMEM((rows, width), F32),
            pltpu.VMEM((width, rows), BF16),
            pltpu.VMEM((width, rows), BF16),
        ],
    )(dq, dko, dkr, n, r, att, x, cot, gain, own, oth)


def make_per_device(batch, shards):
    cols = batch // 2
    bits = cols.bit_length() - 1
    assert batch == 2 * (1 << bits) and shards == 4

    def swap(array, mask):
        return lax.ppermute(array, "batch", [(b, b ^ mask) for b in range(batch)])

    def in_order(position):
        return ((position % cols) << 1) | (position // cols)

    def place_of(difference):
        return (difference >> 1) | ((difference & 1) * cols)

    def to_relative(array):
        me = lax.axis_index("batch")
        blk = array.shape[-1] // batch
        parts = [
            lax.dynamic_slice_in_dim(array, (me ^ in_order(p)) * blk, blk, array.ndim - 1)
            for p in range(batch)
        ]
        return jnp.concatenate(parts, axis=-1)

    def to_absolute(array):
        me = lax.axis_index("batch")
        blk = array.shape[-1] // batch
        parts = [
            lax.dynamic_slice_in_dim(array, place_of(me ^ p) * blk, blk, array.ndim - 1)
            for p in range(batch)
        ]
        return jnp.concatenate(parts, axis=-1)

    def core_of(z):
        return 0 if z in (0, 3) else 1

    routes = []
    for second in (0, 1):
        route = []
        for b in range(batch):
            for z in range(shards):
                micro = (z // 2) ^ second
                target = ((b - b % 2) + core_of(z)) * shards + 2 * micro + b % 2
                route.append((b * shards + z, target))
        routes.append(route)
    both = ("batch", "group")

    def to_sequence(array):
        first = lax.axis_index("group") // 2
        received = []
        for second, route in enumerate(routes):
            part = lax.dynamic_index_in_dim(array, first ^ second, 0, keepdims=False)
            received.append(lax.ppermute(part, both, route))
        return to_relative(jnp.concatenate(received, axis=0))

    def from_sequence(array):
        array = to_absolute(array)
        rows = array.shape[0] // 2
        back = [
            lax.ppermute(array[i * rows : (i + 1) * rows], both, [(t, s) for s, t in route])
            for i, route in enumerate(routes)
        ]
        first = lax.axis_index("group") // 2
        return jnp.where(first == 0, jnp.stack(back), jnp.stack(back[::-1]))

    def spread(piece, order):
        array = piece.reshape((1,) * bits + piece.shape)
        for bit in order:
            axis = bits - 1 - bit
            array = jnp.concatenate([array, swap(array, 2 << bit)], axis=axis)
        own = array.reshape((cols,) + piece.shape)
        return own, swap(own, 1)

    def collect(own, oth, order):
        total = own.astype(F32) + swap(oth, 1).astype(F32)
        piece = total.shape[1:]
        total = total.reshape((2,) * bits + piece)
        for bit in order:
            axis = bits - 1 - bit
            keep = lax.slice_in_dim(total, 0, 1, axis=axis)
            send = lax.slice_in_dim(total, 1, 2, axis=axis).astype(BF16)
            total = keep + swap(send, 2 << bit).astype(F32)
        return total.reshape(piece).astype(BF16)

    def per_device(
        tokens, memory, dec_segments, enc_segments, buckets,
        self_gain, self_query, self_key, self_value, self_output, rel_bias,
        cross_gain, cross_query, cross_key, cross_value, cross_output,
        ffn_gain, ffn_gate, ffn_up, ffn_down, out_grad,
    ):
        me, z = lax.axis_index("batch"), lax.axis_index("group")
        core, micro, owner = me % 2, z // 2, z % 2
        width = tokens.shape[2]
        blk = width // batch
        qcols = self_query.shape[1]
        chunk, enc_chunk = tokens.shape[1], memory.shape[1]
        up = tuple(range(bits))
        down = up[::-1]

        def interleaved(keys, values):
            parts = []
            for at in range(0, keys.shape[1], HEAD_DIM):
                parts += [keys[:, at : at + HEAD_DIM], values[:, at : at + HEAD_DIM]]
            return jnp.concatenate(parts, axis=1)

        def my_rows(weight):
            return lax.dynamic_slice_in_dim(weight, me * blk, blk, 0)

        def my_cols(weight):
            return lax.dynamic_slice_in_dim(weight, me * blk, blk, 1).T

        def gathered(parts):
            return lax.all_gather(jnp.concatenate(parts, axis=1), "group", axis=0, tiled=False)

        stream = to_sequence(tokens)
        self_piece = gathered(
            [my_rows(self_query), interleaved(my_rows(self_key), my_rows(self_value)), my_cols(self_output)]
        )
        self_own, self_oth = spread(self_piece, up)
        encoder = to_sequence(memory)
        cross_piece = gathered(
            [my_rows(cross_query), interleaved(my_rows(cross_key), my_rows(cross_value)), my_cols(cross_output)]
        )
        cross_own, cross_oth = spread(cross_piece, down)
        ffn_piece = gathered([my_rows(ffn_gate), my_rows(ffn_up), my_cols(ffn_down)])
        ffn_parts = [spread(ffn_piece[:2], up), spread(ffn_piece[2:], down)]
        cot = to_sequence(out_grad)

        segments = jnp.concatenate([dec_segments, enc_segments], axis=1)
        length = dec_segments.shape[1]
        chosen = jnp.where(owner == core, segments, swap(segments, 1))
        chosen = lax.dynamic_index_in_dim(chosen, micro, 0, keepdims=False)
        dec_seg, enc_seg = chosen[:length], chosen[length:]

        def ids_of(which):
            first = jnp.where(micro == 0, which, 3 - which)
            return [first, 3 - first]

        ids = jnp.stack(ids_of(core) + ids_of(1 - core)).astype(jnp.int32)

        def pieces_of(seg, size, count):
            return [lax.dynamic_slice_in_dim(seg, ids[i] * size, size, 0) for i in range(count)]

        qseg = jnp.stack(pieces_of(dec_seg, chunk, 2)).reshape(2, 1, chunk)
        kseg = dec_seg.reshape(length, 1)
        enc_kseg = jnp.concatenate(pieces_of(enc_seg, enc_chunk, 4)).reshape(-1, 1)

        all_bias = lax.all_gather(rel_bias, "group", axis=1, tiled=True)
        bucket_count = rel_bias.shape[0]
        onehot = (buckets[:, None] == jnp.arange(bucket_count)[None, :]).astype(F32)
        distance_bias = lax.dot_general(
            all_bias, onehot, (((0,), (1,)), ((), ())), precision=HIGHEST, preferred_element_type=F32
        )
        slabs = bias_slabs(distance_bias)
        gain_one, gain_two, gain_three = (
            to_relative(gain.reshape(1, width)) for gain in (self_gain, cross_gain, ffn_gain)
        )

        n_one, q_one, kv_one = project_qkv(stream, gain_one, self_own, self_oth, qcols)
        kv_one_oth = swap(kv_one, 1)
        att_one, lse_one = self_attention(ids, q_one, kv_one, kv_one_oth, slabs, kseg, qseg)
        kv_two = project_kv(encoder, cross_own, cross_oth, qcols)
        kv_two_oth = swap(kv_two, 1)
        stream_one, n_two, q_two = output_and_query(
            stream, att_one, gain_two, self_own, self_oth, cross_own, cross_oth, qcols
        )
        att_two, lse_two = cross_attention(q_two, kv_two, kv_two_oth, enc_kseg, qseg)
        stream_two, n_three = output_and_norm(stream_one, att_two, gain_three, cross_own, cross_oth, qcols)

        ffn_sums, ffn_grads = [], []
        for (own, oth), order in zip(ffn_parts, (down, up)):
            y, dn, grad_own, grad_oth = feed_forward(n_three, cot, own, oth)
            ffn_sums.append((y, dn))
            ffn_grads.append(collect(grad_own, grad_oth, order))
        (ya, da), (yb, db) = ffn_sums
        block_out, cot_two, round_two, grad_gain_three, ga_two = after_ffn(
            stream_two, ya, yb, da, db, cot, gain_three, cross_own, cross_oth, qcols
        )
        block_out = from_sequence(block_out)

        dq_two, dkv_two, dkv_two_send = cross_attention_back(
            q_two, ga_two, lse_two, kv_two, kv_two_oth, enc_kseg, qseg
        )
        grad_own, grad_oth, cot_one, round_one, grad_gain_two, memory_grad, ga_one = cross_post(
            dq_two, dkv_two, swap(dkv_two_send, 1), n_two, encoder, round_two, att_two, stream_one,
            cot_two, gain_two, cross_own, cross_oth, self_own, self_oth, qcols,
        )
        cross_grads = collect(grad_own, grad_oth, down)
        memory_grad = from_sequence(memory_grad).astype(F32)
        dq_one, dkv_one, dkv_one_send, folded = self_attention_back(
            ids, q_one, ga_one, lse_one, kv_one, kv_one_oth, slabs, kseg, qseg
        )
        grad_own, grad_oth, tokens_grad, grad_gain_one = self_post(
            dq_one, dkv_one, swap(dkv_one_send, 1), n_one, round_one, att_one, stream, cot_one,
            gain_one, self_own, self_oth, qcols,
        )
        self_grads = collect(grad_own, grad_oth, up)
        tokens_grad = from_sequence(tokens_grad).astype(F32)

        def finish(piece):
            mine = lax.psum_scatter(piece, "group", scatter_dimension=0, tiled=False)
            return lax.all_gather(mine, "batch", axis=0, tiled=True)

        ffn_final = finish(jnp.concatenate(ffn_grads, axis=0))
        cross_final = finish(cross_grads)
        self_final = finish(self_grads)

        padded = jnp.pad(folded, ((0, 0), (0, 0), (0, 8)))
        distance_grad = sum(padded[:, i, 128 + i : 128 + i + length] for i in range(8))
        bucket_grad = lax.dot_general(
            onehot, distance_grad, (((0,), (1,)), ((), ())), precision=HIGHEST, preferred_element_type=F32
        )
        small = [to_absolute(g).reshape(width) for g in (grad_gain_one, grad_gain_two, grad_gain_three)]
        small = lax.psum(jnp.concatenate(small + [bucket_grad.reshape(-1)]), both)
        gains = [small[i * width : (i + 1) * width] for i in range(3)]
        bucket_grad = small[3 * width :].reshape(bucket_grad.shape)
        heads_here = rel_bias.shape[1]
        bucket_grad = lax.dynamic_slice_in_dim(bucket_grad, z * heads_here, heads_here, 1)

        def unpack(final):
            final = final.astype(F32)
            kv = final[:, qcols : 2 * qcols].reshape(width, -1, 2, HEAD_DIM)
            return (
                final[:, :qcols],
                kv[:, :, 0, :].reshape(width, -1),
                kv[:, :, 1, :].reshape(width, -1),
                final[:, 2 * qcols :].T,
            )

        ff = ffn_gate.shape[1]
        ffn_final = ffn_final.astype(F32)
        return (
            block_out,
            tokens_grad,
            memory_grad,
            gains[0],
            *unpack(self_final),
            bucket_grad,
            gains[1],
            *unpack(cross_final),
            gains[2],
            ffn_final[:, :ff],
            ffn_final[:, ff : 2 * ff],
            ffn_final[:, 2 * ff :].T,
        )

    return per_device


def solution(mesh):
    rows, group_cols, group_rows = P(None, ("batch", "group"), None), P(None, "group"), P("group", None)
    layer = (group_cols, group_cols, group_cols, group_rows)
    return jax.shard_map(
        make_per_device(mesh.shape["batch"], mesh.shape["group"]),
        mesh=mesh,
        in_specs=(
            rows, rows, P(None, "batch"), P(None, "batch"), P(),
            P(), *layer, group_cols,
            P(), *layer,
            P(), group_cols, group_cols, group_rows, rows,
        ),
        out_specs=(
            rows, rows, rows,
            P(), *layer, group_cols,
            P(), *layer,
            P(), group_cols, group_cols, group_rows,
        ),
        check_vma=False,
    )
```

```python
import functools

import jax
import jax.numpy as jnp
from jax import lax
from jax.experimental import pallas as pl
from jax.experimental.pallas import tpu as pltpu
from jax.sharding import PartitionSpec as P

HEAD_DIM = 64
PAIR = 2 * HEAD_DIM
EPSILON = 1e-06
MASKED = -1e30
HIGHEST = lax.Precision.HIGHEST
BF16 = jnp.bfloat16
F32 = jnp.float32
FLOPS_PER_MICRO = 1_000_000_000
BYTES_PER_MICRO = 3_000_000


def dot_nn(left, right):
    return lax.dot_general(left, right, (((1,), (0,)), ((), ())), preferred_element_type=F32)


def dot_nt(left, right):
    return lax.dot_general(left, right, (((1,), (1,)), ((), ())), preferred_element_type=F32)


def dot_tn(left, right):
    return lax.dot_general(left, right, (((0,), (0,)), ((), ())), preferred_element_type=F32)


def call(kernel, outs, grid, in_specs, out_specs, scratch=(), prefetch=0, micros=5):
    return pl.pallas_call(
        kernel,
        out_shape=outs,
        cost_estimate=pl.CostEstimate(
            flops=micros * FLOPS_PER_MICRO, transcendentals=0, bytes_accessed=micros * BYTES_PER_MICRO
        ),
        grid_spec=pltpu.PrefetchScalarGridSpec(
            num_scalar_prefetch=prefetch,
            grid=grid,
            in_specs=in_specs,
            out_specs=out_specs,
            scratch_shapes=list(scratch),
        ),
        compiler_params=pltpu.CompilerParams(
            dimension_semantics=("arbitrary",) * len(grid),
        ),
    )


def shape(*dims, dtype=BF16):
    return jax.ShapeDtypeStruct(dims, dtype)


def whole(array):
    dims = array.shape
    return pl.BlockSpec(dims, lambda *ids: (0,) * len(dims))


def fixed(*dims):
    return pl.BlockSpec(dims, lambda *ids: (0,) * len(dims))


def rows_of(ref):
    block = ref[...]
    return block.reshape(block.shape[0] * block.shape[2], block.shape[3])


def store_rows(ref, value):
    ref[...] = value.reshape(ref.shape).astype(ref.dtype)


def weight_spec(weights, columns, index):
    cols, _, blk, _ = weights.shape
    return pl.BlockSpec((cols, 1, blk, columns), index)


def norm(values, gain):
    return values * lax.rsqrt(jnp.mean(values * values, axis=-1, keepdims=True) + EPSILON) * gain


def norm_back(values, gain, grad):
    scale = lax.rsqrt(jnp.mean(values * values, axis=-1, keepdims=True) + EPSILON)
    scaled = grad * gain
    inner = jnp.mean(scaled * values, axis=-1, keepdims=True)
    grad_values = scale * scaled - values * (scale * scale * scale * inner)
    grad_gain = jnp.sum(grad * values * scale, axis=0, keepdims=True)
    return grad_values, grad_gain


def qkv_kernel(x_ref, gain_ref, own_ref, oth_ref, n_ref, q_ref, kv_ref):
    half = x_ref.shape[1] // 2
    qcols = q_ref.shape[1]

    @pl.when(pl.program_id(0) == 0)
    def _():
        n_ref[...] = norm(x_ref[...].astype(F32), gain_ref[...]).astype(BF16)

    out = dot_nn(n_ref[:, :half], rows_of(own_ref)) + dot_nn(n_ref[:, half:], rows_of(oth_ref))
    q_ref[...] = out[:, :qcols].astype(BF16)
    kv_ref[...] = out[:, qcols:].astype(BF16)


def project_qkv(x, gain, own, oth, qcols):
    rows, width = x.shape
    shards = own.shape[1]
    spec = weight_spec(own, 2 * qcols, lambda z: (0, z, 0, 0))
    out = pl.BlockSpec((rows, qcols), lambda z: (0, z))
    return call(
        qkv_kernel,
        (shape(rows, width), shape(rows, shards * qcols), shape(rows, shards * qcols)),
        (shards,),
        [whole(x), whole(gain), spec, spec],
        (fixed(rows, width), out, out),
        micros=7,
    )(x, gain, own, oth)


def kv_kernel(x_ref, own_ref, oth_ref, kv_ref):
    half = x_ref.shape[1] // 2
    out = dot_nn(x_ref[:, :half], rows_of(own_ref)) + dot_nn(x_ref[:, half:], rows_of(oth_ref))
    kv_ref[...] = out.astype(BF16)


def project_kv(x, own, oth, qcols):
    rows, width = x.shape
    shards = own.shape[1]
    spec = weight_spec(own, qcols, lambda z: (0, z, 0, 1))
    return call(
        kv_kernel,
        shape(rows, shards * qcols),
        (shards,),
        [whole(x), spec, spec],
        pl.BlockSpec((rows, qcols), lambda z: (0, z)),
        micros=4,
    )(x, own, oth)


def mid_kernel(shards, x_ref, att_ref, gain_ref, wo_own, wo_oth, wq_own, wq_oth, s_ref, n_ref, q_ref):
    step = pl.program_id(0)
    half = x_ref.shape[1] // 2

    @pl.when(step == 0)
    def _():
        s_ref[...] = x_ref[...].astype(F32)

    @pl.when(step < shards)
    def _():
        att = att_ref[...]
        s_ref[:, :half] += dot_nt(att, rows_of(wo_own))
        s_ref[:, half:] += dot_nt(att, rows_of(wo_oth))

    @pl.when(step == shards - 1)
    def _():
        n_ref[...] = norm(s_ref[...], gain_ref[...]).astype(BF16)

    @pl.when(step >= shards)
    def _():
        out = dot_nn(n_ref[:, :half], rows_of(wq_own)) + dot_nn(n_ref[:, half:], rows_of(wq_oth))
        q_ref[...] = out.astype(BF16)


def output_and_query(x, att, gain, own, oth, next_own, next_oth, qcols):
    rows, width = x.shape
    shards = own.shape[1]
    first = lambda i: jnp.minimum(i, shards - 1)
    second = lambda i: jnp.maximum(i - shards, 0)
    wo = weight_spec(own, qcols, lambda i: (0, first(i), 0, 2))
    wq = weight_spec(own, qcols, lambda i: (0, second(i), 0, 0))
    return call(
        functools.partial(mid_kernel, shards),
        (shape(rows, width, dtype=F32), shape(rows, width), shape(rows, shards * qcols)),
        (2 * shards,),
        [
            whole(x),
            pl.BlockSpec((rows, qcols), lambda i: (0, first(i))),
            whole(gain),
            wo,
            wo,
            wq,
            wq,
        ],
        (
            fixed(rows, width),
            fixed(rows, width),
            pl.BlockSpec((rows, qcols), lambda i: (0, second(i))),
        ),
        micros=10,
    )(x, att, gain, own, oth, next_own, next_oth)


def out_kernel(x_ref, att_ref, gain_ref, wo_own, wo_oth, s_ref, n_ref):
    half = x_ref.shape[1] // 2

    @pl.when(pl.program_id(0) == 0)
    def _():
        s_ref[...] = x_ref[...]

    att = att_ref[...]
    s_ref[:, :half] += dot_nt(att, rows_of(wo_own))
    s_ref[:, half:] += dot_nt(att, rows_of(wo_oth))

    @pl.when(pl.program_id(0) == pl.num_programs(0) - 1)
    def _():
        n_ref[...] = norm(s_ref[...], gain_ref[...]).astype(BF16)


def output_and_norm(x, att, gain, own, oth, qcols):
    rows, width = x.shape
    shards = own.shape[1]
    wo = weight_spec(own, qcols, lambda z: (0, z, 0, 2))
    return call(
        out_kernel,
        (shape(rows, width, dtype=F32), shape(rows, width)),
        (shards,),
        [whole(x), pl.BlockSpec((rows, qcols), lambda z: (0, z)), whole(gain), wo, wo],
        (fixed(rows, width), fixed(rows, width)),
        micros=7,
    )(x, att, gain, own, oth)


def ffn_kernel(ff, n_ref, r_ref, own_ref, oth_ref, y_ref, dn_ref, gown_ref, goth_ref, nt_ref, rt_ref):
    half = n_ref.shape[1] // 2

    @pl.when(pl.program_id(0) == 0)
    def _():
        y_ref[...] = jnp.zeros_like(y_ref)
        dn_ref[...] = jnp.zeros_like(dn_ref)
        nt_ref[...] = n_ref[...].T
        rt_ref[...] = r_ref[...].T

    own, oth = rows_of(own_ref), rows_of(oth_ref)
    up_own, up_oth = own[:, : 2 * ff], oth[:, : 2 * ff]
    down_own, down_oth = own[:, 2 * ff : 3 * ff], oth[:, 2 * ff : 3 * ff]
    both = dot_nn(n_ref[:, :half], up_own) + dot_nn(n_ref[:, half:], up_oth)
    gate, upval = both[:, :ff], both[:, ff:]
    grad_hidden = dot_nn(r_ref[:, :half], down_own) + dot_nn(r_ref[:, half:], down_oth)
    grad_hidden = grad_hidden.astype(BF16).astype(F32)
    root = 0.7978845608028654
    square = gate * gate
    tanh = jnp.tanh(root * gate * (1.0 + 0.044715 * square))
    cdf = 0.5 * (1.0 + tanh)
    gelu = gate * cdf
    slope = cdf + 0.5 * gate * (1.0 - tanh * tanh) * root * (1.0 + 3 * 0.044715 * square)
    hidden = (gelu * upval).astype(BF16)
    grad_gate = (grad_hidden * upval * slope).astype(BF16)
    grad_up = (grad_hidden * gelu).astype(BF16)
    grad_both = jnp.concatenate([grad_gate, grad_up], axis=1)
    y_ref[:, :half] += dot_nt(hidden, down_own)
    y_ref[:, half:] += dot_nt(hidden, down_oth)
    dn_ref[:, :half] += dot_nt(grad_both, up_own)
    dn_ref[:, half:] += dot_nt(grad_both, up_oth)
    cols, _, blk, packed = gown_ref.shape
    for ref, first in ((gown_ref, 0), (goth_ref, half)):
        grad = dot_nn(nt_ref[first : first + half, :], grad_both).astype(BF16)
        ref[:, 0, :, : 2 * ff] = grad.reshape(cols, blk, 2 * ff)
        grad = dot_nn(rt_ref[first : first + half, :], hidden).astype(BF16)
        ref[:, 0, :, 2 * ff : 3 * ff] = grad.reshape(cols, blk, ff)
        spare = packed - 3 * ff
        if spare:
            ref[:, 0, :, 3 * ff :] = jnp.zeros((cols, blk, spare), BF16)


def feed_forward(n, r, own, oth, ff):
    rows, width = n.shape
    cols, shards, blk, packed = own.shape
    spec = weight_spec(own, packed, lambda z: (0, z, 0, 0))
    return call(
        functools.partial(ffn_kernel, ff),
        (
            shape(rows, width, dtype=F32),
            shape(rows, width, dtype=F32),
            shape(*own.shape),
            shape(*own.shape),
        ),
        (shards,),
        [whole(n), whole(r), spec, spec],
        (fixed(rows, width), fixed(rows, width), spec, spec),
        [pltpu.VMEM((width, rows), BF16), pltpu.VMEM((width, rows), BF16)],
        micros=22,
    )(n, r, own, oth)


def after_ffn_kernel(
    s_ref, ya_ref, yb_ref, da_ref, db_ref, cot_ref, gain_ref, wo_own, wo_oth,
    out_ref, new_ref, round_ref, gg_ref, ga_ref,
):
    half = s_ref.shape[1] // 2

    @pl.when(pl.program_id(0) == 0)
    def _():
        s = s_ref[...]
        out_ref[...] = (s + ya_ref[...] + yb_ref[...]).astype(BF16)
        dv, gg = norm_back(s, gain_ref[...], da_ref[...] + db_ref[...])
        gg_ref[...] = gg
        new = cot_ref[...].astype(F32) + dv
        new_ref[...] = new
        round_ref[...] = new.astype(BF16)

    out = dot_nn(round_ref[:, :half], rows_of(wo_own)) + dot_nn(round_ref[:, half:], rows_of(wo_oth))
    ga_ref[...] = out.astype(BF16)


def after_ffn(s, ya, yb, da, db, cot, gain, own, oth, qcols):
    rows, width = s.shape
    shards = own.shape[1]
    wo = weight_spec(own, qcols, lambda z: (0, z, 0, 2))
    full = fixed(rows, width)
    return call(
        after_ffn_kernel,
        (
            shape(rows, width),
            shape(rows, width, dtype=F32),
            shape(rows, width),
            shape(1, width, dtype=F32),
            shape(rows, shards * qcols),
        ),
        (shards,),
        [full] * 6 + [whole(gain), wo, wo],
        (full, full, full, fixed(1, width), pl.BlockSpec((rows, qcols), lambda z: (0, z))),
        micros=10,
    )(s, ya, yb, da, db, cot, gain, own, oth)


def slab_kernel(base_ref, out_ref):
    base = base_ref[0]
    eight = jnp.concatenate([base] + [pltpu.roll(base, i, 1) for i in range(1, 8)], axis=0)
    for block in range(out_ref.shape[1] // 8):
        moved = eight if block == 0 else pltpu.roll(eight, 8 * block, 1)
        out_ref[0, 8 * block : 8 * block + 8, :] = moved


def bias_slabs(distance_bias):
    heads, length = distance_bias.shape
    width = length + 128
    base = jnp.pad(distance_bias, ((0, 0), (128, 0))).reshape(heads, 1, width)
    return call(
        slab_kernel,
        shape(heads, 128, width, dtype=F32),
        (heads,),
        [pl.BlockSpec((1, 1, width), lambda h: (h, 0, 0))],
        pl.BlockSpec((1, 128, width), lambda h: (h, 0, 0)),
        micros=11,
    )(base)


def stack_heads(block, low_lanes):
    lanes = lax.broadcasted_iota(jnp.int32, block.shape, 1) < HEAD_DIM
    wide = block.astype(F32)
    moved = pltpu.roll(wide, HEAD_DIM, 1)
    if low_lanes:
        parts = [jnp.where(lanes, wide, 0.0), jnp.where(lanes, moved, 0.0)]
    else:
        parts = [jnp.where(lanes, 0.0, moved), jnp.where(lanes, 0.0, wide)]
    return jnp.concatenate(parts, axis=0).astype(BF16)


def join_heads(transposed, rows, first):
    parts = [transposed[first : first + HEAD_DIM, :rows], transposed[first : first + HEAD_DIM, rows:]]
    return jnp.concatenate(parts, axis=0).T


def allowed_mask(kseg, qseg, causal):
    allowed = kseg == qseg
    if causal:
        keys, rows = allowed.shape
        key_at = lax.broadcasted_iota(jnp.int32, allowed.shape, 0) - (keys - rows)
        row_at = lax.broadcasted_iota(jnp.int32, allowed.shape, 1)
        allowed = allowed & (key_at <= row_at)
    return allowed


def head_bias(slab_ref, head, keys, rows):
    blocks = keys // 128
    last = keys - rows
    parts = []
    for block in range(blocks):
        at = last - 128 * block + 128
        parts.append(slab_ref[head, :, at : at + rows])
    return jnp.concatenate(parts, axis=0)


def attend_block(keys, rows, kv, q_ref, kseg, qseg, slab_ref, att_ref, lse_ref):
    stacked = stack_heads(q_ref[...], True)
    scores = dot_nt(kv, stacked)
    allowed = allowed_mask(kseg, qseg, slab_ref is not None)
    outs = []
    for head in range(2):
        part = scores[:, head * rows : (head + 1) * rows]
        if slab_ref is not None:
            part = part + head_bias(slab_ref, head, keys, rows)
        part = jnp.where(allowed, part, MASKED)
        top = jnp.max(part, axis=0, keepdims=True)
        grown = jnp.exp(part - top)
        total = jnp.sum(grown, axis=0, keepdims=True)
        probs = (grown * (1.0 / total)).astype(BF16)
        outs.append(dot_tn(kv, probs))
        lse_ref[0, :, head * rows : (head + 1) * rows] = top + jnp.log(total)
    att_ref[...] = join_heads(jnp.concatenate(outs, axis=1), rows, HEAD_DIM).astype(BF16)


def sort_keys(ids_ref, own_ref, oth_ref, sorted_ref):
    rows = sorted_ref.shape[1]
    for slot in range(4):
        source = own_ref if slot < 2 else oth_ref
        at = (slot % 2) * rows
        sorted_ref[ids_ref[slot]] = source[at : at + rows, :]


def self_kernel(ids_ref, q_ref, own_ref, oth_ref, slab_ref, kseg_ref, qseg_ref, att_ref, lse_ref, sorted_ref):
    rows = q_ref.shape[0]

    @pl.when(pl.program_id(1) == 0)
    def _():
        sort_keys(ids_ref, own_ref, oth_ref, sorted_ref)

    mine = ids_ref[pl.program_id(1)]
    for count in range(1, 5):

        @pl.when(mine == count - 1)
        def _(count=count):
            keys = count * rows
            kv = sorted_ref[0:count].reshape(keys, PAIR)
            attend_block(
                keys, rows, kv, q_ref, kseg_ref[0:keys, :], qseg_ref[0], slab_ref, att_ref, lse_ref
            )


def attention_specs(rows, groups):
    block = pl.BlockSpec((rows, PAIR), lambda g, s, *_: (s, g))
    lse = pl.BlockSpec((1, 1, 2 * rows), lambda g, s, *_: (2 * g + s, 0, 0))
    qseg = pl.BlockSpec((1, 1, rows), lambda g, s, *_: (s, 0, 0))
    return block, lse, qseg


def group_spec(array):
    return pl.BlockSpec((array.shape[0], PAIR), lambda g, s, *_: (0, g))


def self_attention(ids, q, own, oth, slabs, kseg, qseg):
    rows, groups = q.shape[0] // 2, q.shape[1] // PAIR
    block, lse, qs = attention_specs(rows, groups)
    slab = pl.BlockSpec((2,) + slabs.shape[1:], lambda g, s, *_: (g, 0, 0))
    return call(
        self_kernel,
        (shape(*q.shape), shape(2 * groups, 1, 2 * rows, dtype=F32)),
        (groups, 2),
        [block, group_spec(own), group_spec(oth), slab, whole(kseg), qs],
        (block, lse),
        [pltpu.VMEM((4, rows, PAIR), BF16)],
        prefetch=1,
        micros=20,
    )(ids, q, own, oth, slabs, kseg, qseg)


def cross_kernel(q_ref, own_ref, oth_ref, kseg_ref, qseg_ref, att_ref, lse_ref):
    kv = jnp.concatenate([own_ref[...], oth_ref[...]], axis=0)
    attend_block(
        kv.shape[0], q_ref.shape[0], kv, q_ref, kseg_ref[...], qseg_ref[0], None, att_ref, lse_ref
    )


def cross_attention(q, own, oth, kseg, qseg):
    rows, groups = q.shape[0] // 2, q.shape[1] // PAIR
    block, lse, qs = attention_specs(rows, groups)
    return call(
        cross_kernel,
        (shape(*q.shape), shape(2 * groups, 1, 2 * rows, dtype=F32)),
        (groups, 2),
        [block, group_spec(own), group_spec(oth), whole(kseg), qs],
        (block, lse),
        micros=16,
    )(q, own, oth, kseg, qseg)


def back_block(keys, rows, kv, q_ref, ga_ref, lse_ref, kseg, qseg, slab_ref, dslab_ref, dq_ref):
    stacked = stack_heads(q_ref[...], True)
    stacked_grad = stack_heads(ga_ref[...], False)
    scores = dot_nt(kv, stacked)
    grad_probs = dot_nt(kv, stacked_grad)
    allowed = allowed_mask(kseg, qseg, slab_ref is not None)
    queries, grad_kv = [], 0.0
    for head in range(2):
        span = slice(head * rows, (head + 1) * rows)
        part = scores[:, span]
        if slab_ref is not None:
            part = part + head_bias(slab_ref, head, keys, rows)
        part = jnp.where(allowed, part, MASKED)
        probs = jnp.exp(part - lse_ref[0, :, span])
        grad = grad_probs[:, span]
        inner = jnp.sum(probs * grad, axis=0, keepdims=True)
        grad_scores = probs * (grad - inner)
        low = grad_scores.astype(BF16)
        grad_kv = grad_kv + dot_nn(low, stacked[span, :])
        grad_kv = grad_kv + dot_nn(probs.astype(BF16), stacked_grad[span, :])
        queries.append(dot_tn(kv, low))
        if slab_ref is not None:
            last = keys - rows
            for block in range(keys // 128):
                at = last - 128 * block + 128
                dslab_ref[head, :, at : at + rows] += grad_scores[128 * block : 128 * block + 128, :]
    dq_ref[...] = join_heads(jnp.concatenate(queries, axis=1), rows, 0).astype(BF16)
    return grad_kv


def self_back_kernel(
    ids_ref, q_ref, ga_ref, lse_ref, own_ref, oth_ref, slab_ref, kseg_ref, qseg_ref,
    dq_ref, down_ref, doth_ref, fold_ref, sorted_ref, dsorted_ref, dslab_ref,
):
    rows = q_ref.shape[0]

    @pl.when(pl.program_id(1) == 0)
    def _():
        sort_keys(ids_ref, own_ref, oth_ref, sorted_ref)
        dsorted_ref[...] = jnp.zeros_like(dsorted_ref)
        dslab_ref[...] = jnp.zeros_like(dslab_ref)

    mine = ids_ref[pl.program_id(1)]
    for count in range(1, 5):

        @pl.when(mine == count - 1)
        def _(count=count):
            keys = count * rows
            kv = sorted_ref[0:count].reshape(keys, PAIR)
            grad_kv = back_block(
                keys, rows, kv, q_ref, ga_ref, lse_ref, kseg_ref[0:keys, :], qseg_ref[0],
                slab_ref, dslab_ref, dq_ref,
            )
            dsorted_ref[0:count] += grad_kv.reshape(count, rows, PAIR)

    @pl.when(pl.program_id(1) == 1)
    def _():
        for slot in range(4):
            at = (slot % 2) * rows
            value = dsorted_ref[ids_ref[slot]]
            target = down_ref if slot < 2 else doth_ref
            target[at : at + rows, :] = value.astype(target.dtype)
        width = dslab_ref.shape[2]
        for head in range(2):
            folded = dslab_ref[head]
            count = folded.shape[0] // 2
            while count >= 8:
                folded = folded[:count] + pltpu.roll(folded[count:], width - count, 1)
                count //= 2
            fold_ref[head] = folded


def self_attention_back(ids, q, ga, lses, own, oth, slabs, kseg, qseg):
    rows, groups = q.shape[0] // 2, q.shape[1] // PAIR
    block, lse, qs = attention_specs(rows, groups)
    heads, _, width = slabs.shape
    slab = pl.BlockSpec((2,) + slabs.shape[1:], lambda g, s, *_: (g, 0, 0))
    return call(
        self_back_kernel,
        (
            shape(*q.shape),
            shape(*own.shape, dtype=F32),
            shape(*own.shape),
            shape(heads, 8, width, dtype=F32),
        ),
        (groups, 2),
        [block, block, lse, group_spec(own), group_spec(oth), slab, whole(kseg), qs],
        (
            block,
            group_spec(own),
            group_spec(own),
            pl.BlockSpec((2, 8, width), lambda g, s, *_: (g, 0, 0)),
        ),
        [
            pltpu.VMEM((4, rows, PAIR), BF16),
            pltpu.VMEM((4, rows, PAIR), F32),
            pltpu.VMEM((2, 128, width), F32),
        ],
        prefetch=1,
        micros=32,
    )(ids, q, ga, lses, own, oth, slabs, kseg, qseg)


def cross_back_kernel(
    q_ref, ga_ref, lse_ref, own_ref, oth_ref, kseg_ref, qseg_ref, dq_ref, down_ref, doth_ref, acc_ref
):
    kv = jnp.concatenate([own_ref[...], oth_ref[...]], axis=0)
    grad_kv = back_block(
        kv.shape[0], q_ref.shape[0], kv, q_ref, ga_ref, lse_ref, kseg_ref[...], qseg_ref[0],
        None, None, dq_ref,
    )
    half = own_ref.shape[0]

    @pl.when(pl.program_id(1) == 0)
    def _():
        acc_ref[...] = grad_kv

    @pl.when(pl.program_id(1) == 1)
    def _():
        total = acc_ref[...] + grad_kv
        down_ref[...] = total[:half]
        doth_ref[...] = total[half:].astype(BF16)


def cross_attention_back(q, ga, lses, own, oth, kseg, qseg):
    rows, groups = q.shape[0] // 2, q.shape[1] // PAIR
    block, lse, qs = attention_specs(rows, groups)
    return call(
        cross_back_kernel,
        (shape(*q.shape), shape(*own.shape, dtype=F32), shape(*own.shape)),
        (groups, 2),
        [block, block, lse, group_spec(own), group_spec(oth), whole(kseg), qs],
        (block, group_spec(own), group_spec(own)),
        [pltpu.VMEM((2 * own.shape[0], PAIR), F32)],
        micros=21,
    )(q, ga, lses, own, oth, kseg, qseg)


def weight_grads(half, parts, own_ref, oth_ref):
    for ref, first in ((own_ref, 0), (oth_ref, half)):
        for left, right, at in parts:
            grad = dot_nn(left[first : first + half, :], right).astype(BF16)
            cols, _, blk, _ = ref.shape
            ref[:, 0, :, at : at + right.shape[1]] = grad.reshape(cols, blk, right.shape[1])


def cross_post_kernel(
    shards, dq_ref, dko_ref, dkr_ref, n_ref, mem_ref, r_ref, att_ref, s_ref, cot_ref, gain_ref,
    own_ref, oth_ref, wo_own, wo_oth, att_one_ref,
    gown_ref, goth_ref, oown_ref, ooth_ref, new_ref, round_ref, gg_ref, dmem_ref, ga_ref,
    dn_ref, dmo_ref, nt_ref, mt_ref, rt_ref,
):
    step = pl.program_id(0)
    half = n_ref.shape[1] // 2
    qcols = dq_ref.shape[1]

    @pl.when(step == 0)
    def _():
        dn_ref[...] = jnp.zeros_like(dn_ref)
        dmo_ref[...] = jnp.zeros_like(dmo_ref)
        nt_ref[...] = n_ref[...].T
        mt_ref[...] = mem_ref[...].T
        rt_ref[...] = r_ref[...].T

    @pl.when(step < shards)
    def _():
        dq = dq_ref[...]
        dkv = (dko_ref[...] + dkr_ref[...].astype(F32)).astype(BF16)
        own, oth = rows_of(own_ref), rows_of(oth_ref)
        parts = ((nt_ref, dq, 0), (mt_ref, dkv, qcols), (rt_ref, att_ref[...], 2 * qcols))
        weight_grads(half, parts, gown_ref, goth_ref)
        for w, span in ((own, slice(0, half)), (oth, slice(half, 2 * half))):
            dn_ref[:, span] += dot_nt(dq, w[:, :qcols])
            dmo_ref[:, span] += dot_nt(dkv, w[:, qcols : 2 * qcols])

    @pl.when(step == shards - 1)
    def _():
        dmem_ref[...] = dmo_ref[...].astype(BF16)
        dv, gg = norm_back(s_ref[...], gain_ref[...], dn_ref[...])
        gg_ref[...] = gg
        new = cot_ref[...] + dv
        new_ref[...] = new
        round_ref[...] = new.astype(BF16)
        rt_ref[...] = new.astype(BF16).T

    @pl.when(step >= shards)
    def _():
        r = round_ref[...]
        weight_grads(half, ((rt_ref, att_one_ref[...], 0),), oown_ref, ooth_ref)
        out = dot_nn(r[:, :half], rows_of(wo_own)) + dot_nn(r[:, half:], rows_of(wo_oth))
        ga_ref[...] = out.astype(BF16)


def cross_post(
    dq, dko, dkr, n, mem, r, att, s, cot, gain, own, oth, next_own, next_oth, next_att, qcols
):
    rows, width = n.shape
    cols, shards, blk, packed = own.shape
    first = lambda i: jnp.minimum(i, shards - 1)
    second = lambda i: jnp.maximum(i - shards, 0)
    spec = weight_spec(own, packed, lambda i: (0, first(i), 0, 0))
    wo = weight_spec(own, qcols, lambda i: (0, second(i), 0, 2))
    enc_rows = mem.shape[0]
    by_shard = pl.BlockSpec((rows, qcols), lambda i: (0, first(i)))
    enc_by_shard = pl.BlockSpec((enc_rows, qcols), lambda i: (0, first(i)))
    full = fixed(rows, width)
    return call(
        functools.partial(cross_post_kernel, shards),
        (
            shape(*own.shape),
            shape(*own.shape),
            shape(cols, shards, blk, qcols),
            shape(cols, shards, blk, qcols),
            shape(rows, width, dtype=F32),
            shape(rows, width),
            shape(1, width, dtype=F32),
            shape(enc_rows, width),
            shape(rows, shards * qcols),
        ),
        (2 * shards,),
        [by_shard, enc_by_shard, enc_by_shard, full, whole(mem), full, by_shard, full, full]
        + [whole(gain), spec, spec, wo, wo, pl.BlockSpec((rows, qcols), lambda i: (0, second(i)))],
        (
            spec,
            spec,
            weight_spec(own, qcols, lambda i: (0, second(i), 0, 0)),
            weight_spec(own, qcols, lambda i: (0, second(i), 0, 0)),
            full,
            full,
            fixed(1, width),
            fixed(enc_rows, width),
            pl.BlockSpec((rows, qcols), lambda i: (0, second(i))),
        ),
        [
            pltpu.VMEM((rows, width), F32),
            pltpu.VMEM((enc_rows, width), F32),
            pltpu.VMEM((width, rows), BF16),
            pltpu.VMEM((width, enc_rows), BF16),
            pltpu.VMEM((width, rows), BF16),
        ],
        micros=18,
    )(dq, dko, dkr, n, mem, r, att, s, cot, gain, own, oth, next_own, next_oth, next_att)


def self_post_kernel(
    dq_ref, dko_ref, dkr_ref, n_ref, x_ref, cot_ref, gain_ref, own_ref, oth_ref,
    gown_ref, goth_ref, out_ref, gg_ref, dn_ref, nt_ref,
):
    step = pl.program_id(0)
    half = n_ref.shape[1] // 2
    qcols = dq_ref.shape[1]

    @pl.when(step == 0)
    def _():
        dn_ref[...] = jnp.zeros_like(dn_ref)
        nt_ref[...] = n_ref[...].T

    dkv = (dko_ref[...] + dkr_ref[...].astype(F32)).astype(BF16)
    grad = jnp.concatenate([dq_ref[...], dkv], axis=1)
    own, oth = rows_of(own_ref), rows_of(oth_ref)
    weight_grads(half, ((nt_ref, grad, 0),), gown_ref, goth_ref)
    dn_ref[:, :half] += dot_nt(grad, own)
    dn_ref[:, half:] += dot_nt(grad, oth)

    @pl.when(step == pl.num_programs(0) - 1)
    def _():
        dv, gg = norm_back(x_ref[...].astype(F32), gain_ref[...], dn_ref[...])
        gg_ref[...] = gg
        out_ref[...] = (cot_ref[...] + dv).astype(BF16)


def self_post(dq, dko, dkr, n, x, cot, gain, own, oth, qcols):
    rows, width = n.shape
    cols, shards, blk, packed = own.shape
    spec = weight_spec(own, 2 * qcols, lambda i: (0, i, 0, 0))
    by_shard = pl.BlockSpec((rows, qcols), lambda i: (0, i))
    full = fixed(rows, width)
    return call(
        self_post_kernel,
        (
            shape(cols, shards, blk, 2 * qcols),
            shape(cols, shards, blk, 2 * qcols),
            shape(rows, width),
            shape(1, width, dtype=F32),
        ),
        (shards,),
        [by_shard, by_shard, by_shard, full, full, full, whole(gain), spec, spec],
        (spec, spec, full, fixed(1, width)),
        [
            pltpu.VMEM((rows, width), F32),
            pltpu.VMEM((width, rows), BF16),
        ],
        micros=14,
    )(dq, dko, dkr, n, x, cot, gain, own, oth)


def pack_layer_kernel(me_ref, q_ref, k_ref, v_ref, o_ref, out_ref):
    qcols, kcols = q_ref.shape[1], k_ref.shape[1]
    out_ref[:, :qcols] = q_ref[...]
    for at in range(0, kcols, HEAD_DIM):
        first = qcols + 2 * at
        out_ref[:, first : first + HEAD_DIM] = k_ref[:, at : at + HEAD_DIM]
        out_ref[:, first + HEAD_DIM : first + 2 * HEAD_DIM] = v_ref[:, at : at + HEAD_DIM]
    out = o_ref[...]
    out_ref[:, 2 * qcols :] = out if out.shape[0] == out_ref.shape[0] else out.T


def pack_ffn_kernel(me_ref, g_ref, u_ref, d_ref, out_ref):
    rows, packed = out_ref.shape
    parts = [r[...] if r.shape[0] == rows else r[...].T for r in (g_ref, u_ref, d_ref)]
    spare = packed - 3 * parts[0].shape[1]
    if spare:
        parts.append(jnp.zeros((rows, spare), BF16))
    out_ref[...] = jnp.concatenate(parts, axis=1)


def packed_rows(kernel, me, blk, by_row, by_col, packed):
    if blk % 128:
        by_row = by_row + [w.T for w in by_col]
        by_col = []
    specs = [pl.BlockSpec((blk, w.shape[1]), lambda i, at: (at[0], 0)) for w in by_row]
    specs += [pl.BlockSpec((w.shape[0], blk), lambda i, at: (0, at[0])) for w in by_col]
    return call(
        kernel, shape(blk, packed), (1,), specs, fixed(blk, packed), prefetch=1, micros=2
    )(me, *by_row, *by_col)


def unpack_layer_kernel(pos_ref, x_ref, q_ref, k_ref, v_ref, *o_refs):
    x = x_ref[0].astype(F32)
    qcols, kcols = q_ref.shape[1], k_ref.shape[1]
    q_ref[...] = x[:, :qcols]
    for at in range(0, kcols, HEAD_DIM):
        first = qcols + 2 * at
        k_ref[:, at : at + HEAD_DIM] = x[:, first : first + HEAD_DIM]
        v_ref[:, at : at + HEAD_DIM] = x[:, first + HEAD_DIM : first + 2 * HEAD_DIM]
    for i, o_ref in enumerate(o_refs):
        out = x[:, (2 + i) * qcols : (3 + i) * qcols]
        o_ref[...] = out if o_ref.shape == out.shape else out.T


def unpack_ffn_kernel(ff, pos_ref, x_ref, g_ref, u_ref, d_ref):
    x = x_ref[0].astype(F32)
    for i, ref in enumerate((g_ref, u_ref, d_ref)):
        out = x[:, i * ff : (i + 1) * ff]
        ref[...] = out if ref.shape == out.shape else out.T


def unpacked(kernel, position, array, by_row, by_col):
    count, blk, packed = array.shape
    turned = blk % 128 == 0
    outs = [shape(count * blk, c, dtype=F32) for c in by_row]
    specs = [pl.BlockSpec((blk, c), lambda p, pos: (p, 0)) for c in by_row]
    for c in by_col:
        if turned:
            outs.append(shape(c, count * blk, dtype=F32))
            specs.append(pl.BlockSpec((c, blk), lambda p, pos: (0, p)))
        else:
            outs.append(shape(count * blk, c, dtype=F32))
            specs.append(pl.BlockSpec((blk, c), lambda p, pos: (p, 0)))
    results = call(
        kernel,
        tuple(outs),
        (count,),
        [pl.BlockSpec((1, blk, packed), lambda p, pos: (pos[p], 0, 0))],
        tuple(specs),
        prefetch=1,
        micros=5,
    )(position, array)
    rows = len(by_row)
    return results[:rows], [r if turned else r.T for r in results[rows:]]


def unpack_layer(position, array, qcols, turned):
    rows, outs = unpacked(
        unpack_layer_kernel, position, array, (qcols, qcols // 2, qcols // 2), (qcols,) * turned
    )
    return (*rows, *outs)


def unpack_ffn(position, array, ff):
    _, turned = unpacked(functools.partial(unpack_ffn_kernel, ff), position, array, (), (ff, ff, ff))
    return turned[0].T, turned[1].T, turned[2]


def make_per_device(batch, shards):
    cols = batch // 2
    bits = cols.bit_length() - 1
    assert batch == 2 * (1 << bits) and shards == 4

    def swap(array, mask):
        return lax.ppermute(array, "batch", [(b, b ^ mask) for b in range(batch)])

    def in_order(position):
        return ((position % cols) << 1) | (position // cols)

    def place_of(difference):
        return (difference >> 1) | ((difference & 1) * cols)

    def to_relative(array):
        me = lax.axis_index("batch")
        blk = array.shape[-1] // batch
        parts = [
            lax.dynamic_slice_in_dim(array, (me ^ in_order(p)) * blk, blk, array.ndim - 1)
            for p in range(batch)
        ]
        return jnp.concatenate(parts, axis=-1)

    def to_absolute(array):
        me = lax.axis_index("batch")
        blk = array.shape[-1] // batch
        parts = [
            lax.dynamic_slice_in_dim(array, place_of(me ^ p) * blk, blk, array.ndim - 1)
            for p in range(batch)
        ]
        return jnp.concatenate(parts, axis=-1)

    def core_of(z):
        return 0 if z in (0, 3) else 1

    routes = []
    for second in (0, 1):
        route = []
        for b in range(batch):
            for z in range(shards):
                micro = (z // 2) ^ second
                target = ((b - b % 2) + core_of(z)) * shards + 2 * micro + b % 2
                route.append((b * shards + z, target))
        routes.append(route)
    both = ("batch", "group")

    def pin(*values):
        return lax.optimization_barrier(values)

    def after(value, *others):
        return lax.optimization_barrier((value,) + others)[0]

    def to_sequence(array):
        first = lax.axis_index("group") // 2
        received = []
        for second, route in enumerate(routes):
            part = lax.dynamic_index_in_dim(array, first ^ second, 0, keepdims=False)
            received.append(lax.ppermute(part, both, route))
        return jnp.concatenate(received, axis=0)

    def send_back(array):
        array = to_absolute(array)
        rows = array.shape[0] // 2
        return [
            lax.ppermute(array[i * rows : (i + 1) * rows], both, [(t, s) for s, t in route])
            for i, route in enumerate(routes)
        ]

    def as_micros(back):
        first = lax.axis_index("group") // 2
        return jnp.where(first == 0, jnp.stack(back), jnp.stack(back[::-1]))

    def swap_z(array, mask):
        return lax.ppermute(array, "group", [(z, z ^ mask) for z in range(shards)])

    def shards_of(own):
        far = swap_z(own, 2)
        return [own, swap_z(own, 1), far, swap_z(far, 1)]

    class Spread:
        def __init__(self, pieces, order):
            self.piece = (len(pieces),) + pieces[0].shape
            self.order, self.own = list(order), None
            self.array = jnp.stack(pieces).reshape((1,) * bits + self.piece)

        def start(self):
            self.pending = swap(self.array, 2 << self.order[0])

        def land(self):
            axis = bits - 1 - self.order.pop(0)
            self.array = jnp.concatenate([self.array, self.pending], axis=axis)

        def advance(self):
            self.land()
            if self.order:
                self.start()
            else:
                self.own = self.array.reshape((cols,) + self.piece)
                self.oth = swap(self.own, 1)

        def finish(self):
            while self.own is None:
                self.advance()
            return self.own, self.oth

    def total_of(terms):
        total = terms[0].astype(F32)
        for term in terms[1:]:
            total = total + term.astype(F32)
        return total

    def halves(terms, axis):
        first = [lax.slice_in_dim(t, 0, 1, axis=axis) for t in terms]
        second = [lax.slice_in_dim(t, 1, 2, axis=axis) for t in terms]
        return first, second

    def joined(terms):
        return terms[0] if len(terms) == 1 else jnp.concatenate(terms, axis=-1)

    def collecting(parts, order, z_masks):
        piece = parts[0][0].shape[1:-1] + (sum(own.shape[-1] for own, _ in parts),)
        pending = yield [swap(oth, 1) for _, oth in parts]
        cube = (2,) * bits
        terms = [
            joined([own for own, _ in parts]).reshape(cube + piece),
            joined(pending).reshape(cube + piece),
        ]
        for bit in order:
            terms, send = halves(terms, bits - 1 - bit)
            terms = terms + (yield [swap(total_of(send).astype(BF16), 2 << bit)])
        terms = [t.reshape(piece) for t in terms]
        for mask in z_masks:
            count = terms[0].shape[0] // 2
            keep, send = halves([t.reshape((count, 2) + t.shape[1:]) for t in terms], 1)
            received = yield [swap_z(total_of(send).astype(BF16), mask)]
            terms = [t.reshape((count,) + piece[1:]) for t in keep + received]
        return terms

    def sharing(terms):
        piece = terms[0].shape[1:]
        array = total_of(terms).astype(BF16).reshape((1,) * bits + piece)
        for bit in range(bits):
            (pending,) = yield [swap(array, 2 << bit)]
            array = jnp.concatenate([array, pending], axis=bits - 1 - bit)
        array = array.reshape((cols,) + piece)
        (pending,) = yield [swap(array, 1)]
        return jnp.concatenate([array, pending], axis=0)

    def whole_chain(parts, order):
        terms = yield from collecting(parts, order, (1, 2))
        return (yield from sharing(terms))

    def ffn_chain(near, far):
        received = yield [swap_z(total_of(far).astype(BF16), 2)]
        return (yield from sharing(near + received))

    def summing(small):
        for mask in (1, 2):
            (other,) = yield [swap_z(small, mask)]
            small = small + other
        for bit in range(bits + 1):
            (other,) = yield [swap(small, 1 << bit)]
            small = small + other
        return small

    class Chain:
        def __init__(self, steps):
            self.steps, self.result = steps, None
            self.pending = next(steps)

        def advance(self):
            try:
                self.pending = self.steps.send(self.pending)
            except StopIteration as stop:
                self.pending, self.result = [], stop.value

    def land(chains, *extra):
        chains = [c for c in chains if c.pending]
        flat = [p for c in chains for p in c.pending]
        flat = list(lax.optimization_barrier(tuple(flat) + extra))
        for c in chains:
            c.pending = [flat.pop(0) for _ in c.pending]
        for c in chains:
            c.advance()
        return flat

    def per_device(
        tokens, memory, dec_segments, enc_segments, buckets,
        self_gain, self_query, self_key, self_value, self_output, rel_bias,
        cross_gain, cross_query, cross_key, cross_value, cross_output,
        ffn_gain, ffn_gate, ffn_up, ffn_down, out_grad,
    ):
        me, z = lax.axis_index("batch"), lax.axis_index("group")
        core, micro, owner = me % 2, z // 2, z % 2
        width = tokens.shape[2]
        blk = width // batch
        qcols = self_query.shape[1]
        chunk, enc_chunk = tokens.shape[1], memory.shape[1]
        up = tuple(range(bits))
        down = up[::-1]

        ff = ffn_gate.shape[1]
        at = me.reshape(1).astype(jnp.int32)
        self_piece = packed_rows(
            pack_layer_kernel, at, blk, [self_query, self_key, self_value], [self_output], 3 * qcols
        )
        cross_piece = packed_rows(
            pack_layer_kernel, at, blk, [cross_query, cross_key, cross_value], [cross_output], 3 * qcols
        )
        ffn_piece = packed_rows(
            pack_ffn_kernel, at, blk, [], [ffn_gate.T, ffn_up.T, ffn_down], 3 * ff + -3 * ff % 128
        )
        self_far = swap_z(self_piece, 2)
        self_near = swap_z(self_piece, 1)
        cross_far = swap_z(cross_piece, 2)
        cross_near = swap_z(cross_piece, 1)
        self_last = swap_z(self_far, 1)
        self_w = Spread([self_piece, self_near, self_far, self_last], up)
        self_w.start()
        cross_last = swap_z(cross_far, 1)
        cross_w = Spread([cross_piece, cross_near, cross_far, cross_last], down)
        cross_w.start()
        stream = to_sequence(after(tokens, self_far, cross_far))
        first = (self_w.pending, cross_w.pending)
        self_w.advance()
        cross_w.advance()
        ffn_piece = after(ffn_piece, *first)
        ffn_near = swap_z(ffn_piece, 1)
        ffn_far = swap_z(ffn_piece, 2)
        ffn_last = swap_z(ffn_far, 1)
        encoder = to_sequence(after(memory, ffn_far))
        near_w = Spread([ffn_piece, ffn_near], up)
        far_w = Spread([ffn_far, ffn_last], down)
        near_w.array = after(near_w.array, self_w.pending, cross_w.pending)
        near_w.start()
        far_w.array = after(far_w.array, self_w.pending, cross_w.pending)
        far_w.start()
        self_own, self_oth = self_w.finish()
        cross_own, cross_oth = cross_w.finish()
        cot = to_sequence(after(out_grad, encoder))
        stream, encoder = to_relative(stream), to_relative(encoder)

        segments = jnp.concatenate([dec_segments, enc_segments], axis=1)
        length = dec_segments.shape[1]
        chosen = jnp.where(owner == core, segments, swap(segments, 1))
        chosen = lax.dynamic_index_in_dim(chosen, micro, 0, keepdims=False)
        dec_seg, enc_seg = chosen[:length], chosen[length:]

        def ids_of(which):
            first = jnp.where(micro == 0, which, 3 - which)
            return [first, 3 - first]

        ids = jnp.stack(ids_of(core) + ids_of(1 - core)).astype(jnp.int32)

        def pieces_of(seg, size, count):
            return [lax.dynamic_slice_in_dim(seg, ids[i] * size, size, 0) for i in range(count)]

        qseg = jnp.stack(pieces_of(dec_seg, chunk, 2)).reshape(2, 1, chunk)
        kseg = dec_seg.reshape(length, 1)
        enc_kseg = jnp.concatenate(pieces_of(enc_seg, enc_chunk, 4)).reshape(-1, 1)

        all_bias = jnp.concatenate(shards_of(rel_bias), axis=1)
        bucket_count = rel_bias.shape[0]
        onehot = (buckets[:, None] == jnp.arange(bucket_count)[None, :]).astype(F32)
        distance_bias = lax.dot_general(
            all_bias, onehot, (((0,), (1,)), ((), ())), precision=HIGHEST, preferred_element_type=F32
        )
        slabs = bias_slabs(distance_bias)
        gain_one, gain_two, gain_three = (
            to_relative(gain.reshape(1, width)) for gain in (self_gain, cross_gain, ffn_gain)
        )

        n_one, q_one, kv_one = project_qkv(stream, gain_one, self_own, self_oth, qcols)
        kv_one_oth = swap(kv_one, 1)
        kv_two = project_kv(encoder, cross_own, cross_oth, qcols)
        kv_two_oth = swap(kv_two, 1)
        near_w.pending, far_w.pending, q_one = pin(near_w.pending, far_w.pending, q_one)
        near_w.advance()
        far_w.advance()
        att_one, lse_one = self_attention(ids, q_one, kv_one, kv_one_oth, slabs, kseg, qseg)
        stream_one, n_two, q_two = output_and_query(
            stream, att_one, gain_two, self_own, self_oth, cross_own, cross_oth, qcols
        )
        att_two, lse_two = cross_attention(q_two, kv_two, kv_two_oth, enc_kseg, qseg)
        near_w.pending, far_w.pending, att_two = pin(near_w.pending, far_w.pending, att_two)
        near_w.finish()
        far_w.finish()
        stream_two, n_three = output_and_norm(stream_one, att_two, gain_three, cross_own, cross_oth, qcols)

        cot = to_relative(cot)
        ya, da, grad_own, grad_oth = feed_forward(n_three, cot, near_w.own, near_w.oth, ff)
        near_g = Chain(collecting([(grad_own, grad_oth)], down, (1,)))
        n_three, ya = pin(n_three, ya)
        yb, db, grad_own, grad_oth = feed_forward(n_three, cot, far_w.own, far_w.oth, ff)
        far_g = Chain(collecting([(grad_own, grad_oth)], up, (1,)))
        (db,) = land([near_g], db)
        block_out, cot_two, round_two, grad_gain_three, ga_two = after_ffn(
            stream_two, ya, yb, da, db, cot, gain_three, cross_own, cross_oth, qcols
        )
        (ga_two,) = land([far_g], ga_two)
        block_back = send_back(block_out)

        dq_two, dkv_two, dkv_two_send = cross_attention_back(
            q_two, ga_two, lse_two, kv_two, kv_two_oth, enc_kseg, qseg
        )
        (dq_two,) = land([near_g], dq_two)
        (grad_own, grad_oth, out_own, out_oth, cot_one, round_one, grad_gain_two, memory_grad, ga_one) = cross_post(
            dq_two, dkv_two, swap(dkv_two_send, 1), n_two, encoder, round_two, att_two, stream_one,
            cot_two, gain_two, cross_own, cross_oth, self_own, self_oth, att_one, qcols,
        )
        cross_g = Chain(whole_chain([(grad_own, grad_oth), (out_own, out_oth)], up))
        (ga_one,) = land([far_g, cross_g], ga_one)
        dq_one, dkv_one, dkv_one_send, folded = self_attention_back(
            ids, q_one, ga_one, lse_one, kv_one, kv_one_oth, slabs, kseg, qseg
        )
        (dq_one,) = land([near_g, far_g], dq_one)
        grad_own, grad_oth, tokens_grad, grad_gain_one = self_post(
            dq_one, dkv_one, swap(dkv_one_send, 1), n_one, stream, cot_one,
            gain_one, self_own, self_oth, qcols,
        )
        self_g = Chain(whole_chain([(grad_own, grad_oth)], down))
        tokens_back = send_back(tokens_grad)

        padded = jnp.pad(folded, ((0, 0), (0, 0), (0, 8)))
        distance_grad = sum(padded[:, i, 128 + i : 128 + i + length] for i in range(8))
        bucket_grad = lax.dot_general(
            onehot, distance_grad, (((0,), (1,)), ((), ())), precision=HIGHEST, preferred_element_type=F32
        )
        small = [to_absolute(g).reshape(width) for g in (grad_gain_one, grad_gain_two, grad_gain_three)]
        bucket_grad = bucket_grad.reshape(bucket_count, shards, -1)
        bucket_grad = [
            lax.dynamic_index_in_dim(bucket_grad, z ^ p, 1, keepdims=False) for p in range(shards)
        ]
        small = jnp.concatenate(small + [g.reshape(-1) for g in bucket_grad])
        small_g = Chain(summing(small))
        land([self_g, near_g, far_g, cross_g])
        while near_g.pending or far_g.pending:
            land([self_g, near_g, far_g, cross_g])
        ffn_g = Chain(ffn_chain(near_g.result, far_g.result))
        memory_back = send_back(after(memory_grad, *self_g.pending))
        chains = [self_g, cross_g, ffn_g, small_g]
        while any(c.pending for c in chains):
            land(chains)
        position = place_of(me ^ jnp.arange(batch)).astype(jnp.int32)
        ffn_final = unpack_ffn(position, ffn_g.result, ff)
        *cross_final, self_out_grad = unpack_layer(position, cross_g.result, qcols, 2)
        self_final = (*unpack_layer(position, self_g.result, qcols, 0), self_out_grad)
        late = self_g.result
        block_out = as_micros([after(part, late) for part in block_back])
        memory_grad = as_micros([after(part, late) for part in memory_back]).astype(F32)
        tokens_grad = as_micros([after(part, late) for part in tokens_back]).astype(F32)

        small = small_g.result
        gains = [small[i * width : (i + 1) * width] for i in range(3)]
        bucket_grad = small[3 * width :].reshape(shards, bucket_count, -1)
        bucket_grad = lax.dynamic_index_in_dim(bucket_grad, z, 0, keepdims=False)

        return (
            block_out,
            tokens_grad,
            memory_grad,
            gains[0],
            *self_final,
            bucket_grad,
            gains[1],
            *cross_final,
            gains[2],
            *ffn_final,
        )

    return per_device


def solution(mesh):
    rows, group_cols, group_rows = P(None, ("batch", "group"), None), P(None, "group"), P("group", None)
    layer = (group_cols, group_cols, group_cols, group_rows)
    return jax.shard_map(
        make_per_device(mesh.shape["batch"], mesh.shape["group"]),
        mesh=mesh,
        in_specs=(
            rows, rows, P(None, "batch"), P(None, "batch"), P(),
            P(), *layer, group_cols,
            P(), *layer,
            P(), group_cols, group_cols, group_rows, rows,
        ),
        out_specs=(
            rows, rows, rows,
            P(), *layer, group_cols,
            P(), *layer,
            P(), group_cols, group_cols, group_rows,
        ),
        check_vma=False,
    )
```

```python
import functools

import jax
import jax.numpy as jnp
from jax import lax
from jax.experimental import pallas as pl
from jax.experimental.pallas import tpu as pltpu
from jax.sharding import PartitionSpec as P

HEAD_DIM = 64
PAIR = 2 * HEAD_DIM
EPSILON = 1e-06
MASKED = -1e30
HIGHEST = lax.Precision.HIGHEST
BF16 = jnp.bfloat16
F32 = jnp.float32
FLOPS_PER_MICRO = 1_000_000_000
BYTES_PER_MICRO = 3_000_000


def dot_nn(left, right):
    return lax.dot_general(left, right, (((1,), (0,)), ((), ())), preferred_element_type=F32)


def dot_nt(left, right):
    return lax.dot_general(left, right, (((1,), (1,)), ((), ())), preferred_element_type=F32)


def dot_tn(left, right):
    return lax.dot_general(left, right, (((0,), (0,)), ((), ())), preferred_element_type=F32)


def call(kernel, outs, grid, in_specs, out_specs, scratch=(), prefetch=0, micros=5):
    return pl.pallas_call(
        kernel,
        out_shape=outs,
        cost_estimate=pl.CostEstimate(
            flops=micros * FLOPS_PER_MICRO, transcendentals=0, bytes_accessed=micros * BYTES_PER_MICRO
        ),
        grid_spec=pltpu.PrefetchScalarGridSpec(
            num_scalar_prefetch=prefetch,
            grid=grid,
            in_specs=in_specs,
            out_specs=out_specs,
            scratch_shapes=list(scratch),
        ),
        compiler_params=pltpu.CompilerParams(
            dimension_semantics=("arbitrary",) * len(grid),
        ),
    )


def shape(*dims, dtype=BF16):
    return jax.ShapeDtypeStruct(dims, dtype)


def whole(array):
    dims = array.shape
    return pl.BlockSpec(dims, lambda *ids: (0,) * len(dims))


def fixed(*dims):
    return pl.BlockSpec(dims, lambda *ids: (0,) * len(dims))


def rows_of(ref):
    block = ref[...]
    return block.reshape(block.shape[0] * block.shape[2], block.shape[3])


def store_rows(ref, value):
    ref[...] = value.reshape(ref.shape).astype(ref.dtype)


def weight_spec(weights, columns, index):
    cols, _, blk, _ = weights.shape
    return pl.BlockSpec((cols, 1, blk, columns), index)


def norm(values, gain):
    return values * lax.rsqrt(jnp.mean(values * values, axis=-1, keepdims=True) + EPSILON) * gain


def norm_back(values, gain, grad):
    scale = lax.rsqrt(jnp.mean(values * values, axis=-1, keepdims=True) + EPSILON)
    scaled = grad * gain
    inner = jnp.mean(scaled * values, axis=-1, keepdims=True)
    grad_values = scale * scaled - values * (scale * scale * scale * inner)
    grad_gain = jnp.sum(grad * values * scale, axis=0, keepdims=True)
    return grad_values, grad_gain


def qkv_kernel(x_ref, gain_ref, own_ref, oth_ref, n_ref, q_ref, kv_ref):
    half = x_ref.shape[1] // 2
    qcols = q_ref.shape[1]

    @pl.when(pl.program_id(0) == 0)
    def _():
        n_ref[...] = norm(x_ref[...].astype(F32), gain_ref[...]).astype(BF16)

    out = dot_nn(n_ref[:, :half], rows_of(own_ref)) + dot_nn(n_ref[:, half:], rows_of(oth_ref))
    q_ref[...] = out[:, :qcols].astype(BF16)
    kv_ref[...] = out[:, qcols:].astype(BF16)


def project_qkv(x, gain, own, oth, qcols):
    rows, width = x.shape
    shards = own.shape[1]
    spec = weight_spec(own, 2 * qcols, lambda z: (0, z, 0, 0))
    out = pl.BlockSpec((rows, qcols), lambda z: (0, z))
    return call(
        qkv_kernel,
        (shape(rows, width), shape(rows, shards * qcols), shape(rows, shards * qcols)),
        (shards,),
        [whole(x), whole(gain), spec, spec],
        (fixed(rows, width), out, out),
        micros=7,
    )(x, gain, own, oth)


def kv_kernel(x_ref, own_ref, oth_ref, kv_ref):
    half = x_ref.shape[1] // 2
    out = dot_nn(x_ref[:, :half], rows_of(own_ref)) + dot_nn(x_ref[:, half:], rows_of(oth_ref))
    kv_ref[...] = out.astype(BF16)


def project_kv(x, own, oth, qcols):
    rows, width = x.shape
    shards = own.shape[1]
    spec = weight_spec(own, qcols, lambda z: (0, z, 0, 1))
    return call(
        kv_kernel,
        shape(rows, shards * qcols),
        (shards,),
        [whole(x), spec, spec],
        pl.BlockSpec((rows, qcols), lambda z: (0, z)),
        micros=4,
    )(x, own, oth)


def mid_kernel(shards, x_ref, att_ref, gain_ref, wo_own, wo_oth, wq_own, wq_oth, s_ref, n_ref, q_ref):
    step = pl.program_id(0)
    half = x_ref.shape[1] // 2

    @pl.when(step == 0)
    def _():
        s_ref[...] = x_ref[...].astype(F32)

    @pl.when(step < shards)
    def _():
        att = att_ref[...]
        s_ref[:, :half] += dot_nt(att, rows_of(wo_own))
        s_ref[:, half:] += dot_nt(att, rows_of(wo_oth))

    @pl.when(step == shards - 1)
    def _():
        n_ref[...] = norm(s_ref[...], gain_ref[...]).astype(BF16)

    @pl.when(step >= shards)
    def _():
        out = dot_nn(n_ref[:, :half], rows_of(wq_own)) + dot_nn(n_ref[:, half:], rows_of(wq_oth))
        q_ref[...] = out.astype(BF16)


def output_and_query(x, att, gain, own, oth, next_own, next_oth, qcols):
    rows, width = x.shape
    shards = own.shape[1]
    first = lambda i: jnp.minimum(i, shards - 1)
    second = lambda i: jnp.maximum(i - shards, 0)
    wo = weight_spec(own, qcols, lambda i: (0, first(i), 0, 2))
    wq = weight_spec(own, qcols, lambda i: (0, second(i), 0, 0))
    return call(
        functools.partial(mid_kernel, shards),
        (shape(rows, width, dtype=F32), shape(rows, width), shape(rows, shards * qcols)),
        (2 * shards,),
        [
            whole(x),
            pl.BlockSpec((rows, qcols), lambda i: (0, first(i))),
            whole(gain),
            wo,
            wo,
            wq,
            wq,
        ],
        (
            fixed(rows, width),
            fixed(rows, width),
            pl.BlockSpec((rows, qcols), lambda i: (0, second(i))),
        ),
        micros=10,
    )(x, att, gain, own, oth, next_own, next_oth)


def out_kernel(x_ref, att_ref, gain_ref, wo_own, wo_oth, s_ref, n_ref):
    half = x_ref.shape[1] // 2

    @pl.when(pl.program_id(0) == 0)
    def _():
        s_ref[...] = x_ref[...]

    att = att_ref[...]
    s_ref[:, :half] += dot_nt(att, rows_of(wo_own))
    s_ref[:, half:] += dot_nt(att, rows_of(wo_oth))

    @pl.when(pl.program_id(0) == pl.num_programs(0) - 1)
    def _():
        n_ref[...] = norm(s_ref[...], gain_ref[...]).astype(BF16)


def output_and_norm(x, att, gain, own, oth, qcols):
    rows, width = x.shape
    shards = own.shape[1]
    wo = weight_spec(own, qcols, lambda z: (0, z, 0, 2))
    return call(
        out_kernel,
        (shape(rows, width, dtype=F32), shape(rows, width)),
        (shards,),
        [whole(x), pl.BlockSpec((rows, qcols), lambda z: (0, z)), whole(gain), wo, wo],
        (fixed(rows, width), fixed(rows, width)),
        micros=7,
    )(x, att, gain, own, oth)


def ffn_kernel(ff, n_ref, r_ref, own_ref, oth_ref, y_ref, dn_ref, gown_ref, goth_ref, nt_ref, rt_ref):
    half = n_ref.shape[1] // 2

    @pl.when(pl.program_id(0) == 0)
    def _():
        y_ref[...] = jnp.zeros_like(y_ref)
        dn_ref[...] = jnp.zeros_like(dn_ref)
        nt_ref[...] = n_ref[...].T
        rt_ref[...] = r_ref[...].T

    own, oth = rows_of(own_ref), rows_of(oth_ref)
    up_own, up_oth = own[:, : 2 * ff], oth[:, : 2 * ff]
    down_own, down_oth = own[:, 2 * ff : 3 * ff], oth[:, 2 * ff : 3 * ff]
    both = dot_nn(n_ref[:, :half], up_own) + dot_nn(n_ref[:, half:], up_oth)
    gate, upval = both[:, :ff], both[:, ff:]
    grad_hidden = dot_nn(r_ref[:, :half], down_own) + dot_nn(r_ref[:, half:], down_oth)
    grad_hidden = grad_hidden.astype(BF16).astype(F32)
    root = 0.7978845608028654
    square = gate * gate
    tanh = jnp.tanh(root * gate * (1.0 + 0.044715 * square))
    cdf = 0.5 * (1.0 + tanh)
    gelu = gate * cdf
    slope = cdf + 0.5 * gate * (1.0 - tanh * tanh) * root * (1.0 + 3 * 0.044715 * square)
    hidden = (gelu * upval).astype(BF16)
    grad_gate = (grad_hidden * upval * slope).astype(BF16)
    grad_up = (grad_hidden * gelu).astype(BF16)
    grad_both = jnp.concatenate([grad_gate, grad_up], axis=1)
    y_ref[:, :half] += dot_nt(hidden, down_own)
    y_ref[:, half:] += dot_nt(hidden, down_oth)
    dn_ref[:, :half] += dot_nt(grad_both, up_own)
    dn_ref[:, half:] += dot_nt(grad_both, up_oth)
    cols, _, blk, packed = gown_ref.shape
    for ref, first in ((gown_ref, 0), (goth_ref, half)):
        grad = dot_nn(nt_ref[first : first + half, :], grad_both).astype(BF16)
        ref[:, 0, :, : 2 * ff] = grad.reshape(cols, blk, 2 * ff)
        grad = dot_nn(rt_ref[first : first + half, :], hidden).astype(BF16)
        ref[:, 0, :, 2 * ff : 3 * ff] = grad.reshape(cols, blk, ff)
        spare = packed - 3 * ff
        if spare:
            ref[:, 0, :, 3 * ff :] = jnp.zeros((cols, blk, spare), BF16)


def feed_forward(n, r, own, oth, ff):
    rows, width = n.shape
    cols, shards, blk, packed = own.shape
    spec = weight_spec(own, packed, lambda z: (0, z, 0, 0))
    return call(
        functools.partial(ffn_kernel, ff),
        (
            shape(rows, width, dtype=F32),
            shape(rows, width, dtype=F32),
            shape(*own.shape),
            shape(*own.shape),
        ),
        (shards,),
        [whole(n), whole(r), spec, spec],
        (fixed(rows, width), fixed(rows, width), spec, spec),
        [pltpu.VMEM((width, rows), BF16), pltpu.VMEM((width, rows), BF16)],
        micros=22,
    )(n, r, own, oth)


def after_ffn_kernel(
    s_ref, ya_ref, yb_ref, da_ref, db_ref, cot_ref, gain_ref, wo_own, wo_oth,
    out_ref, new_ref, round_ref, gg_ref, ga_ref,
):
    half = s_ref.shape[1] // 2

    @pl.when(pl.program_id(0) == 0)
    def _():
        s = s_ref[...]
        out_ref[...] = (s + ya_ref[...] + yb_ref[...]).astype(BF16)
        dv, gg = norm_back(s, gain_ref[...], da_ref[...] + db_ref[...])
        gg_ref[...] = gg
        new = cot_ref[...].astype(F32) + dv
        new_ref[...] = new
        round_ref[...] = new.astype(BF16)

    out = dot_nn(round_ref[:, :half], rows_of(wo_own)) + dot_nn(round_ref[:, half:], rows_of(wo_oth))
    ga_ref[...] = out.astype(BF16)


def after_ffn(s, ya, yb, da, db, cot, gain, own, oth, qcols):
    rows, width = s.shape
    shards = own.shape[1]
    wo = weight_spec(own, qcols, lambda z: (0, z, 0, 2))
    full = fixed(rows, width)
    return call(
        after_ffn_kernel,
        (
            shape(rows, width),
            shape(rows, width, dtype=F32),
            shape(rows, width),
            shape(1, width, dtype=F32),
            shape(rows, shards * qcols),
        ),
        (shards,),
        [full] * 6 + [whole(gain), wo, wo],
        (full, full, full, fixed(1, width), pl.BlockSpec((rows, qcols), lambda z: (0, z))),
        micros=10,
    )(s, ya, yb, da, db, cot, gain, own, oth)


def slab_kernel(base_ref, out_ref):
    base = base_ref[0]
    eight = jnp.concatenate([base] + [pltpu.roll(base, i, 1) for i in range(1, 8)], axis=0)
    for block in range(out_ref.shape[1] // 8):
        moved = eight if block == 0 else pltpu.roll(eight, 8 * block, 1)
        out_ref[0, 8 * block : 8 * block + 8, :] = moved


def bias_slabs(distance_bias):
    heads, length = distance_bias.shape
    width = length + 128
    base = jnp.pad(distance_bias, ((0, 0), (128, 0))).reshape(heads, 1, width)
    return call(
        slab_kernel,
        shape(heads, 128, width, dtype=F32),
        (heads,),
        [pl.BlockSpec((1, 1, width), lambda h: (h, 0, 0))],
        pl.BlockSpec((1, 128, width), lambda h: (h, 0, 0)),
        micros=11,
    )(base)


def stack_heads(block, low_lanes):
    lanes = lax.broadcasted_iota(jnp.int32, block.shape, 1) < HEAD_DIM
    wide = block.astype(F32)
    moved = pltpu.roll(wide, HEAD_DIM, 1)
    if low_lanes:
        parts = [jnp.where(lanes, wide, 0.0), jnp.where(lanes, moved, 0.0)]
    else:
        parts = [jnp.where(lanes, 0.0, moved), jnp.where(lanes, 0.0, wide)]
    return jnp.concatenate(parts, axis=0).astype(BF16)


def join_heads(transposed, rows, first):
    parts = [transposed[first : first + HEAD_DIM, :rows], transposed[first : first + HEAD_DIM, rows:]]
    return jnp.concatenate(parts, axis=0).T


def allowed_mask(kseg, qseg, causal):
    allowed = kseg == qseg
    if causal:
        keys, rows = allowed.shape
        key_at = lax.broadcasted_iota(jnp.int32, allowed.shape, 0) - (keys - rows)
        row_at = lax.broadcasted_iota(jnp.int32, allowed.shape, 1)
        allowed = allowed & (key_at <= row_at)
    return allowed


def head_bias(slab_ref, head, keys, rows):
    blocks = keys // 128
    last = keys - rows
    parts = []
    for block in range(blocks):
        at = last - 128 * block + 128
        parts.append(slab_ref[head, :, at : at + rows])
    return jnp.concatenate(parts, axis=0)


def attend_block(keys, rows, kv, q_ref, kseg, qseg, slab_ref, att_ref, lse_ref):
    stacked = stack_heads(q_ref[...], True)
    scores = dot_nt(kv, stacked)
    allowed = allowed_mask(kseg, qseg, slab_ref is not None)
    outs = []
    for head in range(2):
        part = scores[:, head * rows : (head + 1) * rows]
        if slab_ref is not None:
            part = part + head_bias(slab_ref, head, keys, rows)
        part = jnp.where(allowed, part, MASKED)
        top = jnp.max(part, axis=0, keepdims=True)
        grown = jnp.exp(part - top)
        total = jnp.sum(grown, axis=0, keepdims=True)
        probs = (grown * (1.0 / total)).astype(BF16)
        outs.append(dot_tn(kv, probs))
        lse_ref[0, :, head * rows : (head + 1) * rows] = top + jnp.log(total)
    att_ref[...] = join_heads(jnp.concatenate(outs, axis=1), rows, HEAD_DIM).astype(BF16)


def sort_keys(ids_ref, own_ref, oth_ref, sorted_ref):
    rows = sorted_ref.shape[1]
    for slot in range(4):
        source = own_ref if slot < 2 else oth_ref
        at = (slot % 2) * rows
        sorted_ref[ids_ref[slot]] = source[at : at + rows, :]


def self_kernel(ids_ref, q_ref, own_ref, oth_ref, slab_ref, kseg_ref, qseg_ref, att_ref, lse_ref, sorted_ref):
    rows = q_ref.shape[0]

    @pl.when(pl.program_id(1) == 0)
    def _():
        sort_keys(ids_ref, own_ref, oth_ref, sorted_ref)

    mine = ids_ref[pl.program_id(1)]
    for count in range(1, 5):

        @pl.when(mine == count - 1)
        def _(count=count):
            keys = count * rows
            kv = sorted_ref[0:count].reshape(keys, PAIR)
            attend_block(
                keys, rows, kv, q_ref, kseg_ref[0:keys, :], qseg_ref[0], slab_ref, att_ref, lse_ref
            )


def attention_specs(rows, groups):
    block = pl.BlockSpec((rows, PAIR), lambda g, s, *_: (s, g))
    lse = pl.BlockSpec((1, 1, 2 * rows), lambda g, s, *_: (2 * g + s, 0, 0))
    qseg = pl.BlockSpec((1, 1, rows), lambda g, s, *_: (s, 0, 0))
    return block, lse, qseg


def group_spec(array):
    return pl.BlockSpec((array.shape[0], PAIR), lambda g, s, *_: (0, g))


def self_attention(ids, q, own, oth, slabs, kseg, qseg):
    rows, groups = q.shape[0] // 2, q.shape[1] // PAIR
    block, lse, qs = attention_specs(rows, groups)
    slab = pl.BlockSpec((2,) + slabs.shape[1:], lambda g, s, *_: (g, 0, 0))
    return call(
        self_kernel,
        (shape(*q.shape), shape(2 * groups, 1, 2 * rows, dtype=F32)),
        (groups, 2),
        [block, group_spec(own), group_spec(oth), slab, whole(kseg), qs],
        (block, lse),
        [pltpu.VMEM((4, rows, PAIR), BF16)],
        prefetch=1,
        micros=20,
    )(ids, q, own, oth, slabs, kseg, qseg)


def cross_kernel(q_ref, own_ref, oth_ref, kseg_ref, qseg_ref, att_ref, lse_ref):
    kv = jnp.concatenate([own_ref[...], oth_ref[...]], axis=0)
    attend_block(
        kv.shape[0], q_ref.shape[0], kv, q_ref, kseg_ref[...], qseg_ref[0], None, att_ref, lse_ref
    )


def cross_attention(q, own, oth, kseg, qseg):
    rows, groups = q.shape[0] // 2, q.shape[1] // PAIR
    block, lse, qs = attention_specs(rows, groups)
    return call(
        cross_kernel,
        (shape(*q.shape), shape(2 * groups, 1, 2 * rows, dtype=F32)),
        (groups, 2),
        [block, group_spec(own), group_spec(oth), whole(kseg), qs],
        (block, lse),
        micros=16,
    )(q, own, oth, kseg, qseg)


def back_block(keys, rows, kv, q_ref, ga_ref, lse_ref, kseg, qseg, slab_ref, dslab_ref, dq_ref):
    stacked = stack_heads(q_ref[...], True)
    stacked_grad = stack_heads(ga_ref[...], False)
    scores = dot_nt(kv, stacked)
    grad_probs = dot_nt(kv, stacked_grad)
    allowed = allowed_mask(kseg, qseg, slab_ref is not None)
    queries, grad_kv = [], 0.0
    for head in range(2):
        span = slice(head * rows, (head + 1) * rows)
        part = scores[:, span]
        if slab_ref is not None:
            part = part + head_bias(slab_ref, head, keys, rows)
        part = jnp.where(allowed, part, MASKED)
        probs = jnp.exp(part - lse_ref[0, :, span])
        grad = grad_probs[:, span]
        inner = jnp.sum(probs * grad, axis=0, keepdims=True)
        grad_scores = probs * (grad - inner)
        low = grad_scores.astype(BF16)
        grad_kv = grad_kv + dot_nn(low, stacked[span, :])
        grad_kv = grad_kv + dot_nn(probs.astype(BF16), stacked_grad[span, :])
        queries.append(dot_tn(kv, low))
        if slab_ref is not None:
            last = keys - rows
            for block in range(keys // 128):
                at = last - 128 * block + 128
                dslab_ref[head, :, at : at + rows] += grad_scores[128 * block : 128 * block + 128, :]
    dq_ref[...] = join_heads(jnp.concatenate(queries, axis=1), rows, 0).astype(BF16)
    return grad_kv


def self_back_kernel(
    ids_ref, q_ref, ga_ref, lse_ref, own_ref, oth_ref, slab_ref, kseg_ref, qseg_ref,
    dq_ref, down_ref, doth_ref, fold_ref, sorted_ref, dsorted_ref, dslab_ref,
):
    rows = q_ref.shape[0]

    @pl.when(pl.program_id(1) == 0)
    def _():
        sort_keys(ids_ref, own_ref, oth_ref, sorted_ref)
        dsorted_ref[...] = jnp.zeros_like(dsorted_ref)
        dslab_ref[...] = jnp.zeros_like(dslab_ref)

    mine = ids_ref[pl.program_id(1)]
    for count in range(1, 5):

        @pl.when(mine == count - 1)
        def _(count=count):
            keys = count * rows
            kv = sorted_ref[0:count].reshape(keys, PAIR)
            grad_kv = back_block(
                keys, rows, kv, q_ref, ga_ref, lse_ref, kseg_ref[0:keys, :], qseg_ref[0],
                slab_ref, dslab_ref, dq_ref,
            )
            dsorted_ref[0:count] += grad_kv.reshape(count, rows, PAIR)

    @pl.when(pl.program_id(1) == 1)
    def _():
        for slot in range(4):
            at = (slot % 2) * rows
            value = dsorted_ref[ids_ref[slot]]
            target = down_ref if slot < 2 else doth_ref
            target[at : at + rows, :] = value.astype(target.dtype)
        width = dslab_ref.shape[2]
        for head in range(2):
            folded = dslab_ref[head]
            count = folded.shape[0] // 2
            while count >= 8:
                folded = folded[:count] + pltpu.roll(folded[count:], width - count, 1)
                count //= 2
            fold_ref[head] = folded


def self_attention_back(ids, q, ga, lses, own, oth, slabs, kseg, qseg):
    rows, groups = q.shape[0] // 2, q.shape[1] // PAIR
    block, lse, qs = attention_specs(rows, groups)
    heads, _, width = slabs.shape
    slab = pl.BlockSpec((2,) + slabs.shape[1:], lambda g, s, *_: (g, 0, 0))
    return call(
        self_back_kernel,
        (
            shape(*q.shape),
            shape(*own.shape, dtype=F32),
            shape(*own.shape),
            shape(heads, 8, width, dtype=F32),
        ),
        (groups, 2),
        [block, block, lse, group_spec(own), group_spec(oth), slab, whole(kseg), qs],
        (
            block,
            group_spec(own),
            group_spec(own),
            pl.BlockSpec((2, 8, width), lambda g, s, *_: (g, 0, 0)),
        ),
        [
            pltpu.VMEM((4, rows, PAIR), BF16),
            pltpu.VMEM((4, rows, PAIR), F32),
            pltpu.VMEM((2, 128, width), F32),
        ],
        prefetch=1,
        micros=32,
    )(ids, q, ga, lses, own, oth, slabs, kseg, qseg)


def cross_back_kernel(
    q_ref, ga_ref, lse_ref, own_ref, oth_ref, kseg_ref, qseg_ref, dq_ref, down_ref, doth_ref, acc_ref
):
    kv = jnp.concatenate([own_ref[...], oth_ref[...]], axis=0)
    grad_kv = back_block(
        kv.shape[0], q_ref.shape[0], kv, q_ref, ga_ref, lse_ref, kseg_ref[...], qseg_ref[0],
        None, None, dq_ref,
    )
    half = own_ref.shape[0]

    @pl.when(pl.program_id(1) == 0)
    def _():
        acc_ref[...] = grad_kv

    @pl.when(pl.program_id(1) == 1)
    def _():
        total = acc_ref[...] + grad_kv
        down_ref[...] = total[:half]
        doth_ref[...] = total[half:].astype(BF16)


def cross_attention_back(q, ga, lses, own, oth, kseg, qseg):
    rows, groups = q.shape[0] // 2, q.shape[1] // PAIR
    block, lse, qs = attention_specs(rows, groups)
    return call(
        cross_back_kernel,
        (shape(*q.shape), shape(*own.shape, dtype=F32), shape(*own.shape)),
        (groups, 2),
        [block, block, lse, group_spec(own), group_spec(oth), whole(kseg), qs],
        (block, group_spec(own), group_spec(own)),
        [pltpu.VMEM((2 * own.shape[0], PAIR), F32)],
        micros=21,
    )(q, ga, lses, own, oth, kseg, qseg)


def weight_grads(half, parts, own_ref, oth_ref):
    for ref, first in ((own_ref, 0), (oth_ref, half)):
        for left, right, at in parts:
            grad = dot_nn(left[first : first + half, :], right).astype(BF16)
            cols, _, blk, _ = ref.shape
            ref[:, 0, :, at : at + right.shape[1]] = grad.reshape(cols, blk, right.shape[1])


def cross_post_kernel(
    shards, dq_ref, dko_ref, dkr_ref, n_ref, mem_ref, r_ref, att_ref, s_ref, cot_ref, gain_ref,
    own_ref, oth_ref, wo_own, wo_oth, att_one_ref,
    gown_ref, goth_ref, oown_ref, ooth_ref, new_ref, round_ref, gg_ref, dmem_ref, ga_ref,
    dn_ref, dmo_ref, nt_ref, mt_ref, rt_ref,
):
    step = pl.program_id(0)
    half = n_ref.shape[1] // 2
    qcols = dq_ref.shape[1]

    @pl.when(step == 0)
    def _():
        dn_ref[...] = jnp.zeros_like(dn_ref)
        dmo_ref[...] = jnp.zeros_like(dmo_ref)
        nt_ref[...] = n_ref[...].T
        mt_ref[...] = mem_ref[...].T
        rt_ref[...] = r_ref[...].T

    @pl.when(step < shards)
    def _():
        dq = dq_ref[...]
        dkv = (dko_ref[...] + dkr_ref[...].astype(F32)).astype(BF16)
        own, oth = rows_of(own_ref), rows_of(oth_ref)
        parts = ((nt_ref, dq, 0), (mt_ref, dkv, qcols), (rt_ref, att_ref[...], 2 * qcols))
        weight_grads(half, parts, gown_ref, goth_ref)
        for w, span in ((own, slice(0, half)), (oth, slice(half, 2 * half))):
            dn_ref[:, span] += dot_nt(dq, w[:, :qcols])
            dmo_ref[:, span] += dot_nt(dkv, w[:, qcols : 2 * qcols])

    @pl.when(step == shards - 1)
    def _():
        dmem_ref[...] = dmo_ref[...].astype(BF16)
        dv, gg = norm_back(s_ref[...], gain_ref[...], dn_ref[...])
        gg_ref[...] = gg
        new = cot_ref[...] + dv
        new_ref[...] = new
        round_ref[...] = new.astype(BF16)
        rt_ref[...] = new.astype(BF16).T

    @pl.when(step >= shards)
    def _():
        r = round_ref[...]
        weight_grads(half, ((rt_ref, att_one_ref[...], 0),), oown_ref, ooth_ref)
        out = dot_nn(r[:, :half], rows_of(wo_own)) + dot_nn(r[:, half:], rows_of(wo_oth))
        ga_ref[...] = out.astype(BF16)


def cross_post(
    dq, dko, dkr, n, mem, r, att, s, cot, gain, own, oth, next_own, next_oth, next_att, qcols
):
    rows, width = n.shape
    cols, shards, blk, packed = own.shape
    first = lambda i: jnp.minimum(i, shards - 1)
    second = lambda i: jnp.maximum(i - shards, 0)
    spec = weight_spec(own, packed, lambda i: (0, first(i), 0, 0))
    wo = weight_spec(own, qcols, lambda i: (0, second(i), 0, 2))
    enc_rows = mem.shape[0]
    by_shard = pl.BlockSpec((rows, qcols), lambda i: (0, first(i)))
    enc_by_shard = pl.BlockSpec((enc_rows, qcols), lambda i: (0, first(i)))
    full = fixed(rows, width)
    return call(
        functools.partial(cross_post_kernel, shards),
        (
            shape(*own.shape),
            shape(*own.shape),
            shape(cols, shards, blk, qcols),
            shape(cols, shards, blk, qcols),
            shape(rows, width, dtype=F32),
            shape(rows, width),
            shape(1, width, dtype=F32),
            shape(enc_rows, width),
            shape(rows, shards * qcols),
        ),
        (2 * shards,),
        [by_shard, enc_by_shard, enc_by_shard, full, whole(mem), full, by_shard, full, full]
        + [whole(gain), spec, spec, wo, wo, pl.BlockSpec((rows, qcols), lambda i: (0, second(i)))],
        (
            spec,
            spec,
            weight_spec(own, qcols, lambda i: (0, second(i), 0, 0)),
            weight_spec(own, qcols, lambda i: (0, second(i), 0, 0)),
            full,
            full,
            fixed(1, width),
            fixed(enc_rows, width),
            pl.BlockSpec((rows, qcols), lambda i: (0, second(i))),
        ),
        [
            pltpu.VMEM((rows, width), F32),
            pltpu.VMEM((enc_rows, width), F32),
            pltpu.VMEM((width, rows), BF16),
            pltpu.VMEM((width, enc_rows), BF16),
            pltpu.VMEM((width, rows), BF16),
        ],
        micros=18,
    )(dq, dko, dkr, n, mem, r, att, s, cot, gain, own, oth, next_own, next_oth, next_att)


def self_post_kernel(
    dq_ref, dko_ref, dkr_ref, n_ref, x_ref, cot_ref, gain_ref, own_ref, oth_ref,
    gown_ref, goth_ref, out_ref, gg_ref, dn_ref, nt_ref,
):
    step = pl.program_id(0)
    half = n_ref.shape[1] // 2
    qcols = dq_ref.shape[1]

    @pl.when(step == 0)
    def _():
        dn_ref[...] = jnp.zeros_like(dn_ref)
        nt_ref[...] = n_ref[...].T

    dkv = (dko_ref[...] + dkr_ref[...].astype(F32)).astype(BF16)
    grad = jnp.concatenate([dq_ref[...], dkv], axis=1)
    own, oth = rows_of(own_ref), rows_of(oth_ref)
    weight_grads(half, ((nt_ref, grad, 0),), gown_ref, goth_ref)
    dn_ref[:, :half] += dot_nt(grad, own)
    dn_ref[:, half:] += dot_nt(grad, oth)

    @pl.when(step == pl.num_programs(0) - 1)
    def _():
        dv, gg = norm_back(x_ref[...].astype(F32), gain_ref[...], dn_ref[...])
        gg_ref[...] = gg
        out_ref[...] = (cot_ref[...] + dv).astype(BF16)


def self_post(dq, dko, dkr, n, x, cot, gain, own, oth, qcols):
    rows, width = n.shape
    cols, shards, blk, packed = own.shape
    spec = weight_spec(own, 2 * qcols, lambda i: (0, i, 0, 0))
    by_shard = pl.BlockSpec((rows, qcols), lambda i: (0, i))
    full = fixed(rows, width)
    return call(
        self_post_kernel,
        (
            shape(cols, shards, blk, 2 * qcols),
            shape(cols, shards, blk, 2 * qcols),
            shape(rows, width),
            shape(1, width, dtype=F32),
        ),
        (shards,),
        [by_shard, by_shard, by_shard, full, full, full, whole(gain), spec, spec],
        (spec, spec, full, fixed(1, width)),
        [
            pltpu.VMEM((rows, width), F32),
            pltpu.VMEM((width, rows), BF16),
        ],
        micros=14,
    )(dq, dko, dkr, n, x, cot, gain, own, oth)


def pack_layer_kernel(me_ref, q_ref, k_ref, v_ref, o_ref, out_ref):
    qcols, kcols = q_ref.shape[1], k_ref.shape[1]
    out_ref[:, :qcols] = q_ref[...]
    for at in range(0, kcols, HEAD_DIM):
        first = qcols + 2 * at
        out_ref[:, first : first + HEAD_DIM] = k_ref[:, at : at + HEAD_DIM]
        out_ref[:, first + HEAD_DIM : first + 2 * HEAD_DIM] = v_ref[:, at : at + HEAD_DIM]
    out = o_ref[...]
    out_ref[:, 2 * qcols :] = out if out.shape[0] == out_ref.shape[0] else out.T


def pack_ffn_kernel(me_ref, g_ref, u_ref, d_ref, out_ref):
    rows, packed = out_ref.shape
    parts = [r[...] if r.shape[0] == rows else r[...].T for r in (g_ref, u_ref, d_ref)]
    spare = packed - 3 * parts[0].shape[1]
    if spare:
        parts.append(jnp.zeros((rows, spare), BF16))
    out_ref[...] = jnp.concatenate(parts, axis=1)


def packed_rows(kernel, me, blk, by_row, by_col, packed):
    if blk % 128:
        by_row = by_row + [w.T for w in by_col]
        by_col = []
    specs = [pl.BlockSpec((blk, w.shape[1]), lambda i, at: (at[0], 0)) for w in by_row]
    specs += [pl.BlockSpec((w.shape[0], blk), lambda i, at: (0, at[0])) for w in by_col]
    return call(
        kernel, shape(blk, packed), (1,), specs, fixed(blk, packed), prefetch=1, micros=2
    )(me, *by_row, *by_col)


def unpack_layer_kernel(pos_ref, x_ref, q_ref, k_ref, v_ref, *o_refs):
    x = x_ref[0].astype(F32)
    qcols, kcols = q_ref.shape[1], k_ref.shape[1]
    q_ref[...] = x[:, :qcols]
    for at in range(0, kcols, HEAD_DIM):
        first = qcols + 2 * at
        k_ref[:, at : at + HEAD_DIM] = x[:, first : first + HEAD_DIM]
        v_ref[:, at : at + HEAD_DIM] = x[:, first + HEAD_DIM : first + 2 * HEAD_DIM]
    for i, o_ref in enumerate(o_refs):
        out = x[:, (2 + i) * qcols : (3 + i) * qcols]
        o_ref[...] = out if o_ref.shape == out.shape else out.T


def unpack_ffn_kernel(ff, pos_ref, x_ref, g_ref, u_ref, d_ref):
    x = x_ref[0].astype(F32)
    for i, ref in enumerate((g_ref, u_ref, d_ref)):
        out = x[:, i * ff : (i + 1) * ff]
        ref[...] = out if ref.shape == out.shape else out.T


def unpacked(kernel, position, array, by_row, by_col):
    count, blk, packed = array.shape
    turned = blk % 128 == 0
    outs = [shape(count * blk, c, dtype=F32) for c in by_row]
    specs = [pl.BlockSpec((blk, c), lambda p, pos: (p, 0)) for c in by_row]
    for c in by_col:
        if turned:
            outs.append(shape(c, count * blk, dtype=F32))
            specs.append(pl.BlockSpec((c, blk), lambda p, pos: (0, p)))
        else:
            outs.append(shape(count * blk, c, dtype=F32))
            specs.append(pl.BlockSpec((blk, c), lambda p, pos: (p, 0)))
    results = call(
        kernel,
        tuple(outs),
        (count,),
        [pl.BlockSpec((1, blk, packed), lambda p, pos: (pos[p], 0, 0))],
        tuple(specs),
        prefetch=1,
        micros=5,
    )(position, array)
    rows = len(by_row)
    return results[:rows], [r if turned else r.T for r in results[rows:]]


def unpack_layer(position, array, qcols, turned):
    rows, outs = unpacked(
        unpack_layer_kernel, position, array, (qcols, qcols // 2, qcols // 2), (qcols,) * turned
    )
    return (*rows, *outs)


def unpack_ffn(position, array, ff):
    _, turned = unpacked(functools.partial(unpack_ffn_kernel, ff), position, array, (), (ff, ff, ff))
    return turned[0].T, turned[1].T, turned[2]


def make_per_device(batch, shards):
    cols = batch // 2
    bits = cols.bit_length() - 1
    assert batch == 2 * (1 << bits) and shards == 4

    def swap(array, mask):
        return lax.ppermute(array, "batch", [(b, b ^ mask) for b in range(batch)])

    def in_order(position):
        return ((position % cols) << 1) | (position // cols)

    def place_of(difference):
        return (difference >> 1) | ((difference & 1) * cols)

    def to_relative(array):
        me = lax.axis_index("batch")
        blk = array.shape[-1] // batch
        parts = [
            lax.dynamic_slice_in_dim(array, (me ^ in_order(p)) * blk, blk, array.ndim - 1)
            for p in range(batch)
        ]
        return jnp.concatenate(parts, axis=-1)

    def to_absolute(array):
        me = lax.axis_index("batch")
        blk = array.shape[-1] // batch
        parts = [
            lax.dynamic_slice_in_dim(array, place_of(me ^ p) * blk, blk, array.ndim - 1)
            for p in range(batch)
        ]
        return jnp.concatenate(parts, axis=-1)

    def core_of(z):
        return 0 if z in (0, 3) else 1

    routes = []
    for second in (0, 1):
        route = []
        for b in range(batch):
            for z in range(shards):
                micro = (z // 2) ^ second
                target = ((b - b % 2) + core_of(z)) * shards + 2 * micro + b % 2
                route.append((b * shards + z, target))
        routes.append(route)
    both = ("batch", "group")

    def pin(*values):
        return lax.optimization_barrier(values)

    def after(value, *others):
        return lax.optimization_barrier((value,) + others)[0]

    def to_sequence(array):
        first = lax.axis_index("group") // 2
        received = []
        for second, route in enumerate(routes):
            part = lax.dynamic_index_in_dim(array, first ^ second, 0, keepdims=False)
            received.append(lax.ppermute(part, both, route))
        return jnp.concatenate(received, axis=0)

    def send_back(array):
        array = to_absolute(array)
        rows = array.shape[0] // 2
        return [
            lax.ppermute(array[i * rows : (i + 1) * rows], both, [(t, s) for s, t in route])
            for i, route in enumerate(routes)
        ]

    def as_micros(back):
        first = lax.axis_index("group") // 2
        return jnp.where(first == 0, jnp.stack(back), jnp.stack(back[::-1]))

    def swap_z(array, mask):
        return lax.ppermute(array, "group", [(z, z ^ mask) for z in range(shards)])

    def shards_of(own):
        far = swap_z(own, 2)
        return [own, swap_z(own, 1), far, swap_z(far, 1)]

    class Spread:
        def __init__(self, pieces, order):
            self.piece = (len(pieces),) + pieces[0].shape
            self.order, self.own = list(order), None
            self.array = jnp.stack(pieces).reshape((1,) * bits + self.piece)

        def start(self):
            self.pending = swap(self.array, 2 << self.order[0])

        def land(self):
            axis = bits - 1 - self.order.pop(0)
            self.array = jnp.concatenate([self.array, self.pending], axis=axis)

        def advance(self):
            self.land()
            if self.order:
                self.start()
            else:
                self.own = self.array.reshape((cols,) + self.piece)
                self.oth = swap(self.own, 1)

        def finish(self):
            while self.own is None:
                self.advance()
            return self.own, self.oth

    def total_of(terms):
        total = terms[0].astype(F32)
        for term in terms[1:]:
            total = total + term.astype(F32)
        return total

    def halves(terms, axis):
        first = [lax.slice_in_dim(t, 0, 1, axis=axis) for t in terms]
        second = [lax.slice_in_dim(t, 1, 2, axis=axis) for t in terms]
        return first, second

    def joined(terms):
        return terms[0] if len(terms) == 1 else jnp.concatenate(terms, axis=-1)

    def collecting(parts, order, z_masks):
        piece = parts[0][0].shape[1:-1] + (sum(own.shape[-1] for own, _ in parts),)
        pending = yield [swap(oth, 1) for _, oth in parts]
        cube = (2,) * bits
        terms = [
            joined([own for own, _ in parts]).reshape(cube + piece),
            joined(pending).reshape(cube + piece),
        ]
        for bit in order:
            terms, send = halves(terms, bits - 1 - bit)
            terms = terms + (yield [swap(total_of(send).astype(BF16), 2 << bit)])
        terms = [t.reshape(piece) for t in terms]
        for mask in z_masks:
            count = terms[0].shape[0] // 2
            keep, send = halves([t.reshape((count, 2) + t.shape[1:]) for t in terms], 1)
            received = yield [swap_z(total_of(send).astype(BF16), mask)]
            terms = [t.reshape((count,) + piece[1:]) for t in keep + received]
        return terms

    def sharing(terms):
        piece = terms[0].shape[1:]
        array = total_of(terms).astype(BF16).reshape((1,) * bits + piece)
        for bit in range(bits):
            (pending,) = yield [swap(array, 2 << bit)]
            array = jnp.concatenate([array, pending], axis=bits - 1 - bit)
        array = array.reshape((cols,) + piece)
        (pending,) = yield [swap(array, 1)]
        return jnp.concatenate([array, pending], axis=0)

    def whole_chain(parts, order):
        terms = yield from collecting(parts, order, (1, 2))
        return (yield from sharing(terms))

    def ffn_chain(near, far):
        received = yield [swap_z(total_of(far).astype(BF16), 2)]
        return (yield from sharing(near + received))

    def summing(small):
        for mask in (1, 2):
            (other,) = yield [swap_z(small, mask)]
            small = small + other
        for bit in range(bits + 1):
            (other,) = yield [swap(small, 1 << bit)]
            small = small + other
        return small

    class Chain:
        def __init__(self, steps):
            self.steps, self.result = steps, None
            self.pending = next(steps)

        def advance(self):
            try:
                self.pending = self.steps.send(self.pending)
            except StopIteration as stop:
                self.pending, self.result = [], stop.value

    def land(chains, *extra):
        chains = [c for c in chains if c.pending]
        flat = [p for c in chains for p in c.pending]
        flat = list(lax.optimization_barrier(tuple(flat) + extra))
        for c in chains:
            c.pending = [flat.pop(0) for _ in c.pending]
        for c in chains:
            c.advance()
        return flat

    def per_device(
        tokens, memory, dec_segments, enc_segments, buckets,
        self_gain, self_query, self_key, self_value, self_output, rel_bias,
        cross_gain, cross_query, cross_key, cross_value, cross_output,
        ffn_gain, ffn_gate, ffn_up, ffn_down, out_grad,
    ):
        me, z = lax.axis_index("batch"), lax.axis_index("group")
        core, micro, owner = me % 2, z // 2, z % 2
        width = tokens.shape[2]
        blk = width // batch
        qcols = self_query.shape[1]
        chunk, enc_chunk = tokens.shape[1], memory.shape[1]
        up = tuple(range(bits))
        down = up[::-1]

        ff = ffn_gate.shape[1]
        at = me.reshape(1).astype(jnp.int32)
        self_piece = packed_rows(
            pack_layer_kernel, at, blk, [self_query, self_key, self_value], [self_output], 3 * qcols
        )
        cross_piece = packed_rows(
            pack_layer_kernel, at, blk, [cross_query, cross_key, cross_value], [cross_output], 3 * qcols
        )
        ffn_piece = packed_rows(
            pack_ffn_kernel, at, blk, [], [ffn_gate.T, ffn_up.T, ffn_down], 3 * ff + -3 * ff % 128
        )
        self_far = swap_z(self_piece, 2)
        self_near = swap_z(self_piece, 1)
        cross_far = swap_z(cross_piece, 2)
        cross_near = swap_z(cross_piece, 1)
        self_last = swap_z(self_far, 1)
        self_w = Spread([self_piece, self_near, self_far, self_last], up)
        self_w.start()
        cross_last = swap_z(cross_far, 1)
        cross_w = Spread([cross_piece, cross_near, cross_far, cross_last], down)
        cross_w.start()
        stream = to_sequence(after(tokens, self_far, cross_far))
        first = (self_w.pending, cross_w.pending)
        self_w.advance()
        cross_w.advance()
        ffn_piece = after(ffn_piece, *first)
        ffn_near = swap_z(ffn_piece, 1)
        ffn_far = swap_z(ffn_piece, 2)
        ffn_last = swap_z(ffn_far, 1)
        encoder = to_sequence(after(memory, ffn_far))
        near_w = Spread([ffn_piece, ffn_near], up)
        far_w = Spread([ffn_far, ffn_last], down)
        near_w.array = after(near_w.array, self_w.pending, cross_w.pending)
        near_w.start()
        far_w.array = after(far_w.array, self_w.pending, cross_w.pending)
        far_w.start()
        self_own, self_oth = self_w.finish()
        cross_own, cross_oth = cross_w.finish()
        cot = to_sequence(after(out_grad, encoder))
        stream, encoder = to_relative(stream), to_relative(encoder)

        segments = jnp.concatenate([dec_segments, enc_segments], axis=1)
        length = dec_segments.shape[1]
        chosen = jnp.where(owner == core, segments, swap(segments, 1))
        chosen = lax.dynamic_index_in_dim(chosen, micro, 0, keepdims=False)
        dec_seg, enc_seg = chosen[:length], chosen[length:]

        def ids_of(which):
            first = jnp.where(micro == 0, which, 3 - which)
            return [first, 3 - first]

        ids = jnp.stack(ids_of(core) + ids_of(1 - core)).astype(jnp.int32)

        def pieces_of(seg, size, count):
            return [lax.dynamic_slice_in_dim(seg, ids[i] * size, size, 0) for i in range(count)]

        qseg = jnp.stack(pieces_of(dec_seg, chunk, 2)).reshape(2, 1, chunk)
        kseg = dec_seg.reshape(length, 1)
        enc_kseg = jnp.concatenate(pieces_of(enc_seg, enc_chunk, 4)).reshape(-1, 1)

        all_bias = jnp.concatenate(shards_of(rel_bias), axis=1)
        bucket_count = rel_bias.shape[0]
        onehot = (buckets[:, None] == jnp.arange(bucket_count)[None, :]).astype(F32)
        distance_bias = lax.dot_general(
            all_bias, onehot, (((0,), (1,)), ((), ())), precision=HIGHEST, preferred_element_type=F32
        )
        slabs = bias_slabs(distance_bias)
        gain_one, gain_two, gain_three = (
            to_relative(gain.reshape(1, width)) for gain in (self_gain, cross_gain, ffn_gain)
        )

        n_one, q_one, kv_one = project_qkv(stream, gain_one, self_own, self_oth, qcols)
        kv_one_oth = swap(kv_one, 1)
        kv_two = project_kv(encoder, cross_own, cross_oth, qcols)
        kv_two_oth = swap(kv_two, 1)
        near_w.pending, far_w.pending, q_one = pin(near_w.pending, far_w.pending, q_one)
        near_w.advance()
        far_w.advance()
        att_one, lse_one = self_attention(ids, q_one, kv_one, kv_one_oth, slabs, kseg, qseg)
        stream_one, n_two, q_two = output_and_query(
            stream, att_one, gain_two, self_own, self_oth, cross_own, cross_oth, qcols
        )
        att_two, lse_two = cross_attention(q_two, kv_two, kv_two_oth, enc_kseg, qseg)
        near_w.pending, far_w.pending, att_two = pin(near_w.pending, far_w.pending, att_two)
        near_w.finish()
        far_w.finish()
        stream_two, n_three = output_and_norm(stream_one, att_two, gain_three, cross_own, cross_oth, qcols)

        cot = to_relative(cot)
        ya, da, grad_own, grad_oth = feed_forward(n_three, cot, near_w.own, near_w.oth, ff)
        near_g = Chain(collecting([(grad_own, grad_oth)], down, (1,)))
        n_three, ya = pin(n_three, ya)
        yb, db, grad_own, grad_oth = feed_forward(n_three, cot, far_w.own, far_w.oth, ff)
        far_g = Chain(collecting([(grad_own, grad_oth)], up, (1,)))
        (db,) = land([near_g], db)
        block_out, cot_two, round_two, grad_gain_three, ga_two = after_ffn(
            stream_two, ya, yb, da, db, cot, gain_three, cross_own, cross_oth, qcols
        )
        (ga_two,) = land([far_g], ga_two)
        block_back = send_back(block_out)

        dq_two, dkv_two, dkv_two_send = cross_attention_back(
            q_two, ga_two, lse_two, kv_two, kv_two_oth, enc_kseg, qseg
        )
        (grad_own, grad_oth, out_own, out_oth, cot_one, round_one, grad_gain_two, memory_grad, ga_one) = cross_post(
            dq_two, dkv_two, swap(dkv_two_send, 1), n_two, encoder, round_two, att_two, stream_one,
            cot_two, gain_two, cross_own, cross_oth, self_own, self_oth, att_one, qcols,
        )
        cross_g = Chain(whole_chain([(grad_own, grad_oth), (out_own, out_oth)], up))
        (ga_one,) = land([near_g, far_g, cross_g], ga_one)
        dq_one, dkv_one, dkv_one_send, folded = self_attention_back(
            ids, q_one, ga_one, lse_one, kv_one, kv_one_oth, slabs, kseg, qseg
        )
        (dq_one,) = land([near_g, far_g], dq_one)
        grad_own, grad_oth, tokens_grad, grad_gain_one = self_post(
            dq_one, dkv_one, swap(dkv_one_send, 1), n_one, stream, cot_one,
            gain_one, self_own, self_oth, qcols,
        )
        self_g = Chain(whole_chain([(grad_own, grad_oth)], up))
        tokens_back = send_back(tokens_grad)

        padded = jnp.pad(folded, ((0, 0), (0, 0), (0, 8)))
        distance_grad = sum(padded[:, i, 128 + i : 128 + i + length] for i in range(8))
        bucket_grad = lax.dot_general(
            onehot, distance_grad, (((0,), (1,)), ((), ())), precision=HIGHEST, preferred_element_type=F32
        )
        small = [to_absolute(g).reshape(width) for g in (grad_gain_one, grad_gain_two, grad_gain_three)]
        bucket_grad = bucket_grad.reshape(bucket_count, shards, -1)
        bucket_grad = [
            lax.dynamic_index_in_dim(bucket_grad, z ^ p, 1, keepdims=False) for p in range(shards)
        ]
        small = jnp.concatenate(small + [g.reshape(-1) for g in bucket_grad])
        position = place_of(me ^ jnp.arange(batch)).astype(jnp.int32)
        small_g = Chain(summing(small))
        land([self_g])
        land([near_g, far_g, cross_g])
        while near_g.pending or far_g.pending:
            land([near_g, far_g])
        ffn_g = Chain(ffn_chain(near_g.result, far_g.result))
        memory_back = send_back(after(memory_grad, *self_g.pending))
        chains = [self_g, cross_g, ffn_g, small_g]
        land(chains)
        while ffn_g.pending:
            land(chains)
        ffn_final = land(chains, *unpack_ffn(position, ffn_g.result, ff))
        while cross_g.pending:
            land(chains)
        *cross_final, self_out_grad = unpack_layer(position, cross_g.result, qcols, 2)
        *cross_final, self_out_grad = land(chains, *cross_final, self_out_grad)
        while any(c.pending for c in chains):
            land(chains)
        self_final = (*unpack_layer(position, self_g.result, qcols, 0), self_out_grad)
        late = self_g.result
        block_back = [after(part, late) for part in block_back]
        memory_back = [after(part, late) for part in memory_back]
        tokens_back = [after(part, late) for part in tokens_back]
        block_out = as_micros(block_back)
        memory_grad = as_micros(memory_back).astype(F32)
        tokens_grad = as_micros(tokens_back).astype(F32)

        small = small_g.result
        gains = [small[i * width : (i + 1) * width] for i in range(3)]
        bucket_grad = small[3 * width :].reshape(shards, bucket_count, -1)
        bucket_grad = lax.dynamic_index_in_dim(bucket_grad, z, 0, keepdims=False)

        return (
            block_out,
            tokens_grad,
            memory_grad,
            gains[0],
            *self_final,
            bucket_grad,
            gains[1],
            *cross_final,
            gains[2],
            *ffn_final,
        )

    return per_device


def solution(mesh):
    rows, group_cols, group_rows = P(None, ("batch", "group"), None), P(None, "group"), P("group", None)
    layer = (group_cols, group_cols, group_cols, group_rows)
    return jax.shard_map(
        make_per_device(mesh.shape["batch"], mesh.shape["group"]),
        mesh=mesh,
        in_specs=(
            rows, rows, P(None, "batch"), P(None, "batch"), P(),
            P(), *layer, group_cols,
            P(), *layer,
            P(), group_cols, group_cols, group_rows, rows,
        ),
        out_specs=(
            rows, rows, rows,
            P(), *layer, group_cols,
            P(), *layer,
            P(), group_cols, group_cols, group_rows,
        ),
        check_vma=False,
    )
```

```python
import functools

import jax
import jax.numpy as jnp
from jax import lax
from jax.experimental import pallas as pl
from jax.experimental.pallas import tpu as pltpu
from jax.sharding import PartitionSpec as P

HEAD_DIM = 64
PAIR = 2 * HEAD_DIM
EPSILON = 1e-06
MASKED = -1e30
HIGHEST = lax.Precision.HIGHEST
BF16 = jnp.bfloat16
F32 = jnp.float32
FLOPS_PER_MICRO = 1_000_000_000
BYTES_PER_MICRO = 3_000_000


def dot_nn(left, right):
    return lax.dot_general(left, right, (((1,), (0,)), ((), ())), preferred_element_type=F32)


def dot_nt(left, right):
    return lax.dot_general(left, right, (((1,), (1,)), ((), ())), preferred_element_type=F32)


def dot_tn(left, right):
    return lax.dot_general(left, right, (((0,), (0,)), ((), ())), preferred_element_type=F32)


def call(kernel, outs, grid, in_specs, out_specs, scratch=(), prefetch=0, micros=5):
    return pl.pallas_call(
        kernel,
        out_shape=outs,
        cost_estimate=pl.CostEstimate(
            flops=micros * FLOPS_PER_MICRO, transcendentals=0, bytes_accessed=micros * BYTES_PER_MICRO
        ),
        grid_spec=pltpu.PrefetchScalarGridSpec(
            num_scalar_prefetch=prefetch,
            grid=grid,
            in_specs=in_specs,
            out_specs=out_specs,
            scratch_shapes=list(scratch),
        ),
        compiler_params=pltpu.CompilerParams(
            dimension_semantics=("arbitrary",) * len(grid),
        ),
    )


def shape(*dims, dtype=BF16):
    return jax.ShapeDtypeStruct(dims, dtype)


def whole(array):
    dims = array.shape
    return pl.BlockSpec(dims, lambda *ids: (0,) * len(dims))


def fixed(*dims):
    return pl.BlockSpec(dims, lambda *ids: (0,) * len(dims))


def rows_of(ref):
    block = ref[...]
    return block.reshape(block.shape[0] * block.shape[2], block.shape[3])


def store_rows(ref, value):
    ref[...] = value.reshape(ref.shape).astype(ref.dtype)


def weight_spec(weights, columns, index):
    cols, _, blk, _ = weights.shape
    return pl.BlockSpec((cols, 1, blk, columns), index)


def norm(values, gain):
    return values * lax.rsqrt(jnp.mean(values * values, axis=-1, keepdims=True) + EPSILON) * gain


def norm_back(values, gain, grad):
    scale = lax.rsqrt(jnp.mean(values * values, axis=-1, keepdims=True) + EPSILON)
    scaled = grad * gain
    inner = jnp.mean(scaled * values, axis=-1, keepdims=True)
    grad_values = scale * scaled - values * (scale * scale * scale * inner)
    grad_gain = jnp.sum(grad * values * scale, axis=0, keepdims=True)
    return grad_values, grad_gain


def qkv_kernel(x_ref, gain_ref, own_ref, oth_ref, n_ref, q_ref, kv_ref):
    half = x_ref.shape[1] // 2
    qcols = q_ref.shape[1]

    @pl.when(pl.program_id(0) == 0)
    def _():
        n_ref[...] = norm(x_ref[...].astype(F32), gain_ref[...]).astype(BF16)

    out = dot_nn(n_ref[:, :half], rows_of(own_ref)) + dot_nn(n_ref[:, half:], rows_of(oth_ref))
    q_ref[...] = out[:, :qcols].astype(BF16)
    kv_ref[...] = out[:, qcols:].astype(BF16)


def project_qkv(x, gain, own, oth, qcols):
    rows, width = x.shape
    shards = own.shape[1]
    spec = weight_spec(own, 2 * qcols, lambda z: (0, z, 0, 0))
    out = pl.BlockSpec((rows, qcols), lambda z: (0, z))
    return call(
        qkv_kernel,
        (shape(rows, width), shape(rows, shards * qcols), shape(rows, shards * qcols)),
        (shards,),
        [whole(x), whole(gain), spec, spec],
        (fixed(rows, width), out, out),
        micros=7,
    )(x, gain, own, oth)


def kv_kernel(x_ref, own_ref, oth_ref, kv_ref):
    half = x_ref.shape[1] // 2
    out = dot_nn(x_ref[:, :half], rows_of(own_ref)) + dot_nn(x_ref[:, half:], rows_of(oth_ref))
    kv_ref[...] = out.astype(BF16)


def project_kv(x, own, oth, qcols):
    rows, width = x.shape
    shards = own.shape[1]
    spec = weight_spec(own, qcols, lambda z: (0, z, 0, 1))
    return call(
        kv_kernel,
        shape(rows, shards * qcols),
        (shards,),
        [whole(x), spec, spec],
        pl.BlockSpec((rows, qcols), lambda z: (0, z)),
        micros=4,
    )(x, own, oth)


def mid_kernel(shards, x_ref, att_ref, gain_ref, wo_own, wo_oth, wq_own, wq_oth, s_ref, n_ref, q_ref):
    step = pl.program_id(0)
    half = x_ref.shape[1] // 2

    @pl.when(step == 0)
    def _():
        s_ref[...] = x_ref[...].astype(F32)

    @pl.when(step < shards)
    def _():
        att = att_ref[...]
        s_ref[:, :half] += dot_nt(att, rows_of(wo_own))
        s_ref[:, half:] += dot_nt(att, rows_of(wo_oth))

    @pl.when(step == shards - 1)
    def _():
        n_ref[...] = norm(s_ref[...], gain_ref[...]).astype(BF16)

    @pl.when(step >= shards)
    def _():
        out = dot_nn(n_ref[:, :half], rows_of(wq_own)) + dot_nn(n_ref[:, half:], rows_of(wq_oth))
        q_ref[...] = out.astype(BF16)


def output_and_query(x, att, gain, own, oth, next_own, next_oth, qcols):
    rows, width = x.shape
    shards = own.shape[1]
    first = lambda i: jnp.minimum(i, shards - 1)
    second = lambda i: jnp.maximum(i - shards, 0)
    wo = weight_spec(own, qcols, lambda i: (0, first(i), 0, 2))
    wq = weight_spec(own, qcols, lambda i: (0, second(i), 0, 0))
    return call(
        functools.partial(mid_kernel, shards),
        (shape(rows, width, dtype=F32), shape(rows, width), shape(rows, shards * qcols)),
        (2 * shards,),
        [
            whole(x),
            pl.BlockSpec((rows, qcols), lambda i: (0, first(i))),
            whole(gain),
            wo,
            wo,
            wq,
            wq,
        ],
        (
            fixed(rows, width),
            fixed(rows, width),
            pl.BlockSpec((rows, qcols), lambda i: (0, second(i))),
        ),
        micros=10,
    )(x, att, gain, own, oth, next_own, next_oth)


def out_kernel(x_ref, att_ref, gain_ref, wo_own, wo_oth, s_ref, n_ref):
    half = x_ref.shape[1] // 2

    @pl.when(pl.program_id(0) == 0)
    def _():
        s_ref[...] = x_ref[...]

    att = att_ref[...]
    s_ref[:, :half] += dot_nt(att, rows_of(wo_own))
    s_ref[:, half:] += dot_nt(att, rows_of(wo_oth))

    @pl.when(pl.program_id(0) == pl.num_programs(0) - 1)
    def _():
        n_ref[...] = norm(s_ref[...], gain_ref[...]).astype(BF16)


def output_and_norm(x, att, gain, own, oth, qcols):
    rows, width = x.shape
    shards = own.shape[1]
    wo = weight_spec(own, qcols, lambda z: (0, z, 0, 2))
    return call(
        out_kernel,
        (shape(rows, width, dtype=F32), shape(rows, width)),
        (shards,),
        [whole(x), pl.BlockSpec((rows, qcols), lambda z: (0, z)), whole(gain), wo, wo],
        (fixed(rows, width), fixed(rows, width)),
        micros=7,
    )(x, att, gain, own, oth)


def ffn_kernel(ff, n_ref, r_ref, own_ref, oth_ref, y_ref, dn_ref, gown_ref, goth_ref, nt_ref, rt_ref):
    half = n_ref.shape[1] // 2

    @pl.when(pl.program_id(0) == 0)
    def _():
        y_ref[...] = jnp.zeros_like(y_ref)
        dn_ref[...] = jnp.zeros_like(dn_ref)
        nt_ref[...] = n_ref[...].T
        rt_ref[...] = r_ref[...].T

    own, oth = rows_of(own_ref), rows_of(oth_ref)
    up_own, up_oth = own[:, : 2 * ff], oth[:, : 2 * ff]
    down_own, down_oth = own[:, 2 * ff : 3 * ff], oth[:, 2 * ff : 3 * ff]
    both = dot_nn(n_ref[:, :half], up_own) + dot_nn(n_ref[:, half:], up_oth)
    gate, upval = both[:, :ff], both[:, ff:]
    grad_hidden = dot_nn(r_ref[:, :half], down_own) + dot_nn(r_ref[:, half:], down_oth)
    grad_hidden = grad_hidden.astype(BF16).astype(F32)
    root = 0.7978845608028654
    square = gate * gate
    tanh = jnp.tanh(root * gate * (1.0 + 0.044715 * square))
    cdf = 0.5 * (1.0 + tanh)
    gelu = gate * cdf
    slope = cdf + 0.5 * gate * (1.0 - tanh * tanh) * root * (1.0 + 3 * 0.044715 * square)
    hidden = (gelu * upval).astype(BF16)
    grad_gate = (grad_hidden * upval * slope).astype(BF16)
    grad_up = (grad_hidden * gelu).astype(BF16)
    grad_both = jnp.concatenate([grad_gate, grad_up], axis=1)
    y_ref[:, :half] += dot_nt(hidden, down_own)
    y_ref[:, half:] += dot_nt(hidden, down_oth)
    dn_ref[:, :half] += dot_nt(grad_both, up_own)
    dn_ref[:, half:] += dot_nt(grad_both, up_oth)
    cols, _, blk, packed = gown_ref.shape
    for ref, first in ((gown_ref, 0), (goth_ref, half)):
        grad = dot_nn(nt_ref[first : first + half, :], grad_both).astype(BF16)
        ref[:, 0, :, : 2 * ff] = grad.reshape(cols, blk, 2 * ff)
        grad = dot_nn(rt_ref[first : first + half, :], hidden).astype(BF16)
        ref[:, 0, :, 2 * ff : 3 * ff] = grad.reshape(cols, blk, ff)
        spare = packed - 3 * ff
        if spare:
            ref[:, 0, :, 3 * ff :] = jnp.zeros((cols, blk, spare), BF16)


def feed_forward(n, r, own, oth, ff):
    rows, width = n.shape
    cols, shards, blk, packed = own.shape
    spec = weight_spec(own, packed, lambda z: (0, z, 0, 0))
    return call(
        functools.partial(ffn_kernel, ff),
        (
            shape(rows, width, dtype=F32),
            shape(rows, width, dtype=F32),
            shape(*own.shape),
            shape(*own.shape),
        ),
        (shards,),
        [whole(n), whole(r), spec, spec],
        (fixed(rows, width), fixed(rows, width), spec, spec),
        [pltpu.VMEM((width, rows), BF16), pltpu.VMEM((width, rows), BF16)],
        micros=22,
    )(n, r, own, oth)


def after_ffn_kernel(
    s_ref, ya_ref, yb_ref, da_ref, db_ref, cot_ref, gain_ref, wo_own, wo_oth,
    out_ref, new_ref, round_ref, gg_ref, ga_ref,
):
    half = s_ref.shape[1] // 2

    @pl.when(pl.program_id(0) == 0)
    def _():
        s = s_ref[...]
        out_ref[...] = (s + ya_ref[...] + yb_ref[...]).astype(BF16)
        dv, gg = norm_back(s, gain_ref[...], da_ref[...] + db_ref[...])
        gg_ref[...] = gg
        new = cot_ref[...].astype(F32) + dv
        new_ref[...] = new
        round_ref[...] = new.astype(BF16)

    out = dot_nn(round_ref[:, :half], rows_of(wo_own)) + dot_nn(round_ref[:, half:], rows_of(wo_oth))
    ga_ref[...] = out.astype(BF16)


def after_ffn(s, ya, yb, da, db, cot, gain, own, oth, qcols):
    rows, width = s.shape
    shards = own.shape[1]
    wo = weight_spec(own, qcols, lambda z: (0, z, 0, 2))
    full = fixed(rows, width)
    return call(
        after_ffn_kernel,
        (
            shape(rows, width),
            shape(rows, width, dtype=F32),
            shape(rows, width),
            shape(1, width, dtype=F32),
            shape(rows, shards * qcols),
        ),
        (shards,),
        [full] * 6 + [whole(gain), wo, wo],
        (full, full, full, fixed(1, width), pl.BlockSpec((rows, qcols), lambda z: (0, z))),
        micros=10,
    )(s, ya, yb, da, db, cot, gain, own, oth)


def slab_kernel(base_ref, out_ref):
    base = base_ref[0]
    eight = jnp.concatenate([base] + [pltpu.roll(base, i, 1) for i in range(1, 8)], axis=0)
    for block in range(out_ref.shape[1] // 8):
        moved = eight if block == 0 else pltpu.roll(eight, 8 * block, 1)
        out_ref[0, 8 * block : 8 * block + 8, :] = moved


def bias_slabs(distance_bias):
    heads, length = distance_bias.shape
    width = length + 128
    base = jnp.pad(distance_bias, ((0, 0), (128, 0))).reshape(heads, 1, width)
    return call(
        slab_kernel,
        shape(heads, 128, width, dtype=F32),
        (heads,),
        [pl.BlockSpec((1, 1, width), lambda h: (h, 0, 0))],
        pl.BlockSpec((1, 128, width), lambda h: (h, 0, 0)),
        micros=11,
    )(base)


def stack_heads(block, low_lanes):
    lanes = lax.broadcasted_iota(jnp.int32, block.shape, 1) < HEAD_DIM
    wide = block.astype(F32)
    moved = pltpu.roll(wide, HEAD_DIM, 1)
    if low_lanes:
        parts = [jnp.where(lanes, wide, 0.0), jnp.where(lanes, moved, 0.0)]
    else:
        parts = [jnp.where(lanes, 0.0, moved), jnp.where(lanes, 0.0, wide)]
    return jnp.concatenate(parts, axis=0).astype(BF16)


def join_heads(transposed, rows, first):
    parts = [transposed[first : first + HEAD_DIM, :rows], transposed[first : first + HEAD_DIM, rows:]]
    return jnp.concatenate(parts, axis=0).T


def allowed_mask(kseg, qseg, causal):
    allowed = kseg == qseg
    if causal:
        keys, rows = allowed.shape
        key_at = lax.broadcasted_iota(jnp.int32, allowed.shape, 0) - (keys - rows)
        row_at = lax.broadcasted_iota(jnp.int32, allowed.shape, 1)
        allowed = allowed & (key_at <= row_at)
    return allowed


def head_bias(slab_ref, head, keys, rows):
    blocks = keys // 128
    last = keys - rows
    parts = []
    for block in range(blocks):
        at = last - 128 * block + 128
        parts.append(slab_ref[head, :, at : at + rows])
    return jnp.concatenate(parts, axis=0)


def attend_block(keys, rows, kv, q_ref, kseg, qseg, slab_ref, att_ref, lse_ref):
    stacked = stack_heads(q_ref[...], True)
    scores = dot_nt(kv, stacked)
    allowed = allowed_mask(kseg, qseg, slab_ref is not None)
    outs = []
    for head in range(2):
        part = scores[:, head * rows : (head + 1) * rows]
        if slab_ref is not None:
            part = part + head_bias(slab_ref, head, keys, rows)
        part = jnp.where(allowed, part, MASKED)
        top = jnp.max(part, axis=0, keepdims=True)
        grown = jnp.exp(part - top)
        total = jnp.sum(grown, axis=0, keepdims=True)
        probs = (grown * (1.0 / total)).astype(BF16)
        outs.append(dot_tn(kv, probs))
        lse_ref[0, :, head * rows : (head + 1) * rows] = top + jnp.log(total)
    att_ref[...] = join_heads(jnp.concatenate(outs, axis=1), rows, HEAD_DIM).astype(BF16)


def sort_keys(ids_ref, own_ref, oth_ref, sorted_ref):
    rows = sorted_ref.shape[1]
    for slot in range(4):
        source = own_ref if slot < 2 else oth_ref
        at = (slot % 2) * rows
        sorted_ref[ids_ref[slot]] = source[at : at + rows, :]


def self_kernel(ids_ref, q_ref, own_ref, oth_ref, slab_ref, kseg_ref, qseg_ref, att_ref, lse_ref, sorted_ref):
    rows = q_ref.shape[0]

    @pl.when(pl.program_id(1) == 0)
    def _():
        sort_keys(ids_ref, own_ref, oth_ref, sorted_ref)

    mine = ids_ref[pl.program_id(1)]
    for count in range(1, 5):

        @pl.when(mine == count - 1)
        def _(count=count):
            keys = count * rows
            kv = sorted_ref[0:count].reshape(keys, PAIR)
            attend_block(
                keys, rows, kv, q_ref, kseg_ref[0:keys, :], qseg_ref[0], slab_ref, att_ref, lse_ref
            )


def attention_specs(rows, groups):
    block = pl.BlockSpec((rows, PAIR), lambda g, s, *_: (s, g))
    lse = pl.BlockSpec((1, 1, 2 * rows), lambda g, s, *_: (2 * g + s, 0, 0))
    qseg = pl.BlockSpec((1, 1, rows), lambda g, s, *_: (s, 0, 0))
    return block, lse, qseg


def group_spec(array):
    return pl.BlockSpec((array.shape[0], PAIR), lambda g, s, *_: (0, g))


def self_attention(ids, q, own, oth, slabs, kseg, qseg):
    rows, groups = q.shape[0] // 2, q.shape[1] // PAIR
    block, lse, qs = attention_specs(rows, groups)
    slab = pl.BlockSpec((2,) + slabs.shape[1:], lambda g, s, *_: (g, 0, 0))
    return call(
        self_kernel,
        (shape(*q.shape), shape(2 * groups, 1, 2 * rows, dtype=F32)),
        (groups, 2),
        [block, group_spec(own), group_spec(oth), slab, whole(kseg), qs],
        (block, lse),
        [pltpu.VMEM((4, rows, PAIR), BF16)],
        prefetch=1,
        micros=20,
    )(ids, q, own, oth, slabs, kseg, qseg)


def cross_kernel(q_ref, own_ref, oth_ref, kseg_ref, qseg_ref, att_ref, lse_ref):
    kv = jnp.concatenate([own_ref[...], oth_ref[...]], axis=0)
    attend_block(
        kv.shape[0], q_ref.shape[0], kv, q_ref, kseg_ref[...], qseg_ref[0], None, att_ref, lse_ref
    )


def cross_attention(q, own, oth, kseg, qseg):
    rows, groups = q.shape[0] // 2, q.shape[1] // PAIR
    block, lse, qs = attention_specs(rows, groups)
    return call(
        cross_kernel,
        (shape(*q.shape), shape(2 * groups, 1, 2 * rows, dtype=F32)),
        (groups, 2),
        [block, group_spec(own), group_spec(oth), whole(kseg), qs],
        (block, lse),
        micros=16,
    )(q, own, oth, kseg, qseg)


def back_block(keys, rows, kv, q_ref, ga_ref, lse_ref, kseg, qseg, slab_ref, dslab_ref, dq_ref):
    stacked = stack_heads(q_ref[...], True)
    stacked_grad = stack_heads(ga_ref[...], False)
    scores = dot_nt(kv, stacked)
    grad_probs = dot_nt(kv, stacked_grad)
    allowed = allowed_mask(kseg, qseg, slab_ref is not None)
    queries, grad_kv = [], 0.0
    for head in range(2):
        span = slice(head * rows, (head + 1) * rows)
        part = scores[:, span]
        if slab_ref is not None:
            part = part + head_bias(slab_ref, head, keys, rows)
        part = jnp.where(allowed, part, MASKED)
        probs = jnp.exp(part - lse_ref[0, :, span])
        grad = grad_probs[:, span]
        inner = jnp.sum(probs * grad, axis=0, keepdims=True)
        grad_scores = probs * (grad - inner)
        low = grad_scores.astype(BF16)
        grad_kv = grad_kv + dot_nn(low, stacked[span, :])
        grad_kv = grad_kv + dot_nn(probs.astype(BF16), stacked_grad[span, :])
        queries.append(dot_tn(kv, low))
        if slab_ref is not None:
            last = keys - rows
            for block in range(keys // 128):
                at = last - 128 * block + 128
                dslab_ref[head, :, at : at + rows] += grad_scores[128 * block : 128 * block + 128, :]
    dq_ref[...] = join_heads(jnp.concatenate(queries, axis=1), rows, 0).astype(BF16)
    return grad_kv


def self_back_kernel(
    ids_ref, q_ref, ga_ref, lse_ref, own_ref, oth_ref, slab_ref, kseg_ref, qseg_ref,
    dq_ref, down_ref, doth_ref, fold_ref, sorted_ref, dsorted_ref, dslab_ref,
):
    rows = q_ref.shape[0]

    @pl.when(pl.program_id(1) == 0)
    def _():
        sort_keys(ids_ref, own_ref, oth_ref, sorted_ref)
        dsorted_ref[...] = jnp.zeros_like(dsorted_ref)
        dslab_ref[...] = jnp.zeros_like(dslab_ref)

    mine = ids_ref[pl.program_id(1)]
    for count in range(1, 5):

        @pl.when(mine == count - 1)
        def _(count=count):
            keys = count * rows
            kv = sorted_ref[0:count].reshape(keys, PAIR)
            grad_kv = back_block(
                keys, rows, kv, q_ref, ga_ref, lse_ref, kseg_ref[0:keys, :], qseg_ref[0],
                slab_ref, dslab_ref, dq_ref,
            )
            dsorted_ref[0:count] += grad_kv.reshape(count, rows, PAIR)

    @pl.when(pl.program_id(1) == 1)
    def _():
        for slot in range(4):
            at = (slot % 2) * rows
            value = dsorted_ref[ids_ref[slot]]
            target = down_ref if slot < 2 else doth_ref
            target[at : at + rows, :] = value.astype(target.dtype)
        width = dslab_ref.shape[2]
        for head in range(2):
            folded = dslab_ref[head]
            count = folded.shape[0] // 2
            while count >= 8:
                folded = folded[:count] + pltpu.roll(folded[count:], width - count, 1)
                count //= 2
            fold_ref[head] = folded


def self_attention_back(ids, q, ga, lses, own, oth, slabs, kseg, qseg):
    rows, groups = q.shape[0] // 2, q.shape[1] // PAIR
    block, lse, qs = attention_specs(rows, groups)
    heads, _, width = slabs.shape
    slab = pl.BlockSpec((2,) + slabs.shape[1:], lambda g, s, *_: (g, 0, 0))
    return call(
        self_back_kernel,
        (
            shape(*q.shape),
            shape(*own.shape, dtype=F32),
            shape(*own.shape),
            shape(heads, 8, width, dtype=F32),
        ),
        (groups, 2),
        [block, block, lse, group_spec(own), group_spec(oth), slab, whole(kseg), qs],
        (
            block,
            group_spec(own),
            group_spec(own),
            pl.BlockSpec((2, 8, width), lambda g, s, *_: (g, 0, 0)),
        ),
        [
            pltpu.VMEM((4, rows, PAIR), BF16),
            pltpu.VMEM((4, rows, PAIR), F32),
            pltpu.VMEM((2, 128, width), F32),
        ],
        prefetch=1,
        micros=32,
    )(ids, q, ga, lses, own, oth, slabs, kseg, qseg)


def cross_back_kernel(
    q_ref, ga_ref, lse_ref, own_ref, oth_ref, kseg_ref, qseg_ref, dq_ref, down_ref, doth_ref, acc_ref
):
    kv = jnp.concatenate([own_ref[...], oth_ref[...]], axis=0)
    grad_kv = back_block(
        kv.shape[0], q_ref.shape[0], kv, q_ref, ga_ref, lse_ref, kseg_ref[...], qseg_ref[0],
        None, None, dq_ref,
    )
    half = own_ref.shape[0]

    @pl.when(pl.program_id(1) == 0)
    def _():
        acc_ref[...] = grad_kv

    @pl.when(pl.program_id(1) == 1)
    def _():
        total = acc_ref[...] + grad_kv
        down_ref[...] = total[:half]
        doth_ref[...] = total[half:].astype(BF16)


def cross_attention_back(q, ga, lses, own, oth, kseg, qseg):
    rows, groups = q.shape[0] // 2, q.shape[1] // PAIR
    block, lse, qs = attention_specs(rows, groups)
    return call(
        cross_back_kernel,
        (shape(*q.shape), shape(*own.shape, dtype=F32), shape(*own.shape)),
        (groups, 2),
        [block, block, lse, group_spec(own), group_spec(oth), whole(kseg), qs],
        (block, group_spec(own), group_spec(own)),
        [pltpu.VMEM((2 * own.shape[0], PAIR), F32)],
        micros=21,
    )(q, ga, lses, own, oth, kseg, qseg)


def weight_grads(half, parts, own_ref, oth_ref):
    for ref, first in ((own_ref, 0), (oth_ref, half)):
        for left, right, at in parts:
            grad = dot_nn(left[first : first + half, :], right).astype(BF16)
            cols, _, blk, _ = ref.shape
            ref[:, 0, :, at : at + right.shape[1]] = grad.reshape(cols, blk, right.shape[1])


def cross_post_kernel(
    shards, dq_ref, dko_ref, dkr_ref, n_ref, mem_ref, r_ref, att_ref, s_ref, cot_ref, gain_ref,
    own_ref, oth_ref, wo_own, wo_oth, att_one_ref,
    gown_ref, goth_ref, oown_ref, ooth_ref, new_ref, round_ref, gg_ref, dmem_ref, ga_ref,
    dn_ref, dmo_ref, nt_ref, mt_ref, rt_ref,
):
    step = pl.program_id(0)
    half = n_ref.shape[1] // 2
    qcols = dq_ref.shape[1]

    @pl.when(step == 0)
    def _():
        dn_ref[...] = jnp.zeros_like(dn_ref)
        dmo_ref[...] = jnp.zeros_like(dmo_ref)
        nt_ref[...] = n_ref[...].T
        mt_ref[...] = mem_ref[...].T
        rt_ref[...] = r_ref[...].T

    @pl.when(step < shards)
    def _():
        dq = dq_ref[...]
        dkv = (dko_ref[...] + dkr_ref[...].astype(F32)).astype(BF16)
        own, oth = rows_of(own_ref), rows_of(oth_ref)
        parts = ((nt_ref, dq, 0), (mt_ref, dkv, qcols), (rt_ref, att_ref[...], 2 * qcols))
        weight_grads(half, parts, gown_ref, goth_ref)
        for w, span in ((own, slice(0, half)), (oth, slice(half, 2 * half))):
            dn_ref[:, span] += dot_nt(dq, w[:, :qcols])
            dmo_ref[:, span] += dot_nt(dkv, w[:, qcols : 2 * qcols])

    @pl.when(step == shards - 1)
    def _():
        dmem_ref[...] = dmo_ref[...].astype(BF16)
        dv, gg = norm_back(s_ref[...], gain_ref[...], dn_ref[...])
        gg_ref[...] = gg
        new = cot_ref[...] + dv
        new_ref[...] = new
        round_ref[...] = new.astype(BF16)
        rt_ref[...] = new.astype(BF16).T

    @pl.when(step >= shards)
    def _():
        r = round_ref[...]
        weight_grads(half, ((rt_ref, att_one_ref[...], 0),), oown_ref, ooth_ref)
        out = dot_nn(r[:, :half], rows_of(wo_own)) + dot_nn(r[:, half:], rows_of(wo_oth))
        ga_ref[...] = out.astype(BF16)


def cross_post(
    dq, dko, dkr, n, mem, r, att, s, cot, gain, own, oth, next_own, next_oth, next_att, qcols
):
    rows, width = n.shape
    cols, shards, blk, packed = own.shape
    first = lambda i: jnp.minimum(i, shards - 1)
    second = lambda i: jnp.maximum(i - shards, 0)
    spec = weight_spec(own, packed, lambda i: (0, first(i), 0, 0))
    wo = weight_spec(own, qcols, lambda i: (0, second(i), 0, 2))
    enc_rows = mem.shape[0]
    by_shard = pl.BlockSpec((rows, qcols), lambda i: (0, first(i)))
    enc_by_shard = pl.BlockSpec((enc_rows, qcols), lambda i: (0, first(i)))
    full = fixed(rows, width)
    return call(
        functools.partial(cross_post_kernel, shards),
        (
            shape(*own.shape),
            shape(*own.shape),
            shape(cols, shards, blk, qcols),
            shape(cols, shards, blk, qcols),
            shape(rows, width, dtype=F32),
            shape(rows, width),
            shape(1, width, dtype=F32),
            shape(enc_rows, width),
            shape(rows, shards * qcols),
        ),
        (2 * shards,),
        [by_shard, enc_by_shard, enc_by_shard, full, whole(mem), full, by_shard, full, full]
        + [whole(gain), spec, spec, wo, wo, pl.BlockSpec((rows, qcols), lambda i: (0, second(i)))],
        (
            spec,
            spec,
            weight_spec(own, qcols, lambda i: (0, second(i), 0, 0)),
            weight_spec(own, qcols, lambda i: (0, second(i), 0, 0)),
            full,
            full,
            fixed(1, width),
            fixed(enc_rows, width),
            pl.BlockSpec((rows, qcols), lambda i: (0, second(i))),
        ),
        [
            pltpu.VMEM((rows, width), F32),
            pltpu.VMEM((enc_rows, width), F32),
            pltpu.VMEM((width, rows), BF16),
            pltpu.VMEM((width, enc_rows), BF16),
            pltpu.VMEM((width, rows), BF16),
        ],
        micros=18,
    )(dq, dko, dkr, n, mem, r, att, s, cot, gain, own, oth, next_own, next_oth, next_att)


def self_post_kernel(
    dq_ref, dko_ref, dkr_ref, n_ref, x_ref, cot_ref, gain_ref, own_ref, oth_ref,
    gown_ref, goth_ref, out_ref, gg_ref, dn_ref, nt_ref,
):
    step = pl.program_id(0)
    half = n_ref.shape[1] // 2
    qcols = dq_ref.shape[1]

    @pl.when(step == 0)
    def _():
        dn_ref[...] = jnp.zeros_like(dn_ref)
        nt_ref[...] = n_ref[...].T

    dkv = (dko_ref[...] + dkr_ref[...].astype(F32)).astype(BF16)
    grad = jnp.concatenate([dq_ref[...], dkv], axis=1)
    own, oth = rows_of(own_ref), rows_of(oth_ref)
    weight_grads(half, ((nt_ref, grad, 0),), gown_ref, goth_ref)
    dn_ref[:, :half] += dot_nt(grad, own)
    dn_ref[:, half:] += dot_nt(grad, oth)

    @pl.when(step == pl.num_programs(0) - 1)
    def _():
        dv, gg = norm_back(x_ref[...].astype(F32), gain_ref[...], dn_ref[...])
        gg_ref[...] = gg
        out_ref[...] = (cot_ref[...] + dv).astype(BF16)


def self_post(dq, dko, dkr, n, x, cot, gain, own, oth, qcols):
    rows, width = n.shape
    cols, shards, blk, packed = own.shape
    spec = weight_spec(own, 2 * qcols, lambda i: (0, i, 0, 0))
    by_shard = pl.BlockSpec((rows, qcols), lambda i: (0, i))
    full = fixed(rows, width)
    return call(
        self_post_kernel,
        (
            shape(cols, shards, blk, 2 * qcols),
            shape(cols, shards, blk, 2 * qcols),
            shape(rows, width),
            shape(1, width, dtype=F32),
        ),
        (shards,),
        [by_shard, by_shard, by_shard, full, full, full, whole(gain), spec, spec],
        (spec, spec, full, fixed(1, width)),
        [
            pltpu.VMEM((rows, width), F32),
            pltpu.VMEM((width, rows), BF16),
        ],
        micros=14,
    )(dq, dko, dkr, n, x, cot, gain, own, oth)


def pack_layer_kernel(me_ref, q_ref, k_ref, v_ref, o_ref, out_ref):
    qcols, kcols = q_ref.shape[1], k_ref.shape[1]
    out_ref[:, :qcols] = q_ref[...]
    for at in range(0, kcols, HEAD_DIM):
        first = qcols + 2 * at
        out_ref[:, first : first + HEAD_DIM] = k_ref[:, at : at + HEAD_DIM]
        out_ref[:, first + HEAD_DIM : first + 2 * HEAD_DIM] = v_ref[:, at : at + HEAD_DIM]
    out = o_ref[...]
    out_ref[:, 2 * qcols :] = out if out.shape[0] == out_ref.shape[0] else out.T


def pack_ffn_kernel(me_ref, g_ref, u_ref, d_ref, out_ref):
    rows, packed = out_ref.shape
    parts = [r[...] if r.shape[0] == rows else r[...].T for r in (g_ref, u_ref, d_ref)]
    spare = packed - 3 * parts[0].shape[1]
    if spare:
        parts.append(jnp.zeros((rows, spare), BF16))
    out_ref[...] = jnp.concatenate(parts, axis=1)


def packed_rows(kernel, me, blk, by_row, by_col, packed):
    if blk % 128:
        by_row = by_row + [w.T for w in by_col]
        by_col = []
    specs = [pl.BlockSpec((blk, w.shape[1]), lambda i, at: (at[0], 0)) for w in by_row]
    specs += [pl.BlockSpec((w.shape[0], blk), lambda i, at: (0, at[0])) for w in by_col]
    return call(
        kernel, shape(blk, packed), (1,), specs, fixed(blk, packed), prefetch=1, micros=2
    )(me, *by_row, *by_col)


def unpack_layer_kernel(pos_ref, x_ref, q_ref, k_ref, v_ref, *o_refs):
    x = x_ref[0].astype(F32)
    qcols, kcols = q_ref.shape[1], k_ref.shape[1]
    q_ref[...] = x[:, :qcols]
    for at in range(0, kcols, HEAD_DIM):
        first = qcols + 2 * at
        k_ref[:, at : at + HEAD_DIM] = x[:, first : first + HEAD_DIM]
        v_ref[:, at : at + HEAD_DIM] = x[:, first + HEAD_DIM : first + 2 * HEAD_DIM]
    for i, o_ref in enumerate(o_refs):
        out = x[:, (2 + i) * qcols : (3 + i) * qcols]
        o_ref[...] = out if o_ref.shape == out.shape else out.T


def unpack_ffn_kernel(ff, pos_ref, x_ref, g_ref, u_ref, d_ref):
    x = x_ref[0].astype(F32)
    for i, ref in enumerate((g_ref, u_ref, d_ref)):
        out = x[:, i * ff : (i + 1) * ff]
        ref[...] = out if ref.shape == out.shape else out.T


def unpacked(kernel, position, array, by_row, by_col):
    count, blk, packed = array.shape
    turned = blk % 128 == 0
    outs = [shape(count * blk, c, dtype=F32) for c in by_row]
    specs = [pl.BlockSpec((blk, c), lambda p, pos: (p, 0)) for c in by_row]
    for c in by_col:
        if turned:
            outs.append(shape(c, count * blk, dtype=F32))
            specs.append(pl.BlockSpec((c, blk), lambda p, pos: (0, p)))
        else:
            outs.append(shape(count * blk, c, dtype=F32))
            specs.append(pl.BlockSpec((blk, c), lambda p, pos: (p, 0)))
    results = call(
        kernel,
        tuple(outs),
        (count,),
        [pl.BlockSpec((1, blk, packed), lambda p, pos: (pos[p], 0, 0))],
        tuple(specs),
        prefetch=1,
        micros=5,
    )(position, array)
    rows = len(by_row)
    return results[:rows], [r if turned else r.T for r in results[rows:]]


def unpack_layer(position, array, qcols, turned):
    rows, outs = unpacked(
        unpack_layer_kernel, position, array, (qcols, qcols // 2, qcols // 2), (qcols,) * turned
    )
    return (*rows, *outs)


def unpack_ffn(position, array, ff):
    _, turned = unpacked(functools.partial(unpack_ffn_kernel, ff), position, array, (), (ff, ff, ff))
    return turned[0].T, turned[1].T, turned[2]


def make_per_device(batch, shards):
    cols = batch // 2
    bits = cols.bit_length() - 1
    assert batch == 2 * (1 << bits) and shards == 4

    def swap(array, mask):
        return lax.ppermute(array, "batch", [(b, b ^ mask) for b in range(batch)])

    def in_order(position):
        return ((position % cols) << 1) | (position // cols)

    def place_of(difference):
        return (difference >> 1) | ((difference & 1) * cols)

    def to_relative(array):
        me = lax.axis_index("batch")
        blk = array.shape[-1] // batch
        parts = [
            lax.dynamic_slice_in_dim(array, (me ^ in_order(p)) * blk, blk, array.ndim - 1)
            for p in range(batch)
        ]
        return jnp.concatenate(parts, axis=-1)

    def to_absolute(array):
        me = lax.axis_index("batch")
        blk = array.shape[-1] // batch
        parts = [
            lax.dynamic_slice_in_dim(array, place_of(me ^ p) * blk, blk, array.ndim - 1)
            for p in range(batch)
        ]
        return jnp.concatenate(parts, axis=-1)

    def core_of(z):
        return 0 if z in (0, 3) else 1

    routes = []
    for second in (0, 1):
        route = []
        for b in range(batch):
            for z in range(shards):
                micro = (z // 2) ^ second
                target = ((b - b % 2) + core_of(z)) * shards + 2 * micro + b % 2
                route.append((b * shards + z, target))
        routes.append(route)
    both = ("batch", "group")

    def pin(*values):
        return lax.optimization_barrier(values)

    def after(value, *others):
        return lax.optimization_barrier((value,) + others)[0]

    def to_sequence(array):
        first = lax.axis_index("group") // 2
        received = []
        for second, route in enumerate(routes):
            part = lax.dynamic_index_in_dim(array, first ^ second, 0, keepdims=False)
            received.append(lax.ppermute(part, both, route))
        return jnp.concatenate(received, axis=0)

    def send_back(array):
        array = to_absolute(array)
        rows = array.shape[0] // 2
        return [
            lax.ppermute(array[i * rows : (i + 1) * rows], both, [(t, s) for s, t in route])
            for i, route in enumerate(routes)
        ]

    def as_micros(back):
        first = lax.axis_index("group") // 2
        return jnp.where(first == 0, jnp.stack(back), jnp.stack(back[::-1]))

    def swap_z(array, mask):
        return lax.ppermute(array, "group", [(z, z ^ mask) for z in range(shards)])

    def shards_of(own):
        far = swap_z(own, 2)
        return [own, swap_z(own, 1), far, swap_z(far, 1)]

    class Spread:
        def __init__(self, pieces, order):
            self.piece = (len(pieces),) + pieces[0].shape
            self.order, self.own = list(order), None
            self.array = jnp.stack(pieces).reshape((1,) * bits + self.piece)

        def start(self):
            self.pending = swap(self.array, 2 << self.order[0])

        def land(self):
            axis = bits - 1 - self.order.pop(0)
            self.array = jnp.concatenate([self.array, self.pending], axis=axis)

        def advance(self):
            self.land()
            if self.order:
                self.start()
            else:
                self.own = self.array.reshape((cols,) + self.piece)
                self.oth = swap(self.own, 1)

        def finish(self):
            while self.own is None:
                self.advance()
            return self.own, self.oth

    def total_of(terms):
        total = terms[0].astype(F32)
        for term in terms[1:]:
            total = total + term.astype(F32)
        return total

    def halves(terms, axis):
        first = [lax.slice_in_dim(t, 0, 1, axis=axis) for t in terms]
        second = [lax.slice_in_dim(t, 1, 2, axis=axis) for t in terms]
        return first, second

    def joined(terms):
        return terms[0] if len(terms) == 1 else jnp.concatenate(terms, axis=-1)

    def collecting(parts, order, z_masks):
        piece = parts[0][0].shape[1:-1] + (sum(own.shape[-1] for own, _ in parts),)
        pending = yield [swap(oth, 1) for _, oth in parts]
        cube = (2,) * bits
        terms = [
            joined([own for own, _ in parts]).reshape(cube + piece),
            joined(pending).reshape(cube + piece),
        ]
        for bit in order:
            terms, send = halves(terms, bits - 1 - bit)
            terms = terms + (yield [swap(total_of(send).astype(BF16), 2 << bit)])
        terms = [t.reshape(piece) for t in terms]
        for mask in z_masks:
            count = terms[0].shape[0] // 2
            keep, send = halves([t.reshape((count, 2) + t.shape[1:]) for t in terms], 1)
            received = yield [swap_z(total_of(send).astype(BF16), mask)]
            terms = [t.reshape((count,) + piece[1:]) for t in keep + received]
        return terms

    def sharing(terms):
        piece = terms[0].shape[1:]
        array = total_of(terms).astype(BF16).reshape((1,) * bits + piece)
        for bit in range(bits):
            (pending,) = yield [swap(array, 2 << bit)]
            array = jnp.concatenate([array, pending], axis=bits - 1 - bit)
        array = array.reshape((cols,) + piece)
        (pending,) = yield [swap(array, 1)]
        return jnp.concatenate([array, pending], axis=0)

    def whole_chain(parts, order):
        terms = yield from collecting(parts, order, (1, 2))
        return (yield from sharing(terms))

    def ffn_chain(near, far):
        received = yield [swap_z(total_of(far).astype(BF16), 2)]
        return (yield from sharing(near + received))

    def summing(small):
        for mask in (1, 2):
            (other,) = yield [swap_z(small, mask)]
            small = small + other
        for bit in range(bits + 1):
            (other,) = yield [swap(small, 1 << bit)]
            small = small + other
        return small

    class Chain:
        def __init__(self, steps):
            self.steps, self.result = steps, None
            self.pending = next(steps)

        def advance(self):
            try:
                self.pending = self.steps.send(self.pending)
            except StopIteration as stop:
                self.pending, self.result = [], stop.value

    def land(chains, *extra):
        chains = [c for c in chains if c.pending]
        flat = [p for c in chains for p in c.pending]
        flat = list(lax.optimization_barrier(tuple(flat) + extra))
        for c in chains:
            c.pending = [flat.pop(0) for _ in c.pending]
        for c in chains:
            c.advance()
        return flat

    def per_device(
        tokens, memory, dec_segments, enc_segments, buckets,
        self_gain, self_query, self_key, self_value, self_output, rel_bias,
        cross_gain, cross_query, cross_key, cross_value, cross_output,
        ffn_gain, ffn_gate, ffn_up, ffn_down, out_grad,
    ):
        me, z = lax.axis_index("batch"), lax.axis_index("group")
        core, micro, owner = me % 2, z // 2, z % 2
        width = tokens.shape[2]
        blk = width // batch
        qcols = self_query.shape[1]
        chunk, enc_chunk = tokens.shape[1], memory.shape[1]
        up = tuple(range(bits))
        down = up[::-1]

        ff = ffn_gate.shape[1]
        at = me.reshape(1).astype(jnp.int32)
        self_piece = packed_rows(
            pack_layer_kernel, at, blk, [self_query, self_key, self_value], [self_output], 3 * qcols
        )
        cross_piece = packed_rows(
            pack_layer_kernel, at, blk, [cross_query, cross_key, cross_value], [cross_output], 3 * qcols
        )
        ffn_piece = packed_rows(
            pack_ffn_kernel, at, blk, [], [ffn_gate.T, ffn_up.T, ffn_down], 3 * ff + -3 * ff % 128
        )
        self_far = swap_z(self_piece, 2)
        self_near = swap_z(self_piece, 1)
        cross_far = swap_z(cross_piece, 2)
        cross_near = swap_z(cross_piece, 1)
        self_last = swap_z(self_far, 1)
        self_w = Spread([self_piece, self_near, self_far, self_last], up)
        self_w.start()
        cross_last = swap_z(cross_far, 1)
        cross_w = Spread([cross_piece, cross_near, cross_far, cross_last], down)
        cross_w.start()
        stream = to_sequence(after(tokens, self_far, cross_far))
        first = (self_w.pending, cross_w.pending)
        self_w.advance()
        cross_w.advance()
        ffn_piece = after(ffn_piece, *first)
        ffn_near = swap_z(ffn_piece, 1)
        ffn_far = swap_z(ffn_piece, 2)
        ffn_last = swap_z(ffn_far, 1)
        encoder = to_sequence(after(memory, ffn_far))
        near_w = Spread([ffn_piece, ffn_near], up)
        far_w = Spread([ffn_far, ffn_last], down)
        near_w.array = after(near_w.array, self_w.pending, cross_w.pending)
        near_w.start()
        far_w.array = after(far_w.array, self_w.pending, cross_w.pending)
        far_w.start()
        self_own, self_oth = self_w.finish()
        cross_own, cross_oth = cross_w.finish()
        cot = to_sequence(after(out_grad, encoder, near_w.array))
        stream, encoder = to_relative(stream), to_relative(encoder)

        segments = jnp.concatenate([dec_segments, enc_segments], axis=1)
        length = dec_segments.shape[1]
        chosen = jnp.where(owner == core, segments, swap(segments, 1))
        chosen = lax.dynamic_index_in_dim(chosen, micro, 0, keepdims=False)
        dec_seg, enc_seg = chosen[:length], chosen[length:]

        def ids_of(which):
            first = jnp.where(micro == 0, which, 3 - which)
            return [first, 3 - first]

        ids = jnp.stack(ids_of(core) + ids_of(1 - core)).astype(jnp.int32)

        def pieces_of(seg, size, count):
            return [lax.dynamic_slice_in_dim(seg, ids[i] * size, size, 0) for i in range(count)]

        qseg = jnp.stack(pieces_of(dec_seg, chunk, 2)).reshape(2, 1, chunk)
        kseg = dec_seg.reshape(length, 1)
        enc_kseg = jnp.concatenate(pieces_of(enc_seg, enc_chunk, 4)).reshape(-1, 1)

        all_bias = jnp.concatenate(shards_of(rel_bias), axis=1)
        bucket_count = rel_bias.shape[0]
        onehot = (buckets[:, None] == jnp.arange(bucket_count)[None, :]).astype(F32)
        distance_bias = lax.dot_general(
            all_bias, onehot, (((0,), (1,)), ((), ())), precision=HIGHEST, preferred_element_type=F32
        )
        slabs = bias_slabs(after(distance_bias, *first))
        gain_one, gain_two, gain_three = (
            to_relative(gain.reshape(1, width)) for gain in (self_gain, cross_gain, ffn_gain)
        )

        n_one, q_one, kv_one = project_qkv(stream, gain_one, self_own, self_oth, qcols)
        kv_one_oth = swap(kv_one, 1)
        kv_two = project_kv(encoder, cross_own, cross_oth, qcols)
        kv_two_oth = swap(kv_two, 1)
        near_w.pending, far_w.pending, q_one = pin(near_w.pending, far_w.pending, q_one)
        near_w.advance()
        far_w.advance()
        att_one, lse_one = self_attention(ids, q_one, kv_one, kv_one_oth, slabs, kseg, qseg)
        stream_one, n_two, q_two = output_and_query(
            stream, att_one, gain_two, self_own, self_oth, cross_own, cross_oth, qcols
        )
        att_two, lse_two = cross_attention(q_two, kv_two, kv_two_oth, enc_kseg, qseg)
        near_w.pending, far_w.pending, att_two = pin(near_w.pending, far_w.pending, att_two)
        near_w.finish()
        far_w.finish()
        stream_two, n_three = output_and_norm(stream_one, att_two, gain_three, cross_own, cross_oth, qcols)

        cot = to_relative(cot)
        ya, da, grad_own, grad_oth = feed_forward(n_three, cot, near_w.own, near_w.oth, ff)
        near_g = Chain(collecting([(grad_own, grad_oth)], down, (1,)))
        n_three, ya = pin(n_three, ya)
        yb, db, grad_own, grad_oth = feed_forward(n_three, cot, far_w.own, far_w.oth, ff)
        far_g = Chain(collecting([(grad_own, grad_oth)], up, (1,)))
        (db,) = land([near_g], db)
        block_out, cot_two, round_two, grad_gain_three, ga_two = after_ffn(
            stream_two, ya, yb, da, db, cot, gain_three, cross_own, cross_oth, qcols
        )
        (ga_two,) = land([far_g], ga_two)
        block_back = send_back(block_out)

        dq_two, dkv_two, dkv_two_send = cross_attention_back(
            q_two, ga_two, lse_two, kv_two, kv_two_oth, enc_kseg, qseg
        )
        (grad_own, grad_oth, out_own, out_oth, cot_one, round_one, grad_gain_two, memory_grad, ga_one) = cross_post(
            dq_two, dkv_two, swap(dkv_two_send, 1), n_two, encoder, round_two, att_two, stream_one,
            cot_two, gain_two, cross_own, cross_oth, self_own, self_oth, att_one, qcols,
        )
        cross_g = Chain(whole_chain([(grad_own, grad_oth), (out_own, out_oth)], up))
        (ga_one,) = land([near_g, far_g, cross_g], ga_one)
        dq_one, dkv_one, dkv_one_send, folded = self_attention_back(
            ids, q_one, ga_one, lse_one, kv_one, kv_one_oth, slabs, kseg, qseg
        )
        (dq_one,) = land([near_g, far_g], dq_one)
        grad_own, grad_oth, tokens_grad, grad_gain_one = self_post(
            dq_one, dkv_one, swap(dkv_one_send, 1), n_one, stream, cot_one,
            gain_one, self_own, self_oth, qcols,
        )
        self_g = Chain(whole_chain([(grad_own, grad_oth)], up))
        tokens_back = send_back(tokens_grad)

        padded = jnp.pad(folded, ((0, 0), (0, 0), (0, 8)))
        distance_grad = sum(padded[:, i, 128 + i : 128 + i + length] for i in range(8))
        bucket_grad = lax.dot_general(
            onehot, distance_grad, (((0,), (1,)), ((), ())), precision=HIGHEST, preferred_element_type=F32
        )
        small = [to_absolute(g).reshape(width) for g in (grad_gain_one, grad_gain_two, grad_gain_three)]
        bucket_grad = bucket_grad.reshape(bucket_count, shards, -1)
        bucket_grad = [
            lax.dynamic_index_in_dim(bucket_grad, z ^ p, 1, keepdims=False) for p in range(shards)
        ]
        small = jnp.concatenate(small + [g.reshape(-1) for g in bucket_grad])
        position = place_of(me ^ jnp.arange(batch)).astype(jnp.int32)
        small_g = Chain(summing(small))
        land([self_g])
        land([near_g, far_g, cross_g])
        while near_g.pending or far_g.pending:
            land([near_g, far_g])
        ffn_g = Chain(ffn_chain(near_g.result, far_g.result))
        memory_back = send_back(after(memory_grad, *self_g.pending))
        chains = [self_g, cross_g, ffn_g, small_g]
        land(chains)
        while ffn_g.pending:
            land(chains)
        ffn_final = land(chains, *unpack_ffn(position, ffn_g.result, ff))
        while cross_g.pending:
            land(chains)
        *cross_final, self_out_grad = unpack_layer(position, cross_g.result, qcols, 2)
        *cross_final, self_out_grad = land(chains, *cross_final, self_out_grad)
        while any(c.pending for c in chains):
            land(chains)
        self_final = (*unpack_layer(position, self_g.result, qcols, 0), self_out_grad)
        late = self_g.result
        block_back = [after(part, late) for part in block_back]
        memory_back = [after(part, late) for part in memory_back]
        tokens_back = [after(part, late) for part in tokens_back]
        block_out = as_micros(block_back)
        memory_grad = as_micros(memory_back).astype(F32)
        tokens_grad = as_micros(tokens_back).astype(F32)

        small = small_g.result
        gains = [small[i * width : (i + 1) * width] for i in range(3)]
        bucket_grad = small[3 * width :].reshape(shards, bucket_count, -1)
        bucket_grad = lax.dynamic_index_in_dim(bucket_grad, z, 0, keepdims=False)

        return (
            block_out,
            tokens_grad,
            memory_grad,
            gains[0],
            *self_final,
            bucket_grad,
            gains[1],
            *cross_final,
            gains[2],
            *ffn_final,
        )

    return per_device


def solution(mesh):
    rows, group_cols, group_rows = P(None, ("batch", "group"), None), P(None, "group"), P("group", None)
    layer = (group_cols, group_cols, group_cols, group_rows)
    return jax.shard_map(
        make_per_device(mesh.shape["batch"], mesh.shape["group"]),
        mesh=mesh,
        in_specs=(
            rows, rows, P(None, "batch"), P(None, "batch"), P(),
            P(), *layer, group_cols,
            P(), *layer,
            P(), group_cols, group_cols, group_rows, rows,
        ),
        out_specs=(
            rows, rows, rows,
            P(), *layer, group_cols,
            P(), *layer,
            P(), group_cols, group_cols, group_rows,
        ),
        check_vma=False,
    )
```
